128 devices in a mesh: ctx: 8 (over x, y_lo), tp: 8 (over z, core), dp: 2 (over y_hi).
Axes of the slice: x: 4, y: 4 (y_hi: 2, y_lo: 2; y = y_hi * 2 + y_lo), z: 4, core: 2. Of those that a mesh axis runs over, the one named last changes fastest.
Arguments:
- tokens: bfloat16 [16384, 8192], P(('dp', 'ctx', 'tp')), parts along dimension 0, may hold values from -6 to 6
- norm_gain: float32 [8192], replicated, may hold values from 0.1 to 1.9
- w_qkv: bfloat16 [8192, 6144], P(None, 'tp')
- w_out: bfloat16 [4096, 8192], P('tp'), may hold values from -0.75 to 0.75
- doc_lengths: int32 [32], P('dp'), parts along dimension 0, may hold values from 1 to 2048, 8192 in all
- span_slots: int32 [32], P('dp'), parts along dimension 0, may hold values from 0 to 15, as said below
Outputs:
- attn_out: bfloat16 [16384, 8192], P(('dp', 'ctx', 'tp')), parts along dimension 0
The draws below stay inside these ranges and needn't reach their ends.
There are 2 independent parts, one for each index of `dp`. The reference program is written for one: setup_inputs(seed, part) draws one part's arguments, and reference() takes and returns one part's arrays. A program takes and returns all parts, laid end to end along the dimension named above; an argument that names none is the same for every part. Nothing has to cross between parts.
Inputs may be any that keep to these rules, and one draw needn't show every extreme that they name: `span_slots`: every position block appears once; the two slots 2r and 2r + 1 hold blocks whose numbers sum to 15. `doc_lengths`: the lengths sum to 8192 and the longest is exactly 2048.
All inputs are finite; a program needn't handle non-finite values.
Results may differ from the reference program's by a relative error of at most 0.019.
Values may be sent and summed in bfloat16 or wider, within the bound.
No kernel may reach another device: no remote copies, remote signals or barrier semaphores. Data moves between devices by JAX's collectives and lax.ppermute only.
A program may use at most 128 MiB of HBM per device.

```python
import math
import jax
import jax.numpy as jnp
import numpy as np
from jax import lax

D = 8192
HEADS = 32
KVH = 8
HD = 128
NDOC = 16
GROUP = 4
HEADS_DEV = 4
SEQ = 8192
SPANS = 16
SPAN = 512
MOST = 2048
N_TP = 8


def draw_w_qkv(key, part):
    base = jax.random.normal(jax.random.fold_in(key, 11), (D, KVH, GROUP + 2, HD), jnp.float32) * D ** (-0.5)
    return base.reshape(D, KVH * (GROUP + 2) * HD).astype(jnp.bfloat16)


def draw_span_slots(key, part):
    half = SPANS // 2
    order = jax.random.permutation(jax.random.fold_in(key, 21), half).astype(jnp.int32)
    flip = jax.random.randint(jax.random.fold_in(key, 22), (half,), 0, 2).astype(jnp.int32)
    first = jnp.where(flip == 1, SPANS - 1 - order, order).astype(jnp.int32)
    second = (SPANS - 1 - first).astype(jnp.int32)
    return jnp.stack([first, second], axis=1).reshape(SPANS).astype(jnp.int32)


def block_scale(stream_key, dims, cuts, smallest, top_value):
    loudness, own = 1.0, jax.random.fold_in(stream_key, 6)
    for axis_at, parts in cuts:
        draws = jnp.exp(jax.random.uniform(jax.random.fold_in(own, axis_at), (parts,), jnp.float32, smallest / len(cuts), top_value / len(cuts)))
        loudness = loudness * jnp.repeat(draws, dims[axis_at] // parts).reshape([-1 if axis == axis_at else 1 for axis in range(len(dims))])
    return loudness


def split_up(count, total, most, lean):
    portions = [(1 << 20) // math.isqrt(standing ** lean) + 1 for standing in range(2, count + 1)]
    surplus, counts = total - most - (count - 1), [1] * (count - 1)
    while surplus > 0:
        free = [i for i in range(count - 1) if counts[i] < most]
        mass, left = sum([portions[i] for i in free]), surplus
        for i in free:
            addition = min(most - counts[i], max(1, left * portions[i] // mass), surplus)
            counts[i] = counts[i] + addition
            surplus = surplus - addition
    return np.array([most] + counts)


def ragged_sizes(rng, amount, total, reach, skew):
    if amount == 2:
        one = jax.random.randint(rng, (), max(1, total - reach), min(reach, total - 1) + 1)
        return jnp.stack([one, total - one])
    sizes = jnp.asarray(split_up(amount, total, reach, skew), jnp.int32)
    couples = (amount - 1) // 2
    giver, sink = sizes[1:1 + 2 * couples:2], sizes[2:2 + 2 * couples:2]
    margin = jnp.minimum(giver - 1, reach - sink)
    shifted = jax.random.randint(jax.random.fold_in(rng, 1), (couples,), 0, 1 << 20) % (margin + 1)
    sizes = sizes.at[1:1 + 2 * couples:2].set(giver - shifted).at[2:2 + 2 * couples:2].set(sink + shifted)
    return sizes[jax.random.permutation(jax.random.fold_in(rng, 2), amount)]


def noise(own_key, dims, scale, limit, pieces=(), kind=jnp.bfloat16):
    result = scale * jax.random.normal(own_key, dims, jnp.float32)
    if pieces:
        result = result * block_scale(own_key, dims, pieces, -0.22, 0.18)
    return jnp.clip(result, -limit, limit).astype(kind)


def setup_inputs(seed: int = 0, part: int = 0) -> dict:
    key_of = jax.random.split(jax.random.key(seed), 7)
    own_keys = jax.random.split(jax.random.fold_in(key_of[6], part), 7)
    tokens = noise(own_keys[0], (SEQ, D), 1.0, 6.0, ((0, 64),))
    norm_gain = jnp.clip(1.0 + 0.18 * jax.random.normal(key_of[1], (D,), jnp.float32), 0.1, 1.9)
    w_qkv = draw_w_qkv(jax.random.fold_in(key_of[6], 71), part)
    w_out = noise(key_of[3], (HEADS * HD, D), (3.0 / (HEADS * HD) ** 0.5), 0.75, ((0, 8),))
    doc_lengths = ragged_sizes(own_keys[4], NDOC, SEQ, MOST, 2).astype(jnp.int32)
    span_slots = draw_span_slots(jax.random.fold_in(jax.random.fold_in(key_of[6], part), 71), part)
    return dict(tokens=tokens, norm_gain=norm_gain, w_qkv=w_qkv, w_out=w_out, doc_lengths=doc_lengths, span_slots=span_slots)


def attend_group(query_rows, key_rows, value_rows, positions, documents):
    scale = 1.0 / HD ** 0.5
    key_f = lax.optimization_barrier(key_rows).astype(jnp.float32)
    value_f = lax.optimization_barrier(value_rows).astype(jnp.float32)

    def one_block(index):
        start = index * SPAN
        query_blk = lax.dynamic_slice_in_dim(query_rows, start, SPAN, 1)
        query_f = lax.optimization_barrier(query_blk).astype(jnp.float32)
        qpos = lax.dynamic_slice_in_dim(positions, start, SPAN, 0)
        qdoc = lax.dynamic_slice_in_dim(documents, start, SPAN, 0)
        scores = jnp.einsum('gcd,kd->gck', query_f, key_f) * scale
        allowed = (positions[None, :] <= qpos[:, None]) & (documents[None, :] == qdoc[:, None])
        masked = jnp.where(allowed[None], scores, jnp.float32(-1e+30))
        largest = lax.optimization_barrier(jnp.max(masked, axis=-1, keepdims=True))
        expo = jnp.where(allowed[None], jnp.exp(masked - largest), jnp.float32(0.0))
        total = lax.optimization_barrier(jnp.sum(expo, axis=-1))
        weights = lax.optimization_barrier(expo.astype(jnp.bfloat16)).astype(jnp.float32)
        summed = jnp.einsum('gck,kd->gcd', weights, value_f)
        return (summed / total[..., None]).astype(jnp.bfloat16)
    blocks = lax.map(one_block, jnp.arange(SEQ // SPAN, dtype=jnp.int32))
    return jnp.transpose(blocks, (1, 0, 2, 3)).reshape(GROUP, SEQ, HD)

def reference(tokens, norm_gain, w_qkv, w_out, doc_lengths, span_slots):
    rows = jnp.arange(SEQ, dtype=jnp.int32)
    positions = (span_slots[rows // SPAN] * SPAN + rows % SPAN).astype(jnp.int32)
    ends = jnp.cumsum(doc_lengths).astype(jnp.int32)
    documents = lax.optimization_barrier(jnp.sum((positions[:, None] >= ends[None, :]).astype(jnp.int32), axis=1)).astype(jnp.int32)
    values_in = tokens.astype(jnp.float32)
    mean_sq = lax.optimization_barrier(jnp.mean(values_in * values_in, axis=-1, keepdims=True))
    normed = (values_in * lax.rsqrt(mean_sq + 1e-05) * norm_gain).astype(jnp.bfloat16)
    qkv = jnp.dot(normed, w_qkv, preferred_element_type=jnp.float32).astype(jnp.bfloat16)
    qkv = qkv.reshape(SEQ, KVH, GROUP + 2, HD)
    queries = jnp.transpose(qkv[:, :, :GROUP, :], (1, 2, 0, 3))
    keys = jnp.transpose(qkv[:, :, GROUP, :], (1, 0, 2))
    values = jnp.transpose(qkv[:, :, GROUP + 1, :], (1, 0, 2))

    def per_group(items):
        return attend_group(items[0], items[1], items[2], positions, documents)
    heads = lax.map(per_group, (queries, keys, values))
    heads = jnp.transpose(heads, (2, 0, 1, 3)).reshape(SEQ, HEADS * HD)
    width = HEADS_DEV * HD
    summed = jnp.zeros((SEQ, D), jnp.float32)
    for group in range(N_TP):
        part_rows = heads[:, group * width:(group + 1) * width]
        part_w = w_out[group * width:(group + 1) * width, :]
        partial_value = jnp.dot(part_rows, part_w, preferred_element_type=jnp.float32).astype(jnp.bfloat16)
        summed = summed + lax.optimization_barrier(partial_value).astype(jnp.float32)
    return summed.astype(jnp.bfloat16)
```

```python
import functools

import jax
import jax.numpy as jnp
from jax import lax
from jax.experimental import pallas as pl
from jax.experimental.pallas import tpu as pltpu
from jax.sharding import PartitionSpec as P

HD = 128
GROUP = 4
QW = GROUP * HD
NZ = 4
NX = 4
TILE = 128
KTILE = 256
MIB = 1 << 20
MASKED = -3e38
LOWEST = -2e31
LOG2E = 1.4426950408889634

Z_BASE = (0, 512, 768, 256)


def z_perm(dz, dc):
    return [
        (z * 2 + c, ((z + dz) % NZ) * 2 + (c + dc) % 2) for z in range(NZ) for c in range(2)
    ]


def x_perm(dx, dy):
    return [
        (x * 2 + y, ((x + dx) % NX) * 2 + (y + dy) % 2) for x in range(NX) for y in range(2)
    ]


def z_send(value, dz):
    return lax.ppermute(value, "tp", z_perm(dz, 0))


def swap(value):
    return lax.ppermute(value, "tp", z_perm(0, 1))


def x_send(value, dx):
    return lax.ppermute(value, "ctx", x_perm(dx, 0))


def y_swap(value):
    return lax.ppermute(value, "ctx", x_perm(0, 1))


def cost(flops, nbytes, trans=0):
    return pl.CostEstimate(flops=int(flops), bytes_accessed=int(nbytes), transcendentals=int(trans))


def norm_body(x_ref, gain_ref, out_ref):
    x = x_ref[...].astype(jnp.float32)
    mean_sq = jnp.mean(x * x, axis=-1, keepdims=True)
    out_ref[...] = (x * lax.rsqrt(mean_sq + 1e-05) * gain_ref[...]).astype(jnp.bfloat16)


def norm_piece(tokens, gain, piece, rows):
    width = tokens.shape[1]
    block = rows // 2
    return pl.pallas_call(
        norm_body,
        grid=(2,),
        in_specs=[
            pl.BlockSpec((block, width), lambda i: (piece * 2 + i, 0)),
            pl.BlockSpec((1, width), lambda i: (0, 0)),
        ],
        out_specs=pl.BlockSpec((block, width), lambda i: (i, 0)),
        out_shape=jax.ShapeDtypeStruct((rows, width), jnp.bfloat16),
        cost_estimate=cost(6 * rows * width, 4 * rows * width),
        compiler_params=pltpu.CompilerParams(vmem_limit_bytes=16 * MIB),
        name="norm_piece",
    )(tokens, gain)


def project_body(n_in, widths, *refs):
    xs, w_ref = refs[:n_in], refs[n_in]
    outs, acc = refs[n_in + 1 : -1], refs[-1]
    step = pl.program_id(0)
    rows = jnp.concatenate([x[...] for x in xs], axis=0)
    part = jnp.dot(rows, w_ref[...], preferred_element_type=jnp.float32)

    @pl.when(step == 0)
    def _():
        acc[...] = part

    @pl.when(step > 0)
    def _():
        acc[...] += part

    @pl.when(step == pl.num_programs(0) - 1)
    def _():
        at = 0
        for out, width in zip(outs, widths):
            out[...] = acc[:, at : at + width].astype(jnp.bfloat16)
            at += width


def project(xs, w, first, widths, depth=1024):
    total = sum(widths)
    rows = sum(x.shape[0] for x in xs)
    width = w.shape[0]
    column = first // total
    return pl.pallas_call(
        functools.partial(project_body, len(xs), widths),
        grid=(width // depth,),
        in_specs=[pl.BlockSpec((x.shape[0], depth), lambda k: (0, k)) for x in xs]
        + [pl.BlockSpec((depth, total), lambda k: (k, column))],
        out_specs=[pl.BlockSpec((rows, one), lambda k: (0, 0)) for one in widths],
        out_shape=[jax.ShapeDtypeStruct((rows, one), jnp.bfloat16) for one in widths],
        scratch_shapes=[pltpu.VMEM((rows, total), jnp.float32)],
        cost_estimate=cost(2 * rows * width * total, 2 * width * (rows + total)),
        compiler_params=pltpu.CompilerParams(vmem_limit_bytes=24 * MIB),
        name="project",
    )(*xs, w)


def exchange(kv):
    other = y_swap(kv)
    left0, left1 = x_send(kv, 1), x_send(other, 1)
    right0, right1 = x_send(kv, -1), x_send(other, -1)
    far0, far1 = x_send(left0, 1), x_send(right1, -1)
    return [kv, other, right0, right1, far0, far1, left0, left1]


def attend_body(n_doc, n_kv, offsets, table_ref, ends_ref, starts_ref, q_ref, *refs):
    kv_hbm = refs[:n_kv]
    keep_ref, send_ref, kv, sem = refs[n_kv:]
    tile = pl.program_id(0)

    def copies():
        return [
            pltpu.make_async_copy(src, kv.at[pl.ds(at, src.shape[0])], sem.at[i])
            for i, (src, at) in enumerate(zip(kv_hbm, offsets))
        ]

    @pl.when(tile == 0)
    def _():
        for one in copies():
            one.start()
        for one in copies():
            one.wait()

    start = starts_ref[tile]
    q = jnp.concatenate([q_ref[:, h * HD : (h + 1) * HD] for h in range(GROUP)], axis=0)
    rows = GROUP * TILE
    q_pos = start + lax.rem(lax.broadcasted_iota(jnp.int32, (rows, 1), 0), TILE)
    doc_start = jnp.zeros((rows, 1), jnp.int32)
    first = jnp.int32(0)
    for i in range(n_doc):
        end = ends_ref[i]
        doc_start = jnp.where(q_pos >= end, end, doc_start)
        first = jnp.where(start >= end, end, first)
    scale = LOG2E / HD**0.5
    ratio = KTILE // TILE

    def step(at, state):
        top, total, acc = state
        spots = [pl.multiple_of(table_ref[at * ratio + i], TILE) for i in range(ratio)]
        keys = jnp.concatenate([kv[pl.ds(spot, TILE), :HD] for spot in spots], axis=0)
        vals = jnp.concatenate([kv[pl.ds(spot, TILE), HD:] for spot in spots], axis=0)
        s = lax.dot_general(q, keys, (((1,), (1,)), ((), ())), preferred_element_type=jnp.float32)
        k_pos = at * KTILE + lax.broadcasted_iota(jnp.int32, (rows, KTILE), 1)
        allowed = (k_pos <= q_pos) & (k_pos >= doc_start)
        s = jnp.where(allowed, s, MASKED)
        new_top = jnp.maximum(top, jnp.max(s, axis=-1, keepdims=True))
        e = jnp.exp2((s - new_top) * scale)
        factor = jnp.exp2((top - new_top) * scale)
        total = total * factor + jnp.sum(e, axis=-1, keepdims=True)
        acc = acc * factor + jnp.dot(
            e.astype(jnp.bfloat16), vals, preferred_element_type=jnp.float32
        )
        return new_top, total, acc

    state = (
        jnp.full((rows, 1), LOWEST, jnp.float32),
        jnp.zeros((rows, 1), jnp.float32),
        jnp.zeros((rows, HD), jnp.float32),
    )
    top, total, acc = lax.fori_loop(first // KTILE, (start + TILE - 1) // KTILE + 1, step, state)
    out = (acc / total).astype(jnp.bfloat16)
    out = jnp.concatenate([out[h * TILE : (h + 1) * TILE] for h in range(GROUP)], axis=1)

    @pl.when(lax.rem(tile, 2) == 0)
    def _():
        keep_ref[...] = out

    @pl.when(lax.rem(tile, 2) == 1)
    def _():
        send_ref[...] = out


def attend(q, kvs, offsets, table, ends, starts, span):
    tiles = q.shape[0] // TILE
    half = q.shape[0] // 2
    count = sum(kv.shape[0] for kv in kvs)
    any_spec = pl.BlockSpec(memory_space=pl.ANY)
    spec = pltpu.PrefetchScalarGridSpec(
        num_scalar_prefetch=3,
        grid=(tiles,),
        in_specs=[pl.BlockSpec((TILE, QW), lambda i, *_: (i, 0))] + [any_spec] * len(kvs),
        out_specs=[pl.BlockSpec((TILE, QW), lambda i, *_: (i // 2, 0))] * 2,
        scratch_shapes=[
            pltpu.VMEM((count, 2 * HD), jnp.bfloat16),
            pltpu.SemaphoreType.DMA((len(kvs),)),
        ],
    )
    return pl.pallas_call(
        functools.partial(attend_body, ends.shape[0], len(kvs), offsets),
        grid_spec=spec,
        out_shape=[jax.ShapeDtypeStruct((half, QW), jnp.bfloat16)] * 2,
        cost_estimate=cost(
            tiles * 4 * GROUP * TILE * span * HD * 2,
            count * 4 * HD + q.size * 4,
            tiles * GROUP * TILE * span,
        ),
        compiler_params=pltpu.CompilerParams(vmem_limit_bytes=32 * MIB),
        name="attend",
    )(table, ends, starts, q, *kvs)


def out_body(own_ref, sib_ref, w_own, w_sib, *outs):
    sums = jnp.dot(own_ref[...], w_own[...], preferred_element_type=jnp.float32)
    sums += jnp.dot(sib_ref[...], w_sib[...], preferred_element_type=jnp.float32)
    for i, out in enumerate(outs):
        out[...] = sums[i * TILE : (i + 1) * TILE].astype(jnp.bfloat16)


def out_project(own, sib, w_own, w_sib, half, step=1024):
    depth, width = w_own.shape
    part = width // 2
    rows = own.shape[0]
    n_out = rows // TILE
    first = half * part // step
    return pl.pallas_call(
        out_body,
        grid=(part // step,),
        in_specs=[pl.BlockSpec((rows, depth), lambda n: (0, 0))] * 2
        + [pl.BlockSpec((depth, step), lambda n: (0, first + n))] * 2,
        out_specs=[pl.BlockSpec((TILE, step), lambda n: (0, n))] * n_out,
        out_shape=[jax.ShapeDtypeStruct((TILE, part), jnp.bfloat16)] * n_out,
        cost_estimate=cost(
            4 * rows * depth * part, 4 * depth * part + 4 * rows * depth + 2 * rows * part
        ),
        compiler_params=pltpu.CompilerParams(vmem_limit_bytes=24 * MIB),
        name="out_project",
    )(own, sib, w_own, w_sib)


def final_body(p_lo, p_hi, a_lo, a_hi, b_lo, b_hi, out_ref):
    f32 = jnp.float32
    half = p_lo.shape[1]
    lo = p_lo[...].astype(f32) + a_lo[...].astype(f32) + b_lo[...].astype(f32)
    hi = p_hi[...].astype(f32) + a_hi[...].astype(f32) + b_hi[...].astype(f32)
    out_ref[:, :half] = lo.astype(jnp.bfloat16)
    out_ref[:, half:] = hi.astype(jnp.bfloat16)


def final_sum(*parts):
    rows, half = parts[0].shape
    block = 32
    return pl.pallas_call(
        final_body,
        grid=(rows // block,),
        in_specs=[pl.BlockSpec((block, half), lambda i: (i, 0))] * 6,
        out_specs=pl.BlockSpec((block, 2 * half), lambda i: (i, 0)),
        out_shape=jax.ShapeDtypeStruct((rows, 2 * half), jnp.bfloat16),
        cost_estimate=cost(6 * rows * half, 16 * rows * half),
        compiler_params=pltpu.CompilerParams(vmem_limit_bytes=24 * MIB),
        name="final_sum",
    )(*parts)


def add_parts(a, b):
    return (a.astype(jnp.float32) + b.astype(jnp.float32)).astype(jnp.bfloat16)


def shards(tokens, norm_gain, w_qkv, w_out, doc_lengths, span_slots):
    ctx = lax.axis_index("ctx")
    tp = lax.axis_index("tp")
    x, y, z, core = ctx // 2, ctx % 2, tp // 2, tp % 2
    piece = tokens.shape[0] // 2
    gain = norm_gain.reshape(1, -1)

    n_spans = span_slots.shape[0]
    per_span = 4
    span = per_span * TILE
    ends = jnp.cumsum(doc_lengths).astype(jnp.int32)
    numbers = jnp.arange(n_spans, dtype=jnp.int32)
    slot_of = jnp.sum(
        jnp.where(span_slots[None, :] == numbers[:, None], numbers[None, :], 0), axis=1
    )
    tile_no = jnp.arange(per_span, dtype=jnp.int32)[None, :]
    slot = slot_of[:, None]
    tile_tp = (slot % 2) * per_span + tile_no
    rank = slot // 2
    rel_z = (tile_tp // 2 - z) % NZ
    z_base = jnp.where(rel_z == 0, Z_BASE[0], 0)
    for i in range(1, NZ):
        z_base = jnp.where(rel_z == i, Z_BASE[i], z_base)
    rel_src = ((rank // 2 - x) % NX) * 2 + (rank % 2 != y).astype(jnp.int32)
    table = rel_src * 1024 + z_base + (tile_tp % 2 != core).astype(jnp.int32) * TILE
    table = table.reshape(-1).astype(jnp.int32)
    own_spans = lax.dynamic_slice_in_dim(span_slots, 2 * ctx, 2, 0)

    def starts_of(*dzs):
        tps = jnp.stack([((z + dz) % NZ) * 2 + c for dz in dzs for c in (core, 1 - core)])
        blocks = jnp.where(tps // per_span == 0, own_spans[0], own_spans[1])
        return (blocks * span + (tps % per_span) * TILE).astype(jnp.int32)

    n0 = norm_piece(tokens, gain, 0, piece)
    n1 = norm_piece(tokens, gain, 1, piece)
    lo0, hi0 = z_send(n0, 1), z_send(n0, -1)
    lo1, hi1 = z_send(n1, 1), z_send(n1, -1)
    far0, far1 = z_send(lo0, 1), z_send(hi1, -1)
    group_a = [n0, n1, swap(n0), swap(n1)]
    group_b = [lo0, lo1, swap(lo0), swap(lo1), hi0, hi1, swap(hi0), swap(hi1)]
    group_d = [far0, far1, swap(far0), swap(far1)]
    w_sib = swap(w_out)

    q_a, kv_a = project(group_a, w_qkv, 0, (QW, 2 * HD))
    q_b, kv_b = project(group_b, w_qkv, 0, (QW, 2 * HD))
    (kv_d,) = project(group_d, w_qkv, QW, (2 * HD,))
    (q_d,) = project(group_d, w_qkv, 0, (QW,))
    kvs, offsets = [], []
    for kv, base in ((kv_a, 0), (kv_b, 256), (kv_d, 768)):
        for i, one in enumerate(exchange(kv)):
            kvs.append(one)
            offsets.append(i * 1024 + base)

    def heads_of(q, *dzs):
        keep, send = attend(q, kvs, offsets, table, ends, starts_of(*dzs), 1024)
        return keep, swap(send)

    d_own, d_sib = heads_of(q_d, 2)
    (d_lo,) = out_project(d_own, d_sib, w_out, w_sib, 0)
    (d_hi,) = out_project(d_own, d_sib, w_out, w_sib, 1)
    from_low, from_high = z_send(d_lo, 1), z_send(d_hi, -1)
    b_own, b_sib = heads_of(q_b, -1, 1)
    prev_lo, next_lo = out_project(b_own, b_sib, w_out, w_sib, 0)
    prev_hi, next_hi = out_project(b_own, b_sib, w_out, w_sib, 1)
    early_hi, early_lo = z_send(next_hi, 1), z_send(prev_lo, -1)
    late_lo = z_send(add_parts(next_lo, from_low), 1)
    late_hi = z_send(add_parts(prev_hi, from_high), -1)
    a_own, a_sib = heads_of(q_a, 0)
    (a_lo,) = out_project(a_own, a_sib, w_out, w_sib, 0)
    (a_hi,) = out_project(a_own, a_sib, w_out, w_sib, 1)
    return final_sum(a_lo, a_hi, early_lo, early_hi, late_lo, late_hi)


def solution(mesh):
    placed = (P(("dp", "ctx", "tp"), None), P(), P(None, "tp"), P("tp", None), P("dp"), P("dp"))
    return jax.shard_map(
        shards, mesh=mesh, in_specs=placed, out_specs=P(("dp", "ctx", "tp"), None), check_vma=False
    )
```

```python
import functools

import jax
import jax.numpy as jnp
from jax import lax
from jax.experimental import pallas as pl
from jax.experimental.pallas import tpu as pltpu
from jax.sharding import PartitionSpec as P

HD = 128
GROUP = 4
QW = GROUP * HD
NZ = 4
NX = 4
TILE = 128
KTILE = 256
MIB = 1 << 20
MASKED = -3e38
LOWEST = -2e31
SHARE = 0.05
LOG2E = 1.4426950408889634

Z_BASE = (0, 512, 768, 256)


def z_perm(dz, dc):
    return [
        (z * 2 + c, ((z + dz) % NZ) * 2 + (c + dc) % 2) for z in range(NZ) for c in range(2)
    ]


def x_perm(dx, dy):
    return [
        (x * 2 + y, ((x + dx) % NX) * 2 + (y + dy) % 2) for x in range(NX) for y in range(2)
    ]


def z_send(value, dz):
    return lax.ppermute(value, "tp", z_perm(dz, 0))


def swap(value):
    return lax.ppermute(value, "tp", z_perm(0, 1))


def x_send(value, dx):
    return lax.ppermute(value, "ctx", x_perm(dx, 0))


def y_swap(value):
    return lax.ppermute(value, "ctx", x_perm(0, 1))


def in_hbm(value):
    return pltpu.with_memory_space_constraint(value, pltpu.HBM)


def cost(flops, nbytes, trans=0):
    return pl.CostEstimate(
        flops=int(flops * SHARE), bytes_accessed=int(nbytes * SHARE), transcendentals=int(trans * SHARE)
    )


def norm_body(x_ref, gain_ref, out_ref):
    x = x_ref[...].astype(jnp.float32)
    mean_sq = jnp.mean(x * x, axis=-1, keepdims=True)
    out_ref[...] = (x * lax.rsqrt(mean_sq + 1e-05) * gain_ref[...]).astype(jnp.bfloat16)


def norm_piece(tokens, gain, piece, rows):
    width = tokens.shape[1]
    block = rows // 2
    return pl.pallas_call(
        norm_body,
        grid=(2,),
        in_specs=[
            pl.BlockSpec((block, width), lambda i: (piece * 2 + i, 0)),
            pl.BlockSpec((1, width), lambda i: (0, 0)),
        ],
        out_specs=pl.BlockSpec((block, width), lambda i: (i, 0)),
        out_shape=jax.ShapeDtypeStruct((rows, width), jnp.bfloat16),
        cost_estimate=cost(6 * rows * width, 4 * rows * width),
        compiler_params=pltpu.CompilerParams(vmem_limit_bytes=16 * MIB),
        name="norm_piece",
    )(tokens, gain)


def project_body(n_in, widths, *refs):
    xs, w_ref = refs[:n_in], refs[n_in]
    outs, acc = refs[n_in + 1 : -1], refs[-1]
    step = pl.program_id(0)
    rows = jnp.concatenate([x[...] for x in xs], axis=0)
    part = jnp.dot(rows, w_ref[...], preferred_element_type=jnp.float32)

    @pl.when(step == 0)
    def _():
        acc[...] = part

    @pl.when(step > 0)
    def _():
        acc[...] += part

    @pl.when(step == pl.num_programs(0) - 1)
    def _():
        at = 0
        for out, width in zip(outs, widths):
            out[...] = acc[:, at : at + width].astype(jnp.bfloat16)
            at += width


def project(xs, w, first, widths, depth=1024):
    total = sum(widths)
    rows = sum(x.shape[0] for x in xs)
    width = w.shape[0]
    column = first // total
    return pl.pallas_call(
        functools.partial(project_body, len(xs), widths),
        grid=(width // depth,),
        in_specs=[pl.BlockSpec((x.shape[0], depth), lambda k: (0, k)) for x in xs]
        + [pl.BlockSpec((depth, total), lambda k: (k, column))],
        out_specs=[pl.BlockSpec((rows, one), lambda k: (0, 0)) for one in widths],
        out_shape=[jax.ShapeDtypeStruct((rows, one), jnp.bfloat16) for one in widths],
        scratch_shapes=[pltpu.VMEM((rows, total), jnp.float32)],
        cost_estimate=cost(2 * rows * width * total, 2 * width * (rows + total)),
        compiler_params=pltpu.CompilerParams(vmem_limit_bytes=24 * MIB),
        name="project",
    )(*xs, w)


def exchange(kv):
    pair = jnp.concatenate([kv, y_swap(kv)], axis=0)
    return [pair, x_send(pair, -1), x_send(pair, 2), x_send(pair, 1)]


def attend_body(n_doc, n_kv, places, pack, table_ref, ends_ref, starts_ref, q_ref, *refs):
    kv_hbm = refs[:n_kv]
    keep_ref, send_ref = refs[n_kv : n_kv + 2]
    packed = refs[n_kv + 2] if pack else None
    kv, sem, out_sem = refs[-3:]
    tile = pl.program_id(0)

    def copies():
        return [
            pltpu.make_async_copy(
                kv_hbm[which].at[pl.ds(src, rows)], kv.at[pl.ds(dst, rows)], sem.at[i]
            )
            for i, (which, src, dst, rows) in enumerate(places)
        ]

    @pl.when(tile == 0)
    def _():
        for one in copies():
            one.start()
        for one in copies():
            one.wait()
        if pack:
            pltpu.make_async_copy(kv, packed, out_sem).start()

    start = starts_ref[tile]
    q_t = jnp.concatenate(
        [q_ref[:, h * HD : (h + 1) * HD].astype(jnp.float32).T for h in range(GROUP)], axis=1
    ).astype(jnp.bfloat16)
    rows = GROUP * TILE
    q_pos = start + lax.rem(lax.broadcasted_iota(jnp.int32, (1, rows), 1), TILE)
    doc_start = jnp.zeros((1, rows), jnp.int32)
    first, last = jnp.int32(0), jnp.int32(0)
    for i in range(n_doc):
        end = ends_ref[i]
        doc_start = jnp.where(q_pos >= end, end, doc_start)
        first = jnp.where(start >= end, end, first)
        last = jnp.where(start + TILE - 1 >= end, end, last)
    scale = LOG2E / HD**0.5
    ratio = KTILE // TILE
    k_iota = lax.broadcasted_iota(jnp.int32, (KTILE, rows), 0)

    def step(at, state, masked):
        top, total, acc = state
        spots = [pl.multiple_of(table_ref[at * ratio + i], TILE) for i in range(ratio)]
        keys = jnp.concatenate([kv[pl.ds(spot, TILE), :HD] for spot in spots], axis=0)
        vals = jnp.concatenate([kv[pl.ds(spot, TILE), HD:] for spot in spots], axis=0)
        s = jnp.dot(keys, q_t, preferred_element_type=jnp.float32)
        if masked:
            base = at * KTILE
            allowed = (k_iota <= q_pos - base) & (k_iota >= doc_start - base)
            s = jnp.where(allowed, s, MASKED)
        new_top = jnp.maximum(top, jnp.max(s, axis=0, keepdims=True))
        e = jnp.exp2((s - new_top) * scale)
        factor = jnp.exp2((top - new_top) * scale)
        total = total * factor + jnp.sum(e, axis=0, keepdims=True)
        acc = acc * factor + lax.dot_general(
            vals,
            e.astype(jnp.bfloat16),
            (((0,), (0,)), ((), ())),
            preferred_element_type=jnp.float32,
        )
        return new_top, total, acc

    state = (
        jnp.full((1, rows), LOWEST, jnp.float32),
        jnp.zeros((1, rows), jnp.float32),
        jnp.zeros((HD, rows), jnp.float32),
    )
    begin, stop = first // KTILE, (start + TILE - 1) // KTILE + 1
    inner = (last + KTILE - 1) // KTILE
    outer = jnp.maximum(inner, start // KTILE)
    masked_step = functools.partial(step, masked=True)
    state = lax.fori_loop(begin, inner, masked_step, state)
    state = lax.fori_loop(inner, outer, functools.partial(step, masked=False), state)
    top, total, acc = lax.fori_loop(outer, stop, masked_step, state)
    out_t = acc / total
    out = jnp.concatenate(
        [out_t[:, h * TILE : (h + 1) * TILE].T for h in range(GROUP)], axis=1
    ).astype(jnp.bfloat16)

    @pl.when(lax.rem(tile, 2) == 0)
    def _():
        keep_ref[...] = out

    @pl.when(lax.rem(tile, 2) == 1)
    def _():
        send_ref[...] = out

    if pack:

        @pl.when(tile == pl.num_programs(0) - 1)
        def _():
            pltpu.make_async_copy(kv, packed, out_sem).wait()


def attend(q, kvs, places, pack, table, ends, starts, span):
    tiles = q.shape[0] // TILE
    half = q.shape[0] // 2
    count = sum(place[3] for place in places)
    hbm = pl.BlockSpec(memory_space=pltpu.HBM)
    spec = pltpu.PrefetchScalarGridSpec(
        num_scalar_prefetch=3,
        grid=(tiles,),
        in_specs=[pl.BlockSpec((TILE, QW), lambda i, *_: (i, 0))] + [hbm] * len(kvs),
        out_specs=[pl.BlockSpec((TILE, QW), lambda i, *_: (i // 2, 0))] * 2 + [hbm] * pack,
        scratch_shapes=[
            pltpu.VMEM((count, 2 * HD), jnp.bfloat16),
            pltpu.SemaphoreType.DMA((len(places),)),
            pltpu.SemaphoreType.DMA,
        ],
    )
    return pl.pallas_call(
        functools.partial(attend_body, ends.shape[0], len(kvs), places, pack),
        grid_spec=spec,
        out_shape=[jax.ShapeDtypeStruct((half, QW), jnp.bfloat16)] * 2
        + [jax.ShapeDtypeStruct((count, 2 * HD), jnp.bfloat16)] * pack,
        cost_estimate=cost(
            tiles * 4 * GROUP * TILE * span * HD * 2,
            count * 4 * HD + q.size * 4,
            tiles * GROUP * TILE * span,
        ),
        compiler_params=pltpu.CompilerParams(vmem_limit_bytes=32 * MIB),
        name="attend",
    )(table, ends, starts, q, *kvs)


def out_body(core_ref, own_ref, sib_ref, w_own, w_sib, *outs):
    sums = jnp.dot(own_ref[...], w_own[...], preferred_element_type=jnp.float32)
    sums += jnp.dot(sib_ref[...], w_sib[...], preferred_element_type=jnp.float32)
    for i, out in enumerate(outs):
        out[...] = sums[i * TILE : (i + 1) * TILE].astype(jnp.bfloat16)


def out_project(core, own, sib, w, half, step=1024):
    depth, width = w.shape[0] // 2, w.shape[1]
    part = width // 2
    rows = own.shape[0]
    n_out = rows // TILE
    first = half * part // step
    spec = pltpu.PrefetchScalarGridSpec(
        num_scalar_prefetch=1,
        grid=(part // step,),
        in_specs=[pl.BlockSpec((rows, depth), lambda n, core: (0, 0))] * 2
        + [
            pl.BlockSpec((depth, step), lambda n, core: (core[0], first + n)),
            pl.BlockSpec((depth, step), lambda n, core: (1 - core[0], first + n)),
        ],
        out_specs=[pl.BlockSpec((TILE, step), lambda n, core: (0, n))] * n_out,
    )
    return pl.pallas_call(
        out_body,
        grid_spec=spec,
        out_shape=[jax.ShapeDtypeStruct((TILE, part), jnp.bfloat16)] * n_out,
        cost_estimate=cost(
            4 * rows * depth * part, 4 * depth * part + 4 * rows * depth + 2 * rows * part
        ),
        compiler_params=pltpu.CompilerParams(vmem_limit_bytes=24 * MIB),
        name="out_project",
    )(core, own, sib, w, w)


def final_body(p_lo, p_hi, a_lo, a_hi, b_lo, b_hi, out_ref):
    f32 = jnp.float32
    half = p_lo.shape[1]
    lo = p_lo[...].astype(f32) + a_lo[...].astype(f32) + b_lo[...].astype(f32)
    hi = p_hi[...].astype(f32) + a_hi[...].astype(f32) + b_hi[...].astype(f32)
    out_ref[:, :half] = lo.astype(jnp.bfloat16)
    out_ref[:, half:] = hi.astype(jnp.bfloat16)


def final_sum(*parts):
    rows, half = parts[0].shape
    block = 32
    return pl.pallas_call(
        final_body,
        grid=(rows // block,),
        in_specs=[pl.BlockSpec((block, half), lambda i: (i, 0))] * 6,
        out_specs=pl.BlockSpec((block, 2 * half), lambda i: (i, 0)),
        out_shape=jax.ShapeDtypeStruct((rows, 2 * half), jnp.bfloat16),
        cost_estimate=cost(6 * rows * half, 16 * rows * half),
        compiler_params=pltpu.CompilerParams(vmem_limit_bytes=24 * MIB),
        name="final_sum",
    )(*parts)


def add_parts(a, b):
    return (a.astype(jnp.float32) + b.astype(jnp.float32)).astype(jnp.bfloat16)


def shards(tokens, norm_gain, w_qkv, w_out, doc_lengths, span_slots):
    ctx = lax.axis_index("ctx")
    tp = lax.axis_index("tp")
    x, y, z, core = ctx // 2, ctx % 2, tp // 2, tp % 2
    piece = tokens.shape[0] // 2
    gain = norm_gain.reshape(1, -1)

    n_spans = span_slots.shape[0]
    per_span = 4
    span = per_span * TILE
    ends = jnp.cumsum(doc_lengths).astype(jnp.int32)
    numbers = jnp.arange(n_spans, dtype=jnp.int32)
    slot_of = jnp.sum(
        jnp.where(span_slots[None, :] == numbers[:, None], numbers[None, :], 0), axis=1
    )
    tile_no = jnp.arange(per_span, dtype=jnp.int32)[None, :]
    slot = slot_of[:, None]
    tile_tp = (slot % 2) * per_span + tile_no
    rank = slot // 2
    rel_z = (tile_tp // 2 - z) % NZ
    z_base = jnp.where(rel_z == 0, Z_BASE[0], 0)
    for i in range(1, NZ):
        z_base = jnp.where(rel_z == i, Z_BASE[i], z_base)
    rel_src = ((rank // 2 - x) % NX) * 2 + (rank % 2 != y).astype(jnp.int32)
    table = rel_src * 1024 + z_base + (tile_tp % 2 != core).astype(jnp.int32) * TILE
    table = table.reshape(-1).astype(jnp.int32)
    own_spans = lax.dynamic_slice_in_dim(span_slots, 2 * ctx, 2, 0)

    def starts_of(*dzs):
        tps = jnp.stack([((z + dz) % NZ) * 2 + c for dz in dzs for c in (core, 1 - core)])
        blocks = jnp.where(tps // per_span == 0, own_spans[0], own_spans[1])
        return (blocks * span + (tps % per_span) * TILE).astype(jnp.int32)

    n0 = norm_piece(tokens, gain, 0, piece)
    n1 = norm_piece(tokens, gain, 1, piece)
    lo0, hi1 = z_send(n0, 1), z_send(n1, -1)
    lo1, hi0 = z_send(n1, 1), z_send(n0, -1)
    far0, far1 = z_send(lo0, 1), z_send(hi1, -1)
    pairs = [[2 * i, 2 * i + 1] for i in range(NZ)]
    w_pair = in_hbm(lax.all_gather(w_out, "tp", axis=0, tiled=True, axis_index_groups=pairs))
    w_qkv = in_hbm(w_qkv)
    core_arg = core.reshape(1).astype(jnp.int32)

    group_a = [in_hbm(one) for one in (n0, n1, swap(n0), swap(n1))]
    q_a, kv_a = project(group_a, w_qkv, 0, (QW, 2 * HD))
    lo0, lo1, hi0, hi1, kv_a, q_a = lax.optimization_barrier((lo0, lo1, hi0, hi1, kv_a, q_a))
    group_b = [lo0, lo1, swap(lo0), swap(lo1), hi0, hi1, swap(hi0), swap(hi1)]
    group_b = [in_hbm(one) for one in group_b]
    q_b, kv_b = project(group_b, w_qkv, 0, (QW, 2 * HD))
    far0, far1, kv_b, q_b = lax.optimization_barrier((far0, far1, kv_b, q_b))
    group_d = [far0, far1, swap(far0), swap(far1)]
    (kv_d,) = project(group_d, w_qkv, QW, (2 * HD,))
    (q_d,) = project(group_d, w_qkv, 0, (QW,))
    kvs, places = [], []
    for kv, base in ((kv_a, 0), (kv_b, 256), (kv_d, 768)):
        rows = kv.shape[0]
        for i, one in enumerate(exchange(kv)):
            for j in range(2):
                places.append((len(kvs), j * rows, (2 * i + j) * 1024 + base, rows))
            kvs.append(in_hbm(one))

    d_own, d_send, packed = attend(q_d, kvs, tuple(places), True, table, ends, starts_of(2), 1024)
    d_sib = swap(d_send)
    (d_lo,) = out_project(core_arg, d_own, d_sib, w_pair, 0)
    (d_hi,) = out_project(core_arg, d_own, d_sib, w_pair, 1)
    from_low, from_high = z_send(d_lo, 1), z_send(d_hi, -1)
    whole = ((0, 0, 0, packed.shape[0]),)
    q_b, packed, d_lo, d_hi = lax.optimization_barrier((q_b, packed, d_lo, d_hi))
    b_own, b_send = attend(q_b, [in_hbm(packed)], whole, False, table, ends, starts_of(-1, 1), 1024)
    b_sib = swap(b_send)
    prev_lo, next_lo = out_project(core_arg, b_own, b_sib, w_pair, 0)
    prev_hi, next_hi = out_project(core_arg, b_own, b_sib, w_pair, 1)
    early_hi, early_lo = z_send(next_hi, 1), z_send(prev_lo, -1)
    q_a, packed, next_hi, prev_hi, next_lo, prev_lo = lax.optimization_barrier(
        (q_a, packed, next_hi, prev_hi, next_lo, prev_lo)
    )
    late_lo = z_send(add_parts(next_lo, from_low), 1)
    late_hi = z_send(add_parts(prev_hi, from_high), -1)
    a_own, a_send = attend(q_a, [in_hbm(packed)], whole, False, table, ends, starts_of(0), 1024)
    a_sib = swap(a_send)
    (a_lo,) = out_project(core_arg, a_own, a_sib, w_pair, 0)
    (a_hi,) = out_project(core_arg, a_own, a_sib, w_pair, 1)
    return final_sum(a_lo, a_hi, early_lo, early_hi, late_lo, late_hi)


def solution(mesh):
    placed = (P(("dp", "ctx", "tp"), None), P(), P(None, "tp"), P("tp", None), P("dp"), P("dp"))
    return jax.shard_map(
        shards, mesh=mesh, in_specs=placed, out_specs=P(("dp", "ctx", "tp"), None), check_vma=False
    )
```

```python
import functools

import jax
import jax.numpy as jnp
from jax import lax
from jax.experimental import pallas as pl
from jax.experimental.pallas import tpu as pltpu
from jax.sharding import PartitionSpec as P

HD = 128
GROUP = 4
QW = GROUP * HD
NZ = 4
NX = 4
TILE = 128
KTILE = 256
MIB = 1 << 20
MASKED = -3e38
LOWEST = -2e31
SHARE = 1e-4
LOG2E = 1.4426950408889634

Z_BASE = (0, 512, 768, 256)


def z_perm(dz, dc):
    return [
        (z * 2 + c, ((z + dz) % NZ) * 2 + (c + dc) % 2) for z in range(NZ) for c in range(2)
    ]


def x_perm(dx, dy):
    return [
        (x * 2 + y, ((x + dx) % NX) * 2 + (y + dy) % 2) for x in range(NX) for y in range(2)
    ]


def z_send(value, dz):
    return lax.ppermute(value, "tp", z_perm(dz, 0))


def swap(value):
    return lax.ppermute(value, "tp", z_perm(0, 1))


def x_send(value, dx):
    return lax.ppermute(value, "ctx", x_perm(dx, 0))


def y_swap(value):
    return lax.ppermute(value, "ctx", x_perm(0, 1))


def in_hbm(value):
    return pltpu.with_memory_space_constraint(value, pltpu.HBM)


def cost(flops, nbytes, trans=0):
    return pl.CostEstimate(
        flops=int(flops * SHARE), bytes_accessed=int(nbytes * SHARE), transcendentals=int(trans * SHARE)
    )


def norm_body(x_ref, gain_ref, out_ref):
    x = x_ref[...].astype(jnp.float32)
    mean_sq = jnp.mean(x * x, axis=-1, keepdims=True)
    out_ref[...] = (x * lax.rsqrt(mean_sq + 1e-05) * gain_ref[...]).astype(jnp.bfloat16)


def norm(tokens, gain, block=32):
    rows, width = tokens.shape
    return pl.pallas_call(
        norm_body,
        grid=(rows // block,),
        in_specs=[
            pl.BlockSpec((block, width), lambda i: (i, 0)),
            pl.BlockSpec((1, width), lambda i: (0, 0)),
        ],
        out_specs=pl.BlockSpec((block, width), lambda i: (i, 0)),
        out_shape=jax.ShapeDtypeStruct((rows, width), jnp.bfloat16),
        cost_estimate=cost(6 * rows * width, 4 * rows * width),
        compiler_params=pltpu.CompilerParams(vmem_limit_bytes=16 * MIB),
        name="norm",
    )(tokens, gain)


def project_body(counts, first, widths, depth, *refs):
    n_in = len(counts)
    xs, w_hbm = refs[:n_in], refs[n_in]
    outs = refs[n_in + 1 : -4]
    rows_v, w_v, x_sem, w_sem = refs[-4:]
    total = sum(widths)
    at, copies = 0, []
    for i, count in enumerate(counts):
        copies.append(pltpu.make_async_copy(xs[i], rows_v.at[pl.ds(at, count)], x_sem.at[i]))
        at += count
    chunks = [
        pltpu.make_async_copy(
            w_hbm.at[pl.ds(k * depth, depth), pl.ds(first, total)],
            w_v.at[pl.ds(k * depth, depth)],
            w_sem.at[k],
        )
        for k in range(w_v.shape[0] // depth)
    ]
    for one in copies + chunks:
        one.start()
    for one in copies:
        one.wait()
    acc = None
    for k, one in enumerate(chunks):
        one.wait()
        part = jnp.dot(
            rows_v[:, k * depth : (k + 1) * depth],
            w_v[k * depth : (k + 1) * depth, :],
            preferred_element_type=jnp.float32,
        )
        acc = part if acc is None else acc + part
    at = 0
    for out, width in zip(outs, widths):
        out[...] = acc[:, at : at + width].astype(jnp.bfloat16)
        at += width


def project(xs, w, first, widths, depth=1024):
    total = sum(widths)
    counts = tuple(x.shape[0] for x in xs)
    rows = sum(counts)
    width = w.shape[0]
    anywhere = pl.BlockSpec(memory_space=pl.ANY)
    return pl.pallas_call(
        functools.partial(project_body, counts, first, widths, depth),
        in_specs=[anywhere] * (len(xs) + 1),
        out_specs=[pl.BlockSpec(memory_space=pltpu.VMEM)] * len(widths),
        out_shape=[jax.ShapeDtypeStruct((rows, one), jnp.bfloat16) for one in widths],
        scratch_shapes=[
            pltpu.VMEM((rows, width), jnp.bfloat16),
            pltpu.VMEM((width, total), jnp.bfloat16),
            pltpu.SemaphoreType.DMA((len(xs),)),
            pltpu.SemaphoreType.DMA((width // depth,)),
        ],
        cost_estimate=cost(2 * rows * width * total, 2 * width * (rows + total)),
        compiler_params=pltpu.CompilerParams(
            vmem_limit_bytes=2 * width * (rows + total) + 10 * rows * total + 4 * MIB
        ),
        name="project",
    )(*xs, w)


def y_pair(kv):
    return jnp.concatenate([kv, y_swap(kv)], axis=0)


def x_all(pair):
    return [pair, x_send(pair, -1), x_send(pair, 2), x_send(pair, 1)]


def attend_body(n_doc, n_kv, places, pack, table_ref, ends_ref, starts_ref, q_ref, *refs):
    kv_hbm = refs[:n_kv]
    keep_ref, send_ref = refs[n_kv : n_kv + 2]
    kv = refs[n_kv + 2] if pack else kv_hbm[0]
    sem = refs[-1]
    tile = pl.program_id(0)

    def copies():
        return [
            pltpu.make_async_copy(
                kv_hbm[which].at[pl.ds(src, rows)], kv.at[pl.ds(dst, rows)], sem.at[i]
            )
            for i, (which, src, dst, rows) in enumerate(places)
        ]

    if pack:

        @pl.when(tile == 0)
        def _():
            for one in copies():
                one.start()
            for one in copies():
                one.wait()

    start = starts_ref[tile]
    q_t = jnp.concatenate(
        [q_ref[:, h * HD : (h + 1) * HD].astype(jnp.float32).T for h in range(GROUP)], axis=1
    ).astype(jnp.bfloat16)
    rows = GROUP * TILE
    q_pos = start + lax.rem(lax.broadcasted_iota(jnp.int32, (1, rows), 1), TILE)
    doc_start = jnp.zeros((1, rows), jnp.int32)
    first, last = jnp.int32(0), jnp.int32(0)
    for i in range(n_doc):
        end = ends_ref[i]
        doc_start = jnp.where(q_pos >= end, end, doc_start)
        first = jnp.where(start >= end, end, first)
        last = jnp.where(start + TILE - 1 >= end, end, last)
    scale = LOG2E / HD**0.5
    ratio = KTILE // TILE
    k_iota = lax.broadcasted_iota(jnp.int32, (KTILE, rows), 0)

    def step(at, state, masked):
        top, total, acc = state
        spots = [pl.multiple_of(table_ref[at * ratio + i], TILE) for i in range(ratio)]
        keys = jnp.concatenate([kv[pl.ds(spot, TILE), :HD] for spot in spots], axis=0)
        vals = jnp.concatenate([kv[pl.ds(spot, TILE), HD:] for spot in spots], axis=0)
        s = jnp.dot(keys, q_t, preferred_element_type=jnp.float32)
        if masked:
            base = at * KTILE
            allowed = (k_iota <= q_pos - base) & (k_iota >= doc_start - base)
            s = jnp.where(allowed, s, MASKED)
        new_top = jnp.maximum(top, jnp.max(s, axis=0, keepdims=True))
        e = jnp.exp2((s - new_top) * scale)
        factor = jnp.exp2((top - new_top) * scale)
        total = total * factor + jnp.sum(e, axis=0, keepdims=True)
        acc = acc * factor + lax.dot_general(
            vals,
            e.astype(jnp.bfloat16),
            (((0,), (0,)), ((), ())),
            preferred_element_type=jnp.float32,
        )
        return new_top, total, acc

    state = (
        jnp.full((1, rows), LOWEST, jnp.float32),
        jnp.zeros((1, rows), jnp.float32),
        jnp.zeros((HD, rows), jnp.float32),
    )
    begin, stop = first // KTILE, (start + TILE - 1) // KTILE + 1
    inner = (last + KTILE - 1) // KTILE
    outer = jnp.maximum(inner, start // KTILE)
    masked_step = functools.partial(step, masked=True)
    state = lax.fori_loop(begin, inner, masked_step, state)
    state = lax.fori_loop(inner, outer, functools.partial(step, masked=False), state)
    top, total, acc = lax.fori_loop(outer, stop, masked_step, state)
    out_t = acc / total
    out = jnp.concatenate(
        [out_t[:, h * TILE : (h + 1) * TILE].T for h in range(GROUP)], axis=1
    ).astype(jnp.bfloat16)

    @pl.when(lax.rem(tile, 2) == 0)
    def _():
        keep_ref[...] = out

    @pl.when(lax.rem(tile, 2) == 1)
    def _():
        send_ref[...] = out


def attend(q, kvs, places, pack, table, ends, starts, span):
    tiles = q.shape[0] // TILE
    half = q.shape[0] // 2
    count = sum(place[3] for place in places)
    anywhere = pl.BlockSpec(memory_space=pl.ANY)
    vmem = pl.BlockSpec(memory_space=pltpu.VMEM)
    spec = pltpu.PrefetchScalarGridSpec(
        num_scalar_prefetch=3,
        grid=(tiles,),
        in_specs=[pl.BlockSpec((TILE, QW), lambda i, *_: (i, 0))] + [anywhere if pack else vmem] * len(kvs),
        out_specs=[pl.BlockSpec((TILE, QW), lambda i, *_: (i // 2, 0))] * 2 + [vmem] * pack,
        scratch_shapes=[
            pltpu.SemaphoreType.DMA((len(places),)),
        ],
    )
    return pl.pallas_call(
        functools.partial(attend_body, ends.shape[0], len(kvs), places, pack),
        grid_spec=spec,
        out_shape=[jax.ShapeDtypeStruct((half, QW), jnp.bfloat16)] * 2
        + [jax.ShapeDtypeStruct((count, 2 * HD), jnp.bfloat16)] * pack,
        cost_estimate=cost(
            tiles * 4 * GROUP * TILE * span * HD * 2,
            count * 4 * HD + q.size * 4,
            tiles * GROUP * TILE * span,
        ),
        compiler_params=pltpu.CompilerParams(vmem_limit_bytes=12 * MIB),
        name="attend",
    )(table, ends, starts, q, *kvs)


def out_body(first, step, core_ref, own_ref, sib_ref, w_hbm, *refs):
    outs, w_v, sem = refs[:-2], refs[-2], refs[-1]
    depth = own_ref.shape[1]
    n_steps = outs[0].shape[1] // step
    core = core_ref[0]
    chunks = []
    for n in range(n_steps):
        for j, at in enumerate((core, 1 - core)):
            chunks.append(
                pltpu.make_async_copy(
                    w_hbm.at[
                        pl.ds(pl.multiple_of(at * depth, depth), depth),
                        pl.ds(first + n * step, step),
                    ],
                    w_v.at[pl.ds(j * depth, depth), pl.ds(n * step, step)],
                    sem.at[n, j],
                )
            )
    for one in chunks:
        one.start()
    heads = jnp.concatenate([own_ref[...], sib_ref[...]], axis=1)
    for n in range(n_steps):
        chunks[2 * n].wait()
        chunks[2 * n + 1].wait()
        sums = jnp.dot(
            heads, w_v[:, n * step : (n + 1) * step], preferred_element_type=jnp.float32
        )
        for i, out in enumerate(outs):
            out[:, n * step : (n + 1) * step] = sums[i * TILE : (i + 1) * TILE].astype(jnp.bfloat16)


def out_project(core, own, sib, w, half, step=512):
    depth, width = w.shape[0] // 2, w.shape[1]
    part = width // 2
    rows = own.shape[0]
    n_out = rows // TILE
    vmem = pl.BlockSpec(memory_space=pltpu.VMEM)
    return pl.pallas_call(
        functools.partial(out_body, half * part, step),
        in_specs=[
            pl.BlockSpec(memory_space=pltpu.SMEM),
            vmem,
            vmem,
            pl.BlockSpec(memory_space=pl.ANY),
        ],
        out_specs=[vmem] * n_out,
        out_shape=[jax.ShapeDtypeStruct((TILE, part), jnp.bfloat16)] * n_out,
        scratch_shapes=[
            pltpu.VMEM((2 * depth, part), jnp.bfloat16),
            pltpu.SemaphoreType.DMA((part // step, 2)),
        ],
        cost_estimate=cost(
            4 * rows * depth * part, 4 * depth * part + 4 * rows * depth + 2 * rows * part
        ),
        compiler_params=pltpu.CompilerParams(vmem_limit_bytes=16 * MIB),
        name="out_project",
    )(core, own, sib, w)


def final_body(p_lo, p_hi, a_lo, a_hi, b_lo, b_hi, out_ref):
    f32 = jnp.float32
    half = p_lo.shape[1]
    lo = p_lo[...].astype(f32) + a_lo[...].astype(f32) + b_lo[...].astype(f32)
    hi = p_hi[...].astype(f32) + a_hi[...].astype(f32) + b_hi[...].astype(f32)
    out_ref[:, :half] = lo.astype(jnp.bfloat16)
    out_ref[:, half:] = hi.astype(jnp.bfloat16)


def final_sum(*parts):
    rows, half = parts[0].shape
    block = 32
    return pl.pallas_call(
        final_body,
        grid=(rows // block,),
        in_specs=[pl.BlockSpec((block, half), lambda i: (i, 0))] * 6,
        out_specs=pl.BlockSpec((block, 2 * half), lambda i: (i, 0)),
        out_shape=jax.ShapeDtypeStruct((rows, 2 * half), jnp.bfloat16),
        cost_estimate=cost(6 * rows * half, 16 * rows * half),
        compiler_params=pltpu.CompilerParams(vmem_limit_bytes=24 * MIB),
        name="final_sum",
    )(*parts)


def add_body(a0, b0, a1, b1, out0, out1):
    f32 = jnp.float32
    out0[...] = (a0[...].astype(f32) + b0[...].astype(f32)).astype(jnp.bfloat16)
    out1[...] = (a1[...].astype(f32) + b1[...].astype(f32)).astype(jnp.bfloat16)


def add_two(a0, b0, a1, b1, block=32):
    rows, width = a0.shape
    one = pl.BlockSpec((block, width), lambda i: (i, 0))
    return pl.pallas_call(
        add_body,
        grid=(rows // block,),
        in_specs=[one] * 4,
        out_specs=[one] * 2,
        out_shape=[jax.ShapeDtypeStruct((rows, width), jnp.bfloat16)] * 2,
        cost_estimate=cost(2 * rows * width, 12 * rows * width),
        compiler_params=pltpu.CompilerParams(vmem_limit_bytes=16 * MIB),
        name="add_two",
    )(a0, b0, a1, b1)


def shards(tokens, norm_gain, w_qkv, w_out, doc_lengths, span_slots):
    ctx = lax.axis_index("ctx")
    tp = lax.axis_index("tp")
    x, y, z, core = ctx // 2, ctx % 2, tp // 2, tp % 2
    piece = tokens.shape[0] // 2
    gain = norm_gain.reshape(1, -1)

    n_spans = span_slots.shape[0]
    per_span = 4
    span = per_span * TILE
    ends = jnp.cumsum(doc_lengths).astype(jnp.int32)
    numbers = jnp.arange(n_spans, dtype=jnp.int32)
    slot_of = jnp.sum(
        jnp.where(span_slots[None, :] == numbers[:, None], numbers[None, :], 0), axis=1
    )
    tile_no = jnp.arange(per_span, dtype=jnp.int32)[None, :]
    slot = slot_of[:, None]
    tile_tp = (slot % 2) * per_span + tile_no
    rank = slot // 2
    rel_z = (tile_tp // 2 - z) % NZ
    z_base = jnp.where(rel_z == 0, Z_BASE[0], 0)
    for i in range(1, NZ):
        z_base = jnp.where(rel_z == i, Z_BASE[i], z_base)
    rel_src = ((rank // 2 - x) % NX) * 2 + (rank % 2 != y).astype(jnp.int32)
    table = rel_src * 1024 + z_base + (tile_tp % 2 != core).astype(jnp.int32) * TILE
    table = table.reshape(-1).astype(jnp.int32)
    own_spans = lax.dynamic_slice_in_dim(span_slots, 2 * ctx, 2, 0)

    def starts_of(*dzs):
        tps = jnp.stack([((z + dz) % NZ) * 2 + c for dz in dzs for c in (core, 1 - core)])
        blocks = jnp.where(tps // per_span == 0, own_spans[0], own_spans[1])
        return (blocks * span + (tps % per_span) * TILE).astype(jnp.int32)

    starts_d, starts_b, starts_a = starts_of(2), starts_of(-1, 1), starts_of(0)
    rows = norm(tokens, gain)
    low, high = z_send(rows, 1), z_send(rows, -1)
    pairs = [[2 * i, 2 * i + 1] for i in range(NZ)]
    w_pair = in_hbm(lax.all_gather(w_out, "tp", axis=0, tiled=True, axis_index_groups=pairs))
    w_qkv = in_hbm(w_qkv)
    core_arg = core.reshape(1).astype(jnp.int32)
    rows, table, ends, starts_d, starts_b, starts_a, core_arg = lax.optimization_barrier(
        (rows, table, ends, starts_d, starts_b, starts_a, core_arg)
    )
    q_a, kv_a = project([rows, swap(rows)], w_qkv, 0, (QW, 2 * HD))
    all_a = x_all(y_pair(kv_a))
    far0, far1 = z_send(low[:piece], 1), z_send(high[piece:], -1)
    low, high, w_pair, q_a, *all_a = lax.optimization_barrier((low, high, w_pair, q_a, *all_a))
    group_b = [in_hbm(one) for one in (low, swap(low), high, swap(high))]
    (kv_b,) = project(group_b, w_qkv, QW, (2 * HD,))
    pair_b = y_pair(kv_b)
    all_b = x_all(pair_b)
    far0, far1, all_b[1] = lax.optimization_barrier((far0, far1, all_b[1]))
    group_d = [far0, far1, swap(far0), swap(far1)]
    (kv_d,) = project(group_d, w_qkv, QW, (2 * HD,))
    pair_d = y_pair(kv_d)
    *group_b, pair_d = lax.optimization_barrier((*group_b, pair_d))
    (q_d,) = project(group_d, w_qkv, 0, (QW,))
    (q_b,) = project(group_b, w_qkv, 0, (QW,))
    q_d, q_b = lax.optimization_barrier((q_d, q_b))
    kvs, places = [], []
    for group, base in ((all_a, 0), (all_b, 256), (x_all(pair_d), 768)):
        count = group[0].shape[0] // 2
        for i, one in enumerate(group):
            for j in range(2):
                places.append((len(kvs), j * count, (2 * i + j) * 1024 + base, count))
            kvs.append(one)

    d_own, d_send, packed = attend(q_d, kvs, tuple(places), True, table, ends, starts_d, 1024)
    d_sib = swap(d_send)
    (d_lo,) = out_project(core_arg, d_own, d_sib, w_pair, 0)
    (d_hi,) = out_project(core_arg, d_own, d_sib, w_pair, 1)
    from_low, from_high = z_send(d_lo, 1), z_send(d_hi, -1)
    whole = ((0, 0, 0, packed.shape[0]),)
    q_b, packed, d_lo, d_hi = lax.optimization_barrier((q_b, packed, d_lo, d_hi))
    b_own, b_send = attend(q_b, [packed], whole, False, table, ends, starts_b, 1024)
    b_sib = swap(b_send)
    prev_lo, next_lo = out_project(core_arg, b_own, b_sib, w_pair, 0)
    prev_hi, next_hi = out_project(core_arg, b_own, b_sib, w_pair, 1)
    early_hi, early_lo = z_send(next_hi, 1), z_send(prev_lo, -1)
    q_a, packed, next_hi, prev_hi, next_lo, prev_lo = lax.optimization_barrier(
        (q_a, packed, next_hi, prev_hi, next_lo, prev_lo)
    )
    sum_lo, sum_hi = add_two(next_lo, from_low, prev_hi, from_high)
    late_lo, late_hi = z_send(sum_lo, 1), z_send(sum_hi, -1)
    a_own, a_send = attend(q_a, [packed], whole, False, table, ends, starts_a, 1024)
    a_sib = swap(a_send)
    (a_lo,) = out_project(core_arg, a_own, a_sib, w_pair, 0)
    (a_hi,) = out_project(core_arg, a_own, a_sib, w_pair, 1)
    return final_sum(a_lo, a_hi, early_lo, early_hi, late_lo, late_hi)


def solution(mesh):
    placed = (P(("dp", "ctx", "tp"), None), P(), P(None, "tp"), P("tp", None), P("dp"), P("dp"))
    return jax.shard_map(
        shards, mesh=mesh, in_specs=placed, out_specs=P(("dp", "ctx", "tp"), None), check_vma=False
    )
```

```python
import functools

import jax
import jax.numpy as jnp
from jax import lax
from jax.experimental import pallas as pl
from jax.experimental.pallas import tpu as pltpu
from jax.sharding import PartitionSpec as P

HD = 128
GROUP = 4
QW = GROUP * HD
NZ = 4
NX = 4
TILE = 128
KTILE = 256
MIB = 1 << 20
MASKED = -3e38
LOWEST = -2e31
SHARE = 1e-4
LOG2E = 1.4426950408889634

Z_BASE = (0, 512, 768, 256)


def z_perm(dz, dc):
    return [
        (z * 2 + c, ((z + dz) % NZ) * 2 + (c + dc) % 2) for z in range(NZ) for c in range(2)
    ]


def x_perm(dx, dy):
    return [
        (x * 2 + y, ((x + dx) % NX) * 2 + (y + dy) % 2) for x in range(NX) for y in range(2)
    ]


def z_send(value, dz):
    return lax.ppermute(value, "tp", z_perm(dz, 0))


def swap(value):
    return lax.ppermute(value, "tp", z_perm(0, 1))


def x_send(value, dx):
    return lax.ppermute(value, "ctx", x_perm(dx, 0))


def y_swap(value):
    return lax.ppermute(value, "ctx", x_perm(0, 1))


def in_hbm(value):
    return pltpu.with_memory_space_constraint(value, pltpu.HBM)


def cost(flops, nbytes, trans=0):
    return pl.CostEstimate(
        flops=int(flops * SHARE), bytes_accessed=int(nbytes * SHARE), transcendentals=int(trans * SHARE)
    )


def norm_body(x_ref, gain_ref, out_ref):
    x = x_ref[...].astype(jnp.float32)
    mean_sq = jnp.mean(x * x, axis=-1, keepdims=True)
    out_ref[...] = (x * lax.rsqrt(mean_sq + 1e-05) * gain_ref[...]).astype(jnp.bfloat16)


def norm(tokens, gain, block=32):
    rows, width = tokens.shape
    return pl.pallas_call(
        norm_body,
        grid=(rows // block,),
        in_specs=[
            pl.BlockSpec((block, width), lambda i: (i, 0)),
            pl.BlockSpec((1, width), lambda i: (0, 0)),
        ],
        out_specs=pl.BlockSpec((block, width), lambda i: (i, 0)),
        out_shape=jax.ShapeDtypeStruct((rows, width), jnp.bfloat16),
        cost_estimate=cost(6 * rows * width, 4 * rows * width),
        compiler_params=pltpu.CompilerParams(vmem_limit_bytes=16 * MIB),
        name="norm",
    )(tokens, gain)


def project_body(n_in, first, widths, depth, ahead, *refs):
    xs, w_hbm = refs[:n_in], refs[n_in]
    outs = refs[n_in + 1 : -2]
    w_v, sem = refs[-2:]
    total = sum(widths)
    chunks = [
        pltpu.make_async_copy(
            w_hbm.at[pl.ds(k * depth, depth), pl.ds(first, total)],
            w_v.at[pl.ds(k * depth, depth)],
            sem.at[k],
        )
        for k in range(w_v.shape[0] // depth)
    ]
    for one in chunks[:ahead]:
        one.start()
    acc = None
    for k, one in enumerate(chunks):
        if k + ahead < len(chunks):
            chunks[k + ahead].start()
        one.wait()
        span = slice(k * depth, (k + 1) * depth)
        part = jnp.dot(
            jnp.concatenate([x[:, span] for x in xs], axis=0),
            w_v[span, :],
            preferred_element_type=jnp.float32,
        )
        acc = part if acc is None else acc + part
    at = 0
    for out, width in zip(outs, widths):
        out[...] = acc[:, at : at + width].astype(jnp.bfloat16)
        at += width


def project(xs, w, first, widths, depth=1024, ahead=4):
    total = sum(widths)
    rows = sum(x.shape[0] for x in xs)
    width = w.shape[0]
    vmem = pl.BlockSpec(memory_space=pltpu.VMEM)
    return pl.pallas_call(
        functools.partial(project_body, len(xs), first, widths, depth, ahead),
        in_specs=[vmem] * len(xs) + [pl.BlockSpec(memory_space=pl.ANY)],
        out_specs=[vmem] * len(widths),
        out_shape=[jax.ShapeDtypeStruct((rows, one), jnp.bfloat16) for one in widths],
        scratch_shapes=[
            pltpu.VMEM((width, total), jnp.bfloat16),
            pltpu.SemaphoreType.DMA((width // depth,)),
        ],
        cost_estimate=cost(2 * rows * width * total, 2 * width * (rows + total)),
        compiler_params=pltpu.CompilerParams(
            vmem_limit_bytes=2 * width * (total + rows) + 10 * rows * total + 4 * MIB
        ),
        name="project",
    )(*xs, w)


def y_pair(kv):
    return jnp.concatenate([kv, y_swap(kv)], axis=0)


def x_ring(pair):
    half = pair.shape[0] // 2
    left, right = x_send(pair, 1), x_send(pair, -1)
    return [pair, right, (x_send(left[:half], 1), x_send(right[half:], -1)), left]


def x_all(pair):
    return [pair, x_send(pair, -1), x_send(pair, 2), x_send(pair, 1)]


def attend_body(n_doc, n_kv, places, pack, table_ref, ends_ref, starts_ref, q_ref, *refs):
    kv_hbm = refs[:n_kv]
    keep_ref, send_ref = refs[n_kv : n_kv + 2]
    kv = refs[n_kv + 2] if pack else kv_hbm[0]
    sem = refs[-1]
    pair = pl.program_id(0)

    if pack:
        copies = [
            pltpu.make_async_copy(
                kv_hbm[which].at[pl.ds(src, count)], kv.at[pl.ds(dst, count)], sem.at[i]
            )
            for i, (which, src, dst, count) in enumerate(places)
        ]

        @pl.when(pair == 0)
        def _():
            for one in copies:
                one.start()
            for one in copies:
                one.wait()

    rows = GROUP * TILE
    starts = [starts_ref[2 * pair + j] for j in range(2)]
    low = jnp.minimum(starts[0], starts[1])
    high = jnp.maximum(starts[0], starts[1]) + TILE - 1
    offset = lax.rem(lax.broadcasted_iota(jnp.int32, (1, rows), 1), TILE)
    q_pos = [start + offset for start in starts]
    doc_start = [jnp.zeros((1, rows), jnp.int32) for _ in range(2)]
    first, last = jnp.int32(0), jnp.int32(0)
    for i in range(n_doc):
        end = ends_ref[i]
        doc_start = [jnp.where(q_pos[j] >= end, end, doc_start[j]) for j in range(2)]
        first = jnp.where(low >= end, end, first)
        last = jnp.where(high >= end, end, last)
    q_t = []
    for j in range(2):
        block = q_ref[j * TILE : (j + 1) * TILE].astype(jnp.float32)
        q_t.append(
            jnp.concatenate(
                [block[:, h * HD : (h + 1) * HD].T for h in range(GROUP)], axis=1
            ).astype(jnp.bfloat16)
        )
    scale = LOG2E / HD**0.5
    ratio = KTILE // TILE
    k_iota = lax.broadcasted_iota(jnp.int32, (KTILE, rows), 0)

    def step(at, state, masked):
        spots = [pl.multiple_of(table_ref[at * ratio + i], TILE) for i in range(ratio)]
        keys = jnp.concatenate([kv[pl.ds(spot, TILE), :HD] for spot in spots], axis=0)
        vals = jnp.concatenate([kv[pl.ds(spot, TILE), HD:] for spot in spots], axis=0)
        scores = [jnp.dot(keys, q_t[j], preferred_element_type=jnp.float32) for j in range(2)]
        out = []
        for j in range(2):
            top, total, acc = state[j]
            s = scores[j]
            if masked:
                base = at * KTILE
                allowed = (k_iota <= q_pos[j] - base) & (k_iota >= doc_start[j] - base)
                s = jnp.where(allowed, s, MASKED)
            new_top = jnp.maximum(top, jnp.max(s, axis=0, keepdims=True))
            e = jnp.exp2((s - new_top) * scale)
            factor = jnp.exp2((top - new_top) * scale)
            total = total * factor + jnp.sum(e, axis=0, keepdims=True)
            acc = acc * factor + lax.dot_general(
                vals,
                e.astype(jnp.bfloat16),
                (((0,), (0,)), ((), ())),
                preferred_element_type=jnp.float32,
            )
            out.append((new_top, total, acc))
        return tuple(out)

    state = tuple(
        (
            jnp.full((1, rows), LOWEST, jnp.float32),
            jnp.zeros((1, rows), jnp.float32),
            jnp.zeros((HD, rows), jnp.float32),
        )
        for _ in range(2)
    )
    begin, stop = first // KTILE, high // KTILE + 1
    inner = (last + KTILE - 1) // KTILE
    outer = jnp.maximum(inner, low // KTILE)
    masked_step = functools.partial(step, masked=True)
    state = lax.fori_loop(begin, jnp.minimum(inner, stop), masked_step, state)
    state = lax.fori_loop(inner, outer, functools.partial(step, masked=False), state)
    state = lax.fori_loop(outer, stop, masked_step, state)
    for (top, total, acc), out_ref in zip(state, (keep_ref, send_ref)):
        out_t = acc / total
        out_ref[...] = jnp.concatenate(
            [out_t[:, h * TILE : (h + 1) * TILE].T for h in range(GROUP)], axis=1
        ).astype(jnp.bfloat16)


def attend(q, kvs, places, pack, table, ends, starts, span):
    pairs = q.shape[0] // (2 * TILE)
    half = q.shape[0] // 2
    count = sum(place[3] for place in places)
    anywhere = pl.BlockSpec(memory_space=pl.ANY)
    vmem = pl.BlockSpec(memory_space=pltpu.VMEM)
    spec = pltpu.PrefetchScalarGridSpec(
        num_scalar_prefetch=3,
        grid=(pairs,),
        in_specs=[pl.BlockSpec((2 * TILE, QW), lambda i, *_: (i, 0))]
        + [anywhere if pack else vmem] * len(kvs),
        out_specs=[pl.BlockSpec((TILE, QW), lambda i, *_: (i, 0))] * 2 + [vmem] * pack,
        scratch_shapes=[pltpu.SemaphoreType.DMA((len(places),))],
    )
    return pl.pallas_call(
        functools.partial(attend_body, ends.shape[0], len(kvs), places, pack),
        grid_spec=spec,
        out_shape=[jax.ShapeDtypeStruct((half, QW), jnp.bfloat16)] * 2
        + [jax.ShapeDtypeStruct((count, 2 * HD), jnp.bfloat16)] * pack,
        cost_estimate=cost(
            2 * pairs * 4 * GROUP * TILE * span * HD * 2,
            count * 4 * HD + q.size * 4,
            2 * pairs * GROUP * TILE * span,
        ),
        compiler_params=pltpu.CompilerParams(vmem_limit_bytes=16 * MIB),
        name="attend",
    )(table, ends, starts, q, *kvs)


def out_body(first, step, own_ref, sib_ref, w_own, w_sib, *outs):
    own, sib = own_ref[...], sib_ref[...]
    for n in range(outs[0].shape[1] // step):
        columns = slice(first + n * step, first + (n + 1) * step)
        sums = jnp.dot(own, w_own[:, columns], preferred_element_type=jnp.float32)
        sums += jnp.dot(sib, w_sib[:, columns], preferred_element_type=jnp.float32)
        for i, out in enumerate(outs):
            out[:, n * step : (n + 1) * step] = sums[i * TILE : (i + 1) * TILE].astype(jnp.bfloat16)


def out_project(own, sib, w_own, w_sib, half, step=512):
    depth, width = w_own.shape
    part = width // 2
    rows = own.shape[0]
    n_out = rows // TILE
    vmem = pl.BlockSpec(memory_space=pltpu.VMEM)
    return pl.pallas_call(
        functools.partial(out_body, half * part, step),
        in_specs=[vmem] * 4,
        out_specs=[vmem] * n_out,
        out_shape=[jax.ShapeDtypeStruct((TILE, part), jnp.bfloat16)] * n_out,
        cost_estimate=cost(
            4 * rows * depth * part, 4 * depth * part + 4 * rows * depth + 2 * rows * part
        ),
        compiler_params=pltpu.CompilerParams(vmem_limit_bytes=24 * MIB),
        name="out_project",
    )(own, sib, w_own, w_sib)


def final_body(p_lo, p_hi, a_lo, a_hi, b_lo, b_hi, out_ref):
    f32 = jnp.float32
    half = p_lo.shape[1]
    lo = p_lo[...].astype(f32) + a_lo[...].astype(f32) + b_lo[...].astype(f32)
    hi = p_hi[...].astype(f32) + a_hi[...].astype(f32) + b_hi[...].astype(f32)
    out_ref[:, :half] = lo.astype(jnp.bfloat16)
    out_ref[:, half:] = hi.astype(jnp.bfloat16)


def final_sum(*parts):
    rows, half = parts[0].shape
    block = 32
    return pl.pallas_call(
        final_body,
        grid=(rows // block,),
        in_specs=[pl.BlockSpec((block, half), lambda i: (i, 0))] * 6,
        out_specs=pl.BlockSpec((block, 2 * half), lambda i: (i, 0)),
        out_shape=jax.ShapeDtypeStruct((rows, 2 * half), jnp.bfloat16),
        cost_estimate=cost(6 * rows * half, 16 * rows * half),
        compiler_params=pltpu.CompilerParams(vmem_limit_bytes=24 * MIB),
        name="final_sum",
    )(*parts)


def add_body(a0, b0, a1, b1, out0, out1):
    f32 = jnp.float32
    out0[...] = (a0[...].astype(f32) + b0[...].astype(f32)).astype(jnp.bfloat16)
    out1[...] = (a1[...].astype(f32) + b1[...].astype(f32)).astype(jnp.bfloat16)


def add_two(a0, b0, a1, b1, block=32):
    rows, width = a0.shape
    one = pl.BlockSpec((block, width), lambda i: (i, 0))
    return pl.pallas_call(
        add_body,
        grid=(rows // block,),
        in_specs=[one] * 4,
        out_specs=[one] * 2,
        out_shape=[jax.ShapeDtypeStruct((rows, width), jnp.bfloat16)] * 2,
        cost_estimate=cost(2 * rows * width, 12 * rows * width),
        compiler_params=pltpu.CompilerParams(vmem_limit_bytes=16 * MIB),
        name="add_two",
    )(a0, b0, a1, b1)


def shards(tokens, norm_gain, w_qkv, w_out, doc_lengths, span_slots):
    ctx = lax.axis_index("ctx")
    tp = lax.axis_index("tp")
    x, y, z, core = ctx // 2, ctx % 2, tp // 2, tp % 2
    piece = tokens.shape[0] // 2
    gain = norm_gain.reshape(1, -1)
    rows = norm(tokens, gain)
    low, high = z_send(rows, 1), z_send(rows, -1)
    sib_rows = swap(rows)
    w_sib = swap(w_out)
    sib_rows, doc_lengths, span_slots = lax.optimization_barrier((sib_rows, doc_lengths, span_slots))

    n_spans = span_slots.shape[0]
    per_span = 4
    span = per_span * TILE
    ends = jnp.cumsum(doc_lengths).astype(jnp.int32)
    numbers = jnp.arange(n_spans, dtype=jnp.int32)
    slot_of = jnp.sum(
        jnp.where(span_slots[None, :] == numbers[:, None], numbers[None, :], 0), axis=1
    )
    tile_no = jnp.arange(per_span, dtype=jnp.int32)[None, :]
    slot = slot_of[:, None]
    tile_tp = (slot % 2) * per_span + tile_no
    rank = slot // 2
    rel_z = (tile_tp // 2 - z) % NZ
    z_base = jnp.where(rel_z == 0, Z_BASE[0], 0)
    for i in range(1, NZ):
        z_base = jnp.where(rel_z == i, Z_BASE[i], z_base)
    rel_src = ((rank // 2 - x) % NX) * 2 + (rank % 2 != y).astype(jnp.int32)
    table = rel_src * 1024 + z_base + (tile_tp % 2 != core).astype(jnp.int32) * TILE
    table = table.reshape(-1).astype(jnp.int32)
    own_spans = lax.dynamic_slice_in_dim(span_slots, 2 * ctx, 2, 0)

    def starts_of(*dzs):
        tps = jnp.stack([((z + dz) % NZ) * 2 + c for dz in dzs for c in (core, 1 - core)])
        blocks = jnp.where(tps // per_span == 0, own_spans[0], own_spans[1])
        return (blocks * span + (tps % per_span) * TILE).astype(jnp.int32)

    starts_d, starts_b, starts_a = starts_of(2), starts_of(-1, 1), starts_of(0)
    w_qkv = in_hbm(w_qkv)
    q_a, kv_a = project([rows, sib_rows], w_qkv, 0, (QW, 2 * HD))
    all_a = x_all(y_pair(kv_a))
    far0, far1 = low[:piece], high[piece:]
    low, high, far0, far1, w_sib, table, ends, starts_d, starts_b, starts_a, q_a, *all_a = (
        lax.optimization_barrier(
            (low, high, far0, far1, w_sib, table, ends, starts_d, starts_b, starts_a, q_a, *all_a)
        )
    )
    far0, far1 = z_send(far0, 1), z_send(far1, -1)
    group_b = [low, swap(low), high, swap(high)]
    (kv_b,) = project(group_b, w_qkv, QW, (2 * HD,))
    pair_b = y_pair(kv_b)
    all_b = x_ring(pair_b)
    far0, far1, pair_b = lax.optimization_barrier((far0, far1, pair_b))
    group_d = [far0, far1, swap(far0), swap(far1)]
    (kv_d,) = project(group_d, w_qkv, QW, (2 * HD,))
    pair_d = y_pair(kv_d)
    *group_b, pair_d = lax.optimization_barrier((*group_b, pair_d))
    (q_d,) = project(group_d, w_qkv, 0, (QW,))
    (q_b,) = project(group_b, w_qkv, 0, (QW,))
    q_d, q_b = lax.optimization_barrier((q_d, q_b))
    kvs, places = [], []
    for group, base in ((all_a, 0), (all_b, 256), (x_all(pair_d), 768)):
        count = group[0].shape[0] // 2
        for i, one in enumerate(group):
            for j in range(2):
                dst = (2 * i + j) * 1024 + base
                if isinstance(one, tuple):
                    places.append((len(kvs), 0, dst, count))
                    kvs.append(one[j])
                else:
                    places.append((len(kvs), j * count, dst, count))
            if not isinstance(one, tuple):
                kvs.append(one)

    d_own, d_send, packed = attend(q_d, kvs, tuple(places), True, table, ends, starts_d, 1024)
    d_sib = swap(d_send)
    (d_lo,) = out_project(d_own, d_sib, w_out, w_sib, 0)
    (d_hi,) = out_project(d_own, d_sib, w_out, w_sib, 1)
    from_low, from_high = z_send(d_lo, 1), z_send(d_hi, -1)
    whole = ((0, 0, 0, packed.shape[0]),)
    q_b, packed, d_lo, d_hi = lax.optimization_barrier((q_b, packed, d_lo, d_hi))
    b_own, b_send = attend(q_b, [packed], whole, False, table, ends, starts_b, 1024)
    b_sib = swap(b_send)
    prev_lo, next_lo = out_project(b_own, b_sib, w_out, w_sib, 0)
    prev_hi, next_hi = out_project(b_own, b_sib, w_out, w_sib, 1)
    early_hi, early_lo = z_send(next_hi, 1), z_send(prev_lo, -1)
    q_a, packed, next_hi, prev_hi, next_lo, prev_lo = lax.optimization_barrier(
        (q_a, packed, next_hi, prev_hi, next_lo, prev_lo)
    )
    sum_lo, sum_hi = add_two(next_lo, from_low, prev_hi, from_high)
    late_lo, late_hi = z_send(sum_lo, 1), z_send(sum_hi, -1)
    a_own, a_send = attend(q_a, [packed], whole, False, table, ends, starts_a, 1024)
    a_sib = swap(a_send)
    (a_lo,) = out_project(a_own, a_sib, w_out, w_sib, 0)
    (a_hi,) = out_project(a_own, a_sib, w_out, w_sib, 1)
    return final_sum(a_lo, a_hi, early_lo, early_hi, late_lo, late_hi)


def solution(mesh):
    placed = (P(("dp", "ctx", "tp"), None), P(), P(None, "tp"), P("tp", None), P("dp"), P("dp"))
    return jax.shard_map(
        shards, mesh=mesh, in_specs=placed, out_specs=P(("dp", "ctx", "tp"), None), check_vma=False
    )
```

```python
import functools

import jax
import jax.numpy as jnp
from jax import lax
from jax.experimental import pallas as pl
from jax.experimental.pallas import tpu as pltpu
from jax.sharding import PartitionSpec as P

HD = 128
GROUP = 4
QW = GROUP * HD
NZ = 4
NX = 4
TILE = 128
KTILE = 256
MIB = 1 << 20
MASKED = -3e38
LOWEST = -2e31
SHARE = 1e-4
PROJECT_LIMIT = 8
LOG2E = 1.4426950408889634

Z_BASE = (0, 512, 768, 256)


def z_perm(dz, dc):
    return [
        (z * 2 + c, ((z + dz) % NZ) * 2 + (c + dc) % 2) for z in range(NZ) for c in range(2)
    ]


def x_perm(dx, dy):
    return [
        (x * 2 + y, ((x + dx) % NX) * 2 + (y + dy) % 2) for x in range(NX) for y in range(2)
    ]


def z_send(value, dz):
    return lax.ppermute(value, "tp", z_perm(dz, 0))


def swap(value):
    return lax.ppermute(value, "tp", z_perm(0, 1))


def x_send(value, dx):
    return lax.ppermute(value, "ctx", x_perm(dx, 0))


def y_swap(value):
    return lax.ppermute(value, "ctx", x_perm(0, 1))


def in_hbm(value):
    return pltpu.with_memory_space_constraint(value, pltpu.HBM)


def cost(flops, nbytes, trans=0):
    return pl.CostEstimate(
        flops=int(flops * SHARE), bytes_accessed=int(nbytes * SHARE), transcendentals=int(trans * SHARE)
    )


def norm_body(x_ref, gain_ref, out_ref):
    x = x_ref[...].astype(jnp.float32)
    mean_sq = jnp.mean(x * x, axis=-1, keepdims=True)
    out_ref[...] = (x * lax.rsqrt(mean_sq + 1e-05) * gain_ref[...]).astype(jnp.bfloat16)


def norm(tokens, gain, block=32):
    rows, width = tokens.shape
    return pl.pallas_call(
        norm_body,
        grid=(rows // block,),
        in_specs=[
            pl.BlockSpec((block, width), lambda i: (i, 0)),
            pl.BlockSpec((1, width), lambda i: (0, 0)),
        ],
        out_specs=pl.BlockSpec((block, width), lambda i: (i, 0)),
        out_shape=jax.ShapeDtypeStruct((rows, width), jnp.bfloat16),
        cost_estimate=cost(6 * rows * width, 4 * rows * width),
        compiler_params=pltpu.CompilerParams(vmem_limit_bytes=16 * MIB),
        name="norm",
    )(tokens, gain)


def load_body(n_in, *refs):
    sem = refs[-1]
    copies = [
        pltpu.make_async_copy(refs[i], refs[n_in + i], sem.at[i]) for i in range(n_in)
    ]
    for one in copies:
        one.start()
    for one in copies:
        one.wait()


def load(*values):
    n_in = len(values)
    return pl.pallas_call(
        functools.partial(load_body, n_in),
        in_specs=[pl.BlockSpec(memory_space=pl.ANY)] * n_in,
        out_specs=[pl.BlockSpec(memory_space=pltpu.VMEM)] * n_in,
        out_shape=[jax.ShapeDtypeStruct(one.shape, one.dtype) for one in values],
        scratch_shapes=[pltpu.SemaphoreType.DMA((n_in,))],
        cost_estimate=cost(1, 1),
        compiler_params=pltpu.CompilerParams(vmem_limit_bytes=2 * MIB),
        name="load",
    )(*values)


def project_body(n_in, first, widths, depth, *refs):
    xs, w_ref = refs[:n_in], refs[n_in]
    outs = refs[n_in + 1 :]
    total = sum(widths)
    sums = [None] * n_in
    for k in range(w_ref.shape[0] // depth):
        span = slice(k * depth, (k + 1) * depth)
        for i, x in enumerate(xs):
            part = jnp.dot(
                x[:, span], w_ref[span, first : first + total], preferred_element_type=jnp.float32
            )
            sums[i] = part if sums[i] is None else sums[i] + part
    at = 0
    for out, width in zip(outs, widths):
        row = 0
        for one in sums:
            out[row : row + one.shape[0]] = one[:, at : at + width].astype(jnp.bfloat16)
            row += one.shape[0]
        at += width


def project(xs, w, first, widths, depth=2048):
    total = sum(widths)
    rows = sum(x.shape[0] for x in xs)
    width = w.shape[0]
    vmem = pl.BlockSpec(memory_space=pltpu.VMEM)
    return pl.pallas_call(
        functools.partial(project_body, len(xs), first, widths, depth),
        in_specs=[vmem] * (len(xs) + 1),
        out_specs=[vmem] * len(widths),
        out_shape=[jax.ShapeDtypeStruct((rows, one), jnp.bfloat16) for one in widths],
        cost_estimate=cost(2 * rows * width * total, 2 * width * (rows + total)),
        compiler_params=pltpu.CompilerParams(vmem_limit_bytes=PROJECT_LIMIT * MIB),
        name="project",
    )(*xs, w)


def y_pair(kv):
    return jnp.concatenate([kv, y_swap(kv)], axis=0)


def x_ring(pair):
    half = pair.shape[0] // 2
    left, right = x_send(pair, 1), x_send(pair, -1)
    return [pair, right, (x_send(left[:half], 1), x_send(right[half:], -1)), left]


def x_all(pair):
    return [pair, x_send(pair, -1), x_send(pair, 2), x_send(pair, 1)]


def attend_body(n_doc, n_kv, places, pack, table_ref, ends_ref, starts_ref, q_ref, *refs):
    kv_hbm = refs[:n_kv]
    keep_ref, send_ref = refs[n_kv : n_kv + 2]
    kv = refs[n_kv + 2] if pack else kv_hbm[0]
    sem = refs[-1]
    pair = pl.program_id(0)

    if pack:
        copies = [
            pltpu.make_async_copy(
                kv_hbm[which].at[pl.ds(src, count)], kv.at[pl.ds(dst, count)], sem.at[i]
            )
            for i, (which, src, dst, count) in enumerate(places)
        ]

        @pl.when(pair == 0)
        def _():
            for one in copies:
                one.start()
            for one in copies:
                one.wait()

    rows = GROUP * TILE
    starts = [starts_ref[2 * pair + j] for j in range(2)]
    low = jnp.minimum(starts[0], starts[1])
    high = jnp.maximum(starts[0], starts[1]) + TILE - 1
    offset = lax.rem(lax.broadcasted_iota(jnp.int32, (1, rows), 1), TILE)
    q_pos = [start + offset for start in starts]
    doc_start = [jnp.zeros((1, rows), jnp.int32) for _ in range(2)]
    first, last = jnp.int32(0), jnp.int32(0)
    for i in range(n_doc):
        end = ends_ref[i]
        doc_start = [jnp.where(q_pos[j] >= end, end, doc_start[j]) for j in range(2)]
        first = jnp.where(low >= end, end, first)
        last = jnp.where(high >= end, end, last)
    q_t = []
    for j in range(2):
        block = q_ref[j * TILE : (j + 1) * TILE].astype(jnp.float32)
        q_t.append(
            jnp.concatenate(
                [block[:, h * HD : (h + 1) * HD].T for h in range(GROUP)], axis=1
            ).astype(jnp.bfloat16)
        )
    scale = LOG2E / HD**0.5
    ratio = KTILE // TILE
    k_iota = lax.broadcasted_iota(jnp.int32, (KTILE, rows), 0)

    def step(at, state, masked):
        spots = [pl.multiple_of(table_ref[at * ratio + i], TILE) for i in range(ratio)]
        keys = jnp.concatenate([kv[pl.ds(spot, TILE), :HD] for spot in spots], axis=0)
        vals = jnp.concatenate([kv[pl.ds(spot, TILE), HD:] for spot in spots], axis=0)
        scores = [jnp.dot(keys, q_t[j], preferred_element_type=jnp.float32) for j in range(2)]
        out = []
        for j in range(2):
            top, total, acc = state[j]
            s = scores[j]
            if masked:
                base = at * KTILE
                allowed = (k_iota <= q_pos[j] - base) & (k_iota >= doc_start[j] - base)
                s = jnp.where(allowed, s, MASKED)
            new_top = jnp.maximum(top, jnp.max(s, axis=0, keepdims=True))
            e = jnp.exp2((s - new_top) * scale)
            factor = jnp.exp2((top - new_top) * scale)
            total = total * factor + jnp.sum(e, axis=0, keepdims=True)
            acc = acc * factor + lax.dot_general(
                vals,
                e.astype(jnp.bfloat16),
                (((0,), (0,)), ((), ())),
                preferred_element_type=jnp.float32,
            )
            out.append((new_top, total, acc))
        return tuple(out)

    state = tuple(
        (
            jnp.full((1, rows), LOWEST, jnp.float32),
            jnp.zeros((1, rows), jnp.float32),
            jnp.zeros((HD, rows), jnp.float32),
        )
        for _ in range(2)
    )
    begin, stop = first // KTILE, high // KTILE + 1
    inner = (last + KTILE - 1) // KTILE
    outer = jnp.maximum(inner, low // KTILE)
    masked_step = functools.partial(step, masked=True)
    state = lax.fori_loop(begin, jnp.minimum(inner, stop), masked_step, state)
    state = lax.fori_loop(inner, outer, functools.partial(step, masked=False), state)
    state = lax.fori_loop(outer, stop, masked_step, state)
    for (top, total, acc), out_ref in zip(state, (keep_ref, send_ref)):
        out_t = acc / total
        out_ref[...] = jnp.concatenate(
            [out_t[:, h * TILE : (h + 1) * TILE].T for h in range(GROUP)], axis=1
        ).astype(jnp.bfloat16)


def attend(q, kvs, places, pack, table, ends, starts, span):
    pairs = q.shape[0] // (2 * TILE)
    half = q.shape[0] // 2
    count = sum(place[3] for place in places)
    anywhere = pl.BlockSpec(memory_space=pl.ANY)
    vmem = pl.BlockSpec(memory_space=pltpu.VMEM)
    spec = pltpu.PrefetchScalarGridSpec(
        num_scalar_prefetch=3,
        grid=(pairs,),
        in_specs=[pl.BlockSpec((2 * TILE, QW), lambda i, *_: (i, 0))]
        + [anywhere if pack else vmem] * len(kvs),
        out_specs=[pl.BlockSpec((TILE, QW), lambda i, *_: (i, 0))] * 2 + [vmem] * pack,
        scratch_shapes=[pltpu.SemaphoreType.DMA((len(places),))],
    )
    return pl.pallas_call(
        functools.partial(attend_body, ends.shape[0], len(kvs), places, pack),
        grid_spec=spec,
        out_shape=[jax.ShapeDtypeStruct((half, QW), jnp.bfloat16)] * 2
        + [jax.ShapeDtypeStruct((count, 2 * HD), jnp.bfloat16)] * pack,
        cost_estimate=cost(
            2 * pairs * 4 * GROUP * TILE * span * HD * 2,
            count * 4 * HD + q.size * 4,
            2 * pairs * GROUP * TILE * span,
        ),
        compiler_params=pltpu.CompilerParams(vmem_limit_bytes=6 * MIB),
        name="attend",
    )(table, ends, starts, q, *kvs)


def out_body(first, step, own_ref, sib_ref, w_own, w_sib, *outs):
    own, sib = own_ref[...], sib_ref[...]
    for n in range(outs[0].shape[1] // step):
        columns = slice(first + n * step, first + (n + 1) * step)
        sums = jnp.dot(own, w_own[:, columns], preferred_element_type=jnp.float32)
        sums += jnp.dot(sib, w_sib[:, columns], preferred_element_type=jnp.float32)
        for i, out in enumerate(outs):
            out[:, n * step : (n + 1) * step] = sums[i * TILE : (i + 1) * TILE].astype(jnp.bfloat16)


def out_project(own, sib, w_own, w_sib, half, step=512):
    depth, width = w_own.shape
    part = width // 2
    rows = own.shape[0]
    n_out = rows // TILE
    vmem = pl.BlockSpec(memory_space=pltpu.VMEM)
    return pl.pallas_call(
        functools.partial(out_body, half * part, step),
        in_specs=[vmem] * 4,
        out_specs=[vmem] * n_out,
        out_shape=[jax.ShapeDtypeStruct((TILE, part), jnp.bfloat16)] * n_out,
        cost_estimate=cost(
            4 * rows * depth * part, 4 * depth * part + 4 * rows * depth + 2 * rows * part
        ),
        compiler_params=pltpu.CompilerParams(vmem_limit_bytes=4 * MIB),
        name="out_project",
    )(own, sib, w_own, w_sib)


def final_body(p_lo, p_hi, a_lo, a_hi, b_lo, b_hi, out_ref):
    f32 = jnp.float32
    half = p_lo.shape[1]
    lo = p_lo[...].astype(f32) + a_lo[...].astype(f32) + b_lo[...].astype(f32)
    hi = p_hi[...].astype(f32) + a_hi[...].astype(f32) + b_hi[...].astype(f32)
    out_ref[:, :half] = lo.astype(jnp.bfloat16)
    out_ref[:, half:] = hi.astype(jnp.bfloat16)


def final_sum(*parts):
    rows, half = parts[0].shape
    block = 32
    return pl.pallas_call(
        final_body,
        grid=(rows // block,),
        in_specs=[pl.BlockSpec((block, half), lambda i: (i, 0))] * 6,
        out_specs=pl.BlockSpec((block, 2 * half), lambda i: (i, 0)),
        out_shape=jax.ShapeDtypeStruct((rows, 2 * half), jnp.bfloat16),
        cost_estimate=cost(6 * rows * half, 16 * rows * half),
        compiler_params=pltpu.CompilerParams(vmem_limit_bytes=24 * MIB),
        name="final_sum",
    )(*parts)


def add_body(a0, b0, a1, b1, out0, out1):
    f32 = jnp.float32
    out0[...] = (a0[...].astype(f32) + b0[...].astype(f32)).astype(jnp.bfloat16)
    out1[...] = (a1[...].astype(f32) + b1[...].astype(f32)).astype(jnp.bfloat16)


def add_two(a0, b0, a1, b1, block=32):
    rows, width = a0.shape
    one = pl.BlockSpec((block, width), lambda i: (i, 0))
    return pl.pallas_call(
        add_body,
        grid=(rows // block,),
        in_specs=[one] * 4,
        out_specs=[one] * 2,
        out_shape=[jax.ShapeDtypeStruct((rows, width), jnp.bfloat16)] * 2,
        cost_estimate=cost(2 * rows * width, 12 * rows * width),
        compiler_params=pltpu.CompilerParams(vmem_limit_bytes=16 * MIB),
        name="add_two",
    )(a0, b0, a1, b1)


def shards(tokens, norm_gain, w_qkv, w_out, doc_lengths, span_slots):
    ctx = lax.axis_index("ctx")
    tp = lax.axis_index("tp")
    x, y, z, core = ctx // 2, ctx % 2, tp // 2, tp % 2
    piece = tokens.shape[0] // 2
    gain = norm_gain.reshape(1, -1)
    rows = norm(tokens, gain)
    low, high = z_send(rows, 1), z_send(rows, -1)
    sib_rows = swap(rows)
    w_sib = swap(w_out)
    sib_rows, doc_lengths, span_slots = lax.optimization_barrier((sib_rows, doc_lengths, span_slots))

    n_spans = span_slots.shape[0]
    per_span = 4
    span = per_span * TILE
    ends = jnp.cumsum(doc_lengths).astype(jnp.int32)
    numbers = jnp.arange(n_spans, dtype=jnp.int32)
    slot_of = jnp.sum(
        jnp.where(span_slots[None, :] == numbers[:, None], numbers[None, :], 0), axis=1
    )
    tile_no = jnp.arange(per_span, dtype=jnp.int32)[None, :]
    slot = slot_of[:, None]
    tile_tp = (slot % 2) * per_span + tile_no
    rank = slot // 2
    rel_z = (tile_tp // 2 - z) % NZ
    z_base = jnp.where(rel_z == 0, Z_BASE[0], 0)
    for i in range(1, NZ):
        z_base = jnp.where(rel_z == i, Z_BASE[i], z_base)
    rel_src = ((rank // 2 - x) % NX) * 2 + (rank % 2 != y).astype(jnp.int32)
    table = rel_src * 1024 + z_base + (tile_tp % 2 != core).astype(jnp.int32) * TILE
    table = table.reshape(-1).astype(jnp.int32)
    own_spans = lax.dynamic_slice_in_dim(span_slots, 2 * ctx, 2, 0)

    def starts_of(*dzs):
        tps = jnp.stack([((z + dz) % NZ) * 2 + c for dz in dzs for c in (core, 1 - core)])
        blocks = jnp.where(tps // per_span == 0, own_spans[0], own_spans[1])
        return (blocks * span + (tps % per_span) * TILE).astype(jnp.int32)

    starts_d, starts_b, starts_a = starts_of(2), starts_of(-1, 1), starts_of(0)
    q_a, kv_a = project([rows, sib_rows], w_qkv, 0, (QW, 2 * HD))
    pair_a = y_pair(kv_a)
    all_a = x_all(pair_a)
    w_out, w_sib, w_late, pair_a = lax.optimization_barrier((w_out, w_sib, w_qkv, pair_a))
    w_out, w_sib, w_late = load(in_hbm(w_out), in_hbm(w_sib), in_hbm(w_late))
    far0, far1 = low[:piece], high[piece:]
    low, high, far0, far1, w_out, w_sib, w_late, table, ends, starts_d, starts_b, starts_a, *all_a = (
        lax.optimization_barrier(
            (low, high, far0, far1, w_out, w_sib, w_late, table, ends, starts_d, starts_b, starts_a)
            + tuple(all_a)
        )
    )
    far0, far1 = z_send(far0, 1), z_send(far1, -1)
    group_b = [low, swap(low), high, swap(high)]
    (kv_b,) = project(group_b, w_late, QW, (2 * HD,))
    pair_b = y_pair(kv_b)
    all_b = x_ring(pair_b)
    far0, far1, pair_b = lax.optimization_barrier((far0, far1, pair_b))
    group_d = [far0, far1, swap(far0), swap(far1)]
    (kv_d,) = project(group_d, w_late, QW, (2 * HD,))
    pair_d = y_pair(kv_d)
    *group_b, pair_d = lax.optimization_barrier((*group_b, pair_d))
    (q_d,) = project(group_d, w_late, 0, (QW,))
    (q_b,) = project(group_b, w_late, 0, (QW,))
    q_d, q_b = lax.optimization_barrier((q_d, q_b))
    kvs, places = [], []
    for group, base in ((all_a, 0), (all_b, 256), (x_all(pair_d), 768)):
        count = group[0].shape[0] // 2
        for i, one in enumerate(group):
            for j in range(2):
                dst = (2 * i + j) * 1024 + base
                if isinstance(one, tuple):
                    places.append((len(kvs), 0, dst, count))
                    kvs.append(one[j])
                else:
                    places.append((len(kvs), j * count, dst, count))
            if not isinstance(one, tuple):
                kvs.append(one)

    d_own, d_send, packed = attend(q_d, kvs, tuple(places), True, table, ends, starts_d, 1024)
    d_sib = swap(d_send)
    (d_lo,) = out_project(d_own, d_sib, w_out, w_sib, 0)
    (d_hi,) = out_project(d_own, d_sib, w_out, w_sib, 1)
    from_low, from_high = z_send(d_lo, 1), z_send(d_hi, -1)
    whole = ((0, 0, 0, packed.shape[0]),)
    q_b, packed, d_lo, d_hi = lax.optimization_barrier((q_b, packed, d_lo, d_hi))
    b_own, b_send = attend(q_b, [packed], whole, False, table, ends, starts_b, 1024)
    b_sib = swap(b_send)
    prev_lo, next_lo = out_project(b_own, b_sib, w_out, w_sib, 0)
    prev_hi, next_hi = out_project(b_own, b_sib, w_out, w_sib, 1)
    early_hi, early_lo = z_send(next_hi, 1), z_send(prev_lo, -1)
    q_a, packed, next_hi, prev_hi, next_lo, prev_lo = lax.optimization_barrier(
        (q_a, packed, next_hi, prev_hi, next_lo, prev_lo)
    )
    sum_lo, sum_hi = add_two(next_lo, from_low, prev_hi, from_high)
    late_lo, late_hi = z_send(sum_lo, 1), z_send(sum_hi, -1)
    a_own, a_send = attend(q_a, [packed], whole, False, table, ends, starts_a, 1024)
    a_sib = swap(a_send)
    (a_lo,) = out_project(a_own, a_sib, w_out, w_sib, 0)
    (a_hi,) = out_project(a_own, a_sib, w_out, w_sib, 1)
    return final_sum(a_lo, a_hi, early_lo, early_hi, late_lo, late_hi)


def solution(mesh):
    placed = (P(("dp", "ctx", "tp"), None), P(), P(None, "tp"), P("tp", None), P("dp"), P("dp"))
    return jax.shard_map(
        shards, mesh=mesh, in_specs=placed, out_specs=P(("dp", "ctx", "tp"), None), check_vma=False
    )
```

```python
import functools

import jax
import jax.numpy as jnp
from jax import lax
from jax.experimental import pallas as pl
from jax.experimental.pallas import tpu as pltpu
from jax.sharding import PartitionSpec as P

HD = 128
GROUP = 4
QW = GROUP * HD
NZ = 4
NX = 4
TILE = 128
KTILE = 256
MIB = 1 << 20
MASKED = -3e38
LOWEST = -2e31
SHARE = 1e-4
LOG2E = 1.4426950408889634

Z_BASE = (0, 512, 768, 256)


def z_perm(dz, dc):
    return [
        (z * 2 + c, ((z + dz) % NZ) * 2 + (c + dc) % 2) for z in range(NZ) for c in range(2)
    ]


def x_perm(dx, dy):
    return [
        (x * 2 + y, ((x + dx) % NX) * 2 + (y + dy) % 2) for x in range(NX) for y in range(2)
    ]


def z_send(value, dz):
    return lax.ppermute(value, "tp", z_perm(dz, 0))


def swap(value):
    return lax.ppermute(value, "tp", z_perm(0, 1))


def x_send(value, dx):
    return lax.ppermute(value, "ctx", x_perm(dx, 0))


def y_swap(value):
    return lax.ppermute(value, "ctx", x_perm(0, 1))


def in_hbm(value):
    return pltpu.with_memory_space_constraint(value, pltpu.HBM)


def cost(flops, nbytes, trans=0):
    return pl.CostEstimate(
        flops=int(flops * SHARE), bytes_accessed=int(nbytes * SHARE), transcendentals=int(trans * SHARE)
    )


def norm_body(x_ref, gain_ref, out_ref):
    x = x_ref[...].astype(jnp.float32)
    mean_sq = jnp.mean(x * x, axis=-1, keepdims=True)
    out_ref[...] = (x * lax.rsqrt(mean_sq + 1e-05) * gain_ref[...]).astype(jnp.bfloat16)


def norm(tokens, gain, block=32):
    rows, width = tokens.shape
    return pl.pallas_call(
        norm_body,
        grid=(rows // block,),
        in_specs=[
            pl.BlockSpec((block, width), lambda i: (i, 0)),
            pl.BlockSpec((1, width), lambda i: (0, 0)),
        ],
        out_specs=pl.BlockSpec((block, width), lambda i: (i, 0)),
        out_shape=jax.ShapeDtypeStruct((rows, width), jnp.bfloat16),
        cost_estimate=cost(6 * rows * width, 4 * rows * width),
        compiler_params=pltpu.CompilerParams(vmem_limit_bytes=16 * MIB),
        name="norm",
    )(tokens, gain)


def load_body(firsts, *refs):
    n_in = len(firsts)
    sem = refs[-1]
    copies = []
    for i, first in enumerate(firsts):
        src, dst = refs[i], refs[n_in + i]
        copies.append(
            pltpu.make_async_copy(src.at[:, pl.ds(first, dst.shape[1])], dst, sem.at[i])
        )
    for one in copies:
        one.start()
    for one in copies:
        one.wait()


def load(values, windows):
    n_in = len(values)
    return pl.pallas_call(
        functools.partial(load_body, tuple(first for first, _ in windows)),
        in_specs=[pl.BlockSpec(memory_space=pl.ANY)] * n_in,
        out_specs=[pl.BlockSpec(memory_space=pltpu.VMEM)] * n_in,
        out_shape=[
            jax.ShapeDtypeStruct((one.shape[0], width), one.dtype)
            for one, (_, width) in zip(values, windows)
        ],
        scratch_shapes=[pltpu.SemaphoreType.DMA((n_in,))],
        cost_estimate=cost(1, 1),
        compiler_params=pltpu.CompilerParams(vmem_limit_bytes=2 * MIB),
        name="load",
    )(*[in_hbm(one) for one in values])


def project_body(n_in, first, widths, depth, *refs):
    xs, w_ref = refs[:n_in], refs[n_in]
    outs = refs[n_in + 1 :]
    total = sum(widths)
    halves = [xs[: n_in // 2], xs[n_in // 2 :]] if total <= 2 * HD else [xs]
    sums = [None] * len(halves)
    for k in range(w_ref.shape[0] // depth):
        span = slice(k * depth, (k + 1) * depth)
        for i, half in enumerate(halves):
            part = jnp.dot(
                jnp.concatenate([x[:, span] for x in half], axis=0),
                w_ref[span, first : first + total],
                preferred_element_type=jnp.float32,
            )
            sums[i] = part if sums[i] is None else sums[i] + part
    at = 0
    for out, width in zip(outs, widths):
        row = 0
        for one in sums:
            out[row : row + one.shape[0]] = one[:, at : at + width].astype(jnp.bfloat16)
            row += one.shape[0]
        at += width


def project(xs, w, first, widths, depth=2048):
    total = sum(widths)
    rows = sum(x.shape[0] for x in xs)
    width = w.shape[0]
    vmem = pl.BlockSpec(memory_space=pltpu.VMEM)
    return pl.pallas_call(
        functools.partial(project_body, len(xs), first, widths, depth),
        in_specs=[vmem] * (len(xs) + 1),
        out_specs=[vmem] * len(widths),
        out_shape=[jax.ShapeDtypeStruct((rows, one), jnp.bfloat16) for one in widths],
        cost_estimate=cost(2 * rows * width * total, 2 * width * (rows + total)),
        compiler_params=pltpu.CompilerParams(vmem_limit_bytes=6 * MIB + 4 * rows * total),
        name="project",
    )(*xs, w)


def y_pair(kv):
    return jnp.concatenate([kv, y_swap(kv)], axis=0)


def x_ring(pair):
    half = pair.shape[0] // 2
    left, right = x_send(pair, 1), x_send(pair, -1)
    return [pair, right, (x_send(left[:half], 1), x_send(right[half:], -1)), left]


def x_all(pair):
    return [pair, x_send(pair, -1), x_send(pair, 2), x_send(pair, 1)]


def attend_body(n_doc, n_kv, places, pack, table_ref, ends_ref, starts_ref, q_ref, *refs):
    pieces = refs[:n_kv]
    keep_ref, send_ref = refs[n_kv : n_kv + 2]
    kv = refs[n_kv + 2] if pack else pieces[0]
    pair = pl.program_id(0)

    if pack:

        @pl.when(pair == 0)
        def _():
            for which, src, dst, count in places:
                kv[dst : dst + count] = pieces[which][src : src + count]

    rows = GROUP * TILE
    starts = [starts_ref[2 * pair + j] for j in range(2)]
    low = jnp.minimum(starts[0], starts[1])
    high = jnp.maximum(starts[0], starts[1]) + TILE - 1
    offset = lax.rem(lax.broadcasted_iota(jnp.int32, (1, rows), 1), TILE)
    q_pos = [start + offset for start in starts]
    doc_start = [jnp.zeros((1, rows), jnp.int32) for _ in range(2)]
    first, last = jnp.int32(0), jnp.int32(0)
    for i in range(n_doc):
        end = ends_ref[i]
        doc_start = [jnp.where(q_pos[j] >= end, end, doc_start[j]) for j in range(2)]
        first = jnp.where(low >= end, end, first)
        last = jnp.where(high >= end, end, last)
    q_t = []
    for j in range(2):
        block = q_ref[j * TILE : (j + 1) * TILE].astype(jnp.float32)
        q_t.append(
            jnp.concatenate(
                [block[:, h * HD : (h + 1) * HD].T for h in range(GROUP)], axis=1
            ).astype(jnp.bfloat16)
        )
    scale = LOG2E / HD**0.5
    ratio = KTILE // TILE
    k_iota = lax.broadcasted_iota(jnp.int32, (KTILE, rows), 0)

    def step(at, state, masked):
        spots = [pl.multiple_of(table_ref[at * ratio + i], TILE) for i in range(ratio)]
        keys = jnp.concatenate([kv[pl.ds(spot, TILE), :HD] for spot in spots], axis=0)
        vals = jnp.concatenate([kv[pl.ds(spot, TILE), HD:] for spot in spots], axis=0)
        scores = [jnp.dot(keys, q_t[j], preferred_element_type=jnp.float32) for j in range(2)]
        out = []
        for j in range(2):
            top, total, acc = state[j]
            s = scores[j]
            if masked:
                base = at * KTILE
                allowed = (k_iota <= q_pos[j] - base) & (k_iota >= doc_start[j] - base)
                s = jnp.where(allowed, s, MASKED)
            new_top = jnp.maximum(top, jnp.max(s, axis=0, keepdims=True))
            e = jnp.exp2((s - new_top) * scale)
            factor = jnp.exp2((top - new_top) * scale)
            total = total * factor + jnp.sum(e, axis=0, keepdims=True)
            acc = acc * factor + lax.dot_general(
                vals,
                e.astype(jnp.bfloat16),
                (((0,), (0,)), ((), ())),
                preferred_element_type=jnp.float32,
            )
            out.append((new_top, total, acc))
        return tuple(out)

    state = tuple(
        (
            jnp.full((1, rows), LOWEST, jnp.float32),
            jnp.zeros((1, rows), jnp.float32),
            jnp.zeros((HD, rows), jnp.float32),
        )
        for _ in range(2)
    )
    begin, stop = first // KTILE, high // KTILE + 1
    inner = (last + KTILE - 1) // KTILE
    outer = jnp.maximum(inner, low // KTILE)
    masked_step = functools.partial(step, masked=True)
    state = lax.fori_loop(begin, jnp.minimum(inner, stop), masked_step, state)
    state = lax.fori_loop(inner, outer, functools.partial(step, masked=False), state)
    state = lax.fori_loop(outer, stop, masked_step, state)
    for (top, total, acc), out_ref in zip(state, (keep_ref, send_ref)):
        out_t = acc / total
        out_ref[...] = jnp.concatenate(
            [out_t[:, h * TILE : (h + 1) * TILE].T for h in range(GROUP)], axis=1
        ).astype(jnp.bfloat16)


def attend(q, first, pairs, kvs, places, pack, table, ends, starts, span):
    half = pairs * TILE
    count = sum(place[3] for place in places)
    vmem = pl.BlockSpec(memory_space=pltpu.VMEM)
    spec = pltpu.PrefetchScalarGridSpec(
        num_scalar_prefetch=3,
        grid=(pairs,),
        in_specs=[pl.BlockSpec((2 * TILE, QW), lambda i, *_: (first + i, 0))]
        + [vmem] * len(kvs),
        out_specs=[pl.BlockSpec((TILE, QW), lambda i, *_: (i, 0))] * 2 + [vmem] * pack,
    )
    return pl.pallas_call(
        functools.partial(attend_body, ends.shape[0], len(kvs), places, pack),
        grid_spec=spec,
        out_shape=[jax.ShapeDtypeStruct((half, QW), jnp.bfloat16)] * 2
        + [jax.ShapeDtypeStruct((count, 2 * HD), jnp.bfloat16)] * pack,
        cost_estimate=cost(
            2 * pairs * 4 * GROUP * TILE * span * HD * 2,
            count * 4 * HD + half * QW * 8,
            2 * pairs * GROUP * TILE * span,
        ),
        compiler_params=pltpu.CompilerParams(vmem_limit_bytes=6 * MIB),
        name="attend",
    )(table, ends, starts, q, *kvs)


def out_body(first, step, own_ref, sib_ref, w_own, w_sib, *outs):
    own, sib = own_ref[...], sib_ref[...]
    for n in range(outs[0].shape[1] // step):
        columns = slice(first + n * step, first + (n + 1) * step)
        sums = jnp.dot(own, w_own[:, columns], preferred_element_type=jnp.float32)
        sums += jnp.dot(sib, w_sib[:, columns], preferred_element_type=jnp.float32)
        for i, out in enumerate(outs):
            out[:, n * step : (n + 1) * step] = sums[i * TILE : (i + 1) * TILE].astype(jnp.bfloat16)


def out_project(own, sib, w_own, w_sib, half, step=512):
    depth, width = w_own.shape
    part = width // 2
    rows = own.shape[0]
    n_out = rows // TILE
    vmem = pl.BlockSpec(memory_space=pltpu.VMEM)
    return pl.pallas_call(
        functools.partial(out_body, half * part, step),
        in_specs=[vmem] * 4,
        out_specs=[vmem] * n_out,
        out_shape=[jax.ShapeDtypeStruct((TILE, part), jnp.bfloat16)] * n_out,
        cost_estimate=cost(
            4 * rows * depth * part, 4 * depth * part + 4 * rows * depth + 2 * rows * part
        ),
        compiler_params=pltpu.CompilerParams(vmem_limit_bytes=4 * MIB),
        name="out_project",
    )(own, sib, w_own, w_sib)


def final_body(p_lo, p_hi, a_lo, a_hi, b_lo, b_hi, out_ref):
    f32 = jnp.float32
    half = p_lo.shape[1]
    lo = p_lo[...].astype(f32) + a_lo[...].astype(f32) + b_lo[...].astype(f32)
    hi = p_hi[...].astype(f32) + a_hi[...].astype(f32) + b_hi[...].astype(f32)
    out_ref[:, :half] = lo.astype(jnp.bfloat16)
    out_ref[:, half:] = hi.astype(jnp.bfloat16)


def final_sum(*parts):
    rows, half = parts[0].shape
    block = 32
    return pl.pallas_call(
        final_body,
        grid=(rows // block,),
        in_specs=[pl.BlockSpec((block, half), lambda i: (i, 0))] * 6,
        out_specs=pl.BlockSpec((block, 2 * half), lambda i: (i, 0)),
        out_shape=jax.ShapeDtypeStruct((rows, 2 * half), jnp.bfloat16),
        cost_estimate=cost(6 * rows * half, 16 * rows * half),
        compiler_params=pltpu.CompilerParams(vmem_limit_bytes=24 * MIB),
        name="final_sum",
    )(*parts)


def add_body(a0, b0, a1, b1, out0, out1):
    f32 = jnp.float32
    out0[...] = (a0[...].astype(f32) + b0[...].astype(f32)).astype(jnp.bfloat16)
    out1[...] = (a1[...].astype(f32) + b1[...].astype(f32)).astype(jnp.bfloat16)


def add_two(a0, b0, a1, b1, block=32):
    rows, width = a0.shape
    one = pl.BlockSpec((block, width), lambda i: (i, 0))
    return pl.pallas_call(
        add_body,
        grid=(rows // block,),
        in_specs=[one] * 4,
        out_specs=[one] * 2,
        out_shape=[jax.ShapeDtypeStruct((rows, width), jnp.bfloat16)] * 2,
        cost_estimate=cost(2 * rows * width, 12 * rows * width),
        compiler_params=pltpu.CompilerParams(vmem_limit_bytes=16 * MIB),
        name="add_two",
    )(a0, b0, a1, b1)


def shards(tokens, norm_gain, w_qkv, w_out, doc_lengths, span_slots):
    ctx = lax.axis_index("ctx")
    tp = lax.axis_index("tp")
    x, y, z, core = ctx // 2, ctx % 2, tp // 2, tp % 2
    piece = tokens.shape[0] // 2
    gain = norm_gain.reshape(1, -1)
    rows = norm(in_hbm(tokens), in_hbm(gain))
    low, high = z_send(rows, 1), z_send(rows, -1)
    sib_rows = swap(rows)
    w_sib = swap(w_out)
    w_qkv, rows = lax.optimization_barrier((w_qkv, rows))
    (w_kv,) = load([w_qkv], [(QW, 2 * HD)])
    sib_rows, w_kv = lax.optimization_barrier((sib_rows, w_kv))
    sib_rows, doc_lengths, span_slots = lax.optimization_barrier((sib_rows, doc_lengths, span_slots))

    n_spans = span_slots.shape[0]
    per_span = 4
    span = per_span * TILE
    ends = jnp.cumsum(doc_lengths).astype(jnp.int32)
    numbers = jnp.arange(n_spans, dtype=jnp.int32)
    slot_of = jnp.sum(
        jnp.where(span_slots[None, :] == numbers[:, None], numbers[None, :], 0), axis=1
    )
    tile_no = jnp.arange(per_span, dtype=jnp.int32)[None, :]
    slot = slot_of[:, None]
    tile_tp = (slot % 2) * per_span + tile_no
    rank = slot // 2
    rel_z = (tile_tp // 2 - z) % NZ
    z_base = jnp.where(rel_z == 0, Z_BASE[0], 0)
    for i in range(1, NZ):
        z_base = jnp.where(rel_z == i, Z_BASE[i], z_base)
    rel_src = ((rank // 2 - x) % NX) * 2 + (rank % 2 != y).astype(jnp.int32)
    table = rel_src * 1024 + z_base + (tile_tp % 2 != core).astype(jnp.int32) * TILE
    table = table.reshape(-1).astype(jnp.int32)
    own_spans = lax.dynamic_slice_in_dim(span_slots, 2 * ctx, 2, 0)

    def starts_of(*dzs):
        tps = jnp.stack([((z + dz) % NZ) * 2 + c for dz in dzs for c in (core, 1 - core)])
        blocks = jnp.where(tps // per_span == 0, own_spans[0], own_spans[1])
        return (blocks * span + (tps % per_span) * TILE).astype(jnp.int32)

    starts_d, starts_b, starts_a = starts_of(2), starts_of(-1, 1), starts_of(0)
    (kv_a,) = project([rows, sib_rows], w_kv, 0, (2 * HD,))
    pair_a = y_pair(kv_a)
    all_a = x_all(pair_a)
    far0, far1 = low[:piece], high[piece:]
    low, high, far0, far1, w_sib, table, ends, starts_d, starts_b, starts_a, *all_a = (
        lax.optimization_barrier(
            (low, high, far0, far1, w_sib, table, ends, starts_d, starts_b, starts_a, *all_a)
        )
    )
    far0, far1 = z_send(far0, 1), z_send(far1, -1)
    group_b = [low, swap(low), high, swap(high)]
    (kv_b,) = project(group_b, w_kv, 0, (2 * HD,))
    pair_b = y_pair(kv_b)
    all_b = x_ring(pair_b)
    w_out, w_sib, pair_b = lax.optimization_barrier((w_out, w_sib, pair_b))
    w_out, w_sib = load([w_out, w_sib], [(0, w_out.shape[1])] * 2)
    far0, far1, w_out, w_sib = lax.optimization_barrier((far0, far1, w_out, w_sib))
    group_d = [far0, far1, swap(far0), swap(far1)]
    (kv_d,) = project(group_d, w_kv, 0, (2 * HD,))
    pair_d = y_pair(kv_d)
    every = [rows, sib_rows, *group_b, *group_d]
    *every, pair_d = lax.optimization_barrier((*every, pair_d))
    (q_all,) = project(every, w_qkv, 0, (QW,))
    kvs, places = [], []
    for group, base in ((all_a, 0), (all_b, 256), (x_all(pair_d), 768)):
        count = group[0].shape[0] // 2
        for i, one in enumerate(group):
            for j in range(2):
                dst = (2 * i + j) * 1024 + base
                if isinstance(one, tuple):
                    places.append((len(kvs), 0, dst, count))
                    kvs.append(one[j])
                else:
                    places.append((len(kvs), j * count, dst, count))
            if not isinstance(one, tuple):
                kvs.append(one)

    d_own, d_send, packed = attend(q_all, 3, 1, kvs, tuple(places), True, table, ends, starts_d, 1024)
    d_sib = swap(d_send)
    (d_lo,) = out_project(d_own, d_sib, w_out, w_sib, 0)
    (d_hi,) = out_project(d_own, d_sib, w_out, w_sib, 1)
    from_low, from_high = z_send(d_lo, 1), z_send(d_hi, -1)
    whole = ((0, 0, 0, packed.shape[0]),)
    packed, d_lo, d_hi = lax.optimization_barrier((packed, d_lo, d_hi))
    b_own, b_send = attend(q_all, 1, 2, [packed], whole, False, table, ends, starts_b, 1024)
    b_sib = swap(b_send)
    prev_lo, next_lo = out_project(b_own, b_sib, w_out, w_sib, 0)
    prev_hi, next_hi = out_project(b_own, b_sib, w_out, w_sib, 1)
    early_hi, early_lo = z_send(next_hi, 1), z_send(prev_lo, -1)
    packed, next_hi, prev_hi, next_lo, prev_lo = lax.optimization_barrier(
        (packed, next_hi, prev_hi, next_lo, prev_lo)
    )
    sum_lo, sum_hi = add_two(next_lo, from_low, prev_hi, from_high)
    late_lo, late_hi = z_send(sum_lo, 1), z_send(sum_hi, -1)
    a_own, a_send = attend(q_all, 0, 1, [packed], whole, False, table, ends, starts_a, 1024)
    a_sib = swap(a_send)
    (a_lo,) = out_project(a_own, a_sib, w_out, w_sib, 0)
    (a_hi,) = out_project(a_own, a_sib, w_out, w_sib, 1)
    return final_sum(a_lo, a_hi, early_lo, early_hi, late_lo, late_hi)


def solution(mesh):
    placed = (P(("dp", "ctx", "tp"), None), P(), P(None, "tp"), P("tp", None), P("dp"), P("dp"))
    return jax.shard_map(
        shards, mesh=mesh, in_specs=placed, out_specs=P(("dp", "ctx", "tp"), None), check_vma=False
    )
```

```python
import functools

import jax
import jax.numpy as jnp
from jax import lax
from jax.experimental import pallas as pl
from jax.experimental.pallas import tpu as pltpu
from jax.sharding import PartitionSpec as P

HD = 128
GROUP = 4
QW = GROUP * HD
NZ = 4
NX = 4
TILE = 128
KTILE = 256
MIB = 1 << 20
MASKED = -3e38
LOWEST = -2e31
SHARE = 1e-4
LOG2E = 1.4426950408889634

Z_BASE = (0, 512, 768, 256)


def z_perm(dz, dc):
    return [
        (z * 2 + c, ((z + dz) % NZ) * 2 + (c + dc) % 2) for z in range(NZ) for c in range(2)
    ]


def x_perm(dx, dy):
    return [
        (x * 2 + y, ((x + dx) % NX) * 2 + (y + dy) % 2) for x in range(NX) for y in range(2)
    ]


def z_send(value, dz):
    return lax.ppermute(value, "tp", z_perm(dz, 0))


def swap(value):
    return lax.ppermute(value, "tp", z_perm(0, 1))


def x_send(value, dx):
    return lax.ppermute(value, "ctx", x_perm(dx, 0))


def y_swap(value):
    return lax.ppermute(value, "ctx", x_perm(0, 1))


def in_hbm(value):
    return pltpu.with_memory_space_constraint(value, pltpu.HBM)


def cost(flops, nbytes, trans=0):
    return pl.CostEstimate(
        flops=int(flops * SHARE), bytes_accessed=int(nbytes * SHARE), transcendentals=int(trans * SHARE)
    )


def norm_body(x_ref, gain_ref, out_ref):
    x = x_ref[...].astype(jnp.float32)
    mean_sq = jnp.mean(x * x, axis=-1, keepdims=True)
    out_ref[...] = (x * lax.rsqrt(mean_sq + 1e-05) * gain_ref[...]).astype(jnp.bfloat16)


def norm(tokens, gain, block=32):
    rows, width = tokens.shape
    return pl.pallas_call(
        norm_body,
        grid=(rows // block,),
        in_specs=[
            pl.BlockSpec((block, width), lambda i: (i, 0)),
            pl.BlockSpec((1, width), lambda i: (0, 0)),
        ],
        out_specs=pl.BlockSpec((block, width), lambda i: (i, 0)),
        out_shape=jax.ShapeDtypeStruct((rows, width), jnp.bfloat16),
        cost_estimate=cost(6 * rows * width, 4 * rows * width),
        compiler_params=pltpu.CompilerParams(vmem_limit_bytes=16 * MIB),
        name="norm",
    )(tokens, gain)


def halves_body(low, high, out_low, out_high):
    half = out_low.shape[0]
    out_low[...] = low[:half]
    out_high[...] = high[half:]


def halves(low, high):
    vmem = pl.BlockSpec(memory_space=pltpu.VMEM)
    shape = jax.ShapeDtypeStruct((low.shape[0] // 2, low.shape[1]), low.dtype)
    return pl.pallas_call(
        halves_body,
        in_specs=[vmem] * 2,
        out_specs=[vmem] * 2,
        out_shape=[shape] * 2,
        cost_estimate=cost(1, 1),
        compiler_params=pltpu.CompilerParams(vmem_limit_bytes=8 * MIB),
        name="halves",
    )(low, high)


def load_body(firsts, *refs):
    n_in = len(firsts)
    sem = refs[-1]
    copies = []
    for i, first in enumerate(firsts):
        src, dst = refs[i], refs[n_in + i]
        copies.append(
            pltpu.make_async_copy(src.at[:, pl.ds(first, dst.shape[1])], dst, sem.at[i])
        )
    for one in copies:
        one.start()
    for one in copies:
        one.wait()


def load(values, windows):
    n_in = len(values)
    return pl.pallas_call(
        functools.partial(load_body, tuple(first for first, _ in windows)),
        in_specs=[pl.BlockSpec(memory_space=pl.ANY)] * n_in,
        out_specs=[pl.BlockSpec(memory_space=pltpu.VMEM)] * n_in,
        out_shape=[
            jax.ShapeDtypeStruct((one.shape[0], width), one.dtype)
            for one, (_, width) in zip(values, windows)
        ],
        scratch_shapes=[pltpu.SemaphoreType.DMA((n_in,))],
        cost_estimate=cost(1, 1),
        compiler_params=pltpu.CompilerParams(vmem_limit_bytes=2 * MIB),
        name="load",
    )(*[in_hbm(one) for one in values])


def project_body(n_in, first, widths, depth, *refs):
    xs, w_ref = refs[:n_in], refs[n_in]
    outs = refs[n_in + 1 :]
    total = sum(widths)
    halves = [xs[: n_in // 2], xs[n_in // 2 :]] if total <= 2 * HD else [xs]
    sums = [None] * len(halves)
    for k in range(w_ref.shape[0] // depth):
        span = slice(k * depth, (k + 1) * depth)
        for i, half in enumerate(halves):
            part = jnp.dot(
                jnp.concatenate([x[:, span] for x in half], axis=0),
                w_ref[span, first : first + total],
                preferred_element_type=jnp.float32,
            )
            sums[i] = part if sums[i] is None else sums[i] + part
    at = 0
    for out, width in zip(outs, widths):
        row = 0
        for one in sums:
            out[row : row + one.shape[0]] = one[:, at : at + width].astype(jnp.bfloat16)
            row += one.shape[0]
        at += width


def project(xs, w, first, widths, depth=2048):
    total = sum(widths)
    rows = sum(x.shape[0] for x in xs)
    width = w.shape[0]
    vmem = pl.BlockSpec(memory_space=pltpu.VMEM)
    return pl.pallas_call(
        functools.partial(project_body, len(xs), first, widths, depth),
        in_specs=[vmem] * (len(xs) + 1),
        out_specs=[vmem] * len(widths),
        out_shape=[jax.ShapeDtypeStruct((rows, one), jnp.bfloat16) for one in widths],
        cost_estimate=cost(2 * rows * width * total, 2 * width * (rows + total)),
        compiler_params=pltpu.CompilerParams(vmem_limit_bytes=6 * MIB + 4 * rows * total),
        name="project",
    )(*xs, w)


def y_pair(kv):
    return jnp.concatenate([kv, y_swap(kv)], axis=0)


def x_all(pair):
    return [pair, x_send(pair, -1), x_send(pair, 2), x_send(pair, 1)]


def attend_body(n_doc, n_kv, places, pack, table_ref, ends_ref, starts_ref, q_ref, *refs):
    pieces = refs[:n_kv]
    keep_ref, send_ref = refs[n_kv : n_kv + 2]
    kv = refs[n_kv + 2] if pack else pieces[0]
    pair = pl.program_id(0)

    if pack:

        @pl.when(pair == 0)
        def _():
            for which, src, dst, count in places:
                kv[dst : dst + count] = pieces[which][src : src + count]

    rows = GROUP * TILE
    starts = [starts_ref[2 * pair + j] for j in range(2)]
    low = jnp.minimum(starts[0], starts[1])
    high = jnp.maximum(starts[0], starts[1]) + TILE - 1
    offset = lax.rem(lax.broadcasted_iota(jnp.int32, (1, rows), 1), TILE)
    q_pos = [start + offset for start in starts]
    doc_start = [jnp.zeros((1, rows), jnp.int32) for _ in range(2)]
    first, last = jnp.int32(0), jnp.int32(0)
    for i in range(n_doc):
        end = ends_ref[i]
        doc_start = [jnp.where(q_pos[j] >= end, end, doc_start[j]) for j in range(2)]
        first = jnp.where(low >= end, end, first)
        last = jnp.where(high >= end, end, last)
    q_t = []
    for j in range(2):
        block = q_ref[j * TILE : (j + 1) * TILE].astype(jnp.float32)
        q_t.append(
            jnp.concatenate(
                [block[:, h * HD : (h + 1) * HD].T for h in range(GROUP)], axis=1
            ).astype(jnp.bfloat16)
        )
    scale = LOG2E / HD**0.5
    ratio = KTILE // TILE
    k_iota = lax.broadcasted_iota(jnp.int32, (KTILE, rows), 0)

    def step(at, state, masked):
        spots = [pl.multiple_of(table_ref[at * ratio + i], TILE) for i in range(ratio)]
        keys = jnp.concatenate([kv[pl.ds(spot, TILE), :HD] for spot in spots], axis=0)
        vals = jnp.concatenate([kv[pl.ds(spot, TILE), HD:] for spot in spots], axis=0)
        scores = [jnp.dot(keys, q_t[j], preferred_element_type=jnp.float32) for j in range(2)]
        out = []
        for j in range(2):
            top, total, acc = state[j]
            s = scores[j]
            if masked:
                base = at * KTILE
                allowed = (k_iota <= q_pos[j] - base) & (k_iota >= doc_start[j] - base)
                s = jnp.where(allowed, s, MASKED)
            new_top = jnp.maximum(top, jnp.max(s, axis=0, keepdims=True))
            e = jnp.exp2((s - new_top) * scale)
            factor = jnp.exp2((top - new_top) * scale)
            total = total * factor + jnp.sum(e, axis=0, keepdims=True)
            acc = acc * factor + lax.dot_general(
                vals,
                e.astype(jnp.bfloat16),
                (((0,), (0,)), ((), ())),
                preferred_element_type=jnp.float32,
            )
            out.append((new_top, total, acc))
        return tuple(out)

    state = tuple(
        (
            jnp.full((1, rows), LOWEST, jnp.float32),
            jnp.zeros((1, rows), jnp.float32),
            jnp.zeros((HD, rows), jnp.float32),
        )
        for _ in range(2)
    )
    begin, stop = first // KTILE, high // KTILE + 1
    inner = (last + KTILE - 1) // KTILE
    outer = jnp.maximum(inner, low // KTILE)
    masked_step = functools.partial(step, masked=True)
    state = lax.fori_loop(begin, jnp.minimum(inner, stop), masked_step, state)
    state = lax.fori_loop(inner, outer, functools.partial(step, masked=False), state)
    state = lax.fori_loop(outer, stop, masked_step, state)
    for (top, total, acc), out_ref in zip(state, (keep_ref, send_ref)):
        out_t = acc / total
        out_ref[...] = jnp.concatenate(
            [out_t[:, h * TILE : (h + 1) * TILE].T for h in range(GROUP)], axis=1
        ).astype(jnp.bfloat16)


def attend(q, first, pairs, kvs, places, pack, table, ends, starts, span):
    half = pairs * TILE
    count = sum(place[3] for place in places)
    vmem = pl.BlockSpec(memory_space=pltpu.VMEM)
    spec = pltpu.PrefetchScalarGridSpec(
        num_scalar_prefetch=3,
        grid=(pairs,),
        in_specs=[pl.BlockSpec((2 * TILE, QW), lambda i, *_: (first + i, 0))]
        + [vmem] * len(kvs),
        out_specs=[pl.BlockSpec((TILE, QW), lambda i, *_: (i, 0))] * 2 + [vmem] * pack,
    )
    return pl.pallas_call(
        functools.partial(attend_body, ends.shape[0], len(kvs), places, pack),
        grid_spec=spec,
        out_shape=[jax.ShapeDtypeStruct((half, QW), jnp.bfloat16)] * 2
        + [jax.ShapeDtypeStruct((count, 2 * HD), jnp.bfloat16)] * pack,
        cost_estimate=cost(
            2 * pairs * 4 * GROUP * TILE * span * HD * 2,
            count * 4 * HD + half * QW * 8,
            2 * pairs * GROUP * TILE * span,
        ),
        compiler_params=pltpu.CompilerParams(vmem_limit_bytes=6 * MIB),
        name="attend",
    )(table, ends, starts, q, *kvs)


def out_body(first, step, own_ref, sib_ref, w_own, w_sib, *outs):
    own, sib = own_ref[...], sib_ref[...]
    for n in range(outs[0].shape[1] // step):
        columns = slice(first + n * step, first + (n + 1) * step)
        sums = jnp.dot(own, w_own[:, columns], preferred_element_type=jnp.float32)
        sums += jnp.dot(sib, w_sib[:, columns], preferred_element_type=jnp.float32)
        for i, out in enumerate(outs):
            out[:, n * step : (n + 1) * step] = sums[i * TILE : (i + 1) * TILE].astype(jnp.bfloat16)


def out_project(own, sib, w_own, w_sib, half, step=512):
    depth, width = w_own.shape
    part = width // 2
    rows = own.shape[0]
    n_out = rows // TILE
    vmem = pl.BlockSpec(memory_space=pltpu.VMEM)
    return pl.pallas_call(
        functools.partial(out_body, half * part, step),
        in_specs=[vmem] * 4,
        out_specs=[vmem] * n_out,
        out_shape=[jax.ShapeDtypeStruct((TILE, part), jnp.bfloat16)] * n_out,
        cost_estimate=cost(
            4 * rows * depth * part, 4 * depth * part + 4 * rows * depth + 2 * rows * part
        ),
        compiler_params=pltpu.CompilerParams(vmem_limit_bytes=4 * MIB),
        name="out_project",
    )(own, sib, w_own, w_sib)


def final_body(p_lo, p_hi, a_lo, a_hi, b_lo, b_hi, out_ref):
    f32 = jnp.float32
    half = p_lo.shape[1]
    lo = p_lo[...].astype(f32) + a_lo[...].astype(f32) + b_lo[...].astype(f32)
    hi = p_hi[...].astype(f32) + a_hi[...].astype(f32) + b_hi[...].astype(f32)
    out_ref[:, :half] = lo.astype(jnp.bfloat16)
    out_ref[:, half:] = hi.astype(jnp.bfloat16)


def final_sum(*parts):
    rows, half = parts[0].shape
    block = 32
    return pl.pallas_call(
        final_body,
        grid=(rows // block,),
        in_specs=[pl.BlockSpec((block, half), lambda i: (i, 0))] * 6,
        out_specs=pl.BlockSpec((block, 2 * half), lambda i: (i, 0)),
        out_shape=jax.ShapeDtypeStruct((rows, 2 * half), jnp.bfloat16),
        cost_estimate=cost(6 * rows * half, 16 * rows * half),
        compiler_params=pltpu.CompilerParams(vmem_limit_bytes=24 * MIB),
        name="final_sum",
    )(*parts)


def add_body(a0, b0, a1, b1, out0, out1):
    f32 = jnp.float32
    out0[...] = (a0[...].astype(f32) + b0[...].astype(f32)).astype(jnp.bfloat16)
    out1[...] = (a1[...].astype(f32) + b1[...].astype(f32)).astype(jnp.bfloat16)


def add_two(a0, b0, a1, b1, block=32):
    rows, width = a0.shape
    one = pl.BlockSpec((block, width), lambda i: (i, 0))
    return pl.pallas_call(
        add_body,
        grid=(rows // block,),
        in_specs=[one] * 4,
        out_specs=[one] * 2,
        out_shape=[jax.ShapeDtypeStruct((rows, width), jnp.bfloat16)] * 2,
        cost_estimate=cost(2 * rows * width, 12 * rows * width),
        compiler_params=pltpu.CompilerParams(vmem_limit_bytes=16 * MIB),
        name="add_two",
    )(a0, b0, a1, b1)


def shards(tokens, norm_gain, w_qkv, w_out, doc_lengths, span_slots):
    ctx = lax.axis_index("ctx")
    tp = lax.axis_index("tp")
    x, y, z, core = ctx // 2, ctx % 2, tp // 2, tp % 2
    gain = norm_gain.reshape(1, -1)
    rows = norm(in_hbm(tokens), in_hbm(gain))
    low, high = z_send(rows, 1), z_send(rows, -1)
    sib_rows = swap(rows)
    w_sib = swap(w_out)
    w_qkv, rows = lax.optimization_barrier((w_qkv, rows))
    (w_kv,) = load([w_qkv], [(QW, 2 * HD)])
    sib_rows, w_kv = lax.optimization_barrier((sib_rows, w_kv))
    sib_rows, doc_lengths, span_slots = lax.optimization_barrier((sib_rows, doc_lengths, span_slots))

    n_spans = span_slots.shape[0]
    per_span = 4
    span = per_span * TILE
    ends = jnp.cumsum(doc_lengths).astype(jnp.int32)
    numbers = jnp.arange(n_spans, dtype=jnp.int32)
    slot_of = jnp.sum(
        jnp.where(span_slots[None, :] == numbers[:, None], numbers[None, :], 0), axis=1
    )
    tile_no = jnp.arange(per_span, dtype=jnp.int32)[None, :]
    slot = slot_of[:, None]
    tile_tp = (slot % 2) * per_span + tile_no
    rank = slot // 2
    rel_z = (tile_tp // 2 - z) % NZ
    z_base = jnp.where(rel_z == 0, Z_BASE[0], 0)
    for i in range(1, NZ):
        z_base = jnp.where(rel_z == i, Z_BASE[i], z_base)
    rel_src = ((rank // 2 - x) % NX) * 2 + (rank % 2 != y).astype(jnp.int32)
    table = rel_src * 1024 + z_base + (tile_tp % 2 != core).astype(jnp.int32) * TILE
    table = table.reshape(-1).astype(jnp.int32)
    own_spans = lax.dynamic_slice_in_dim(span_slots, 2 * ctx, 2, 0)

    def starts_of(*dzs):
        tps = jnp.stack([((z + dz) % NZ) * 2 + c for dz in dzs for c in (core, 1 - core)])
        blocks = jnp.where(tps // per_span == 0, own_spans[0], own_spans[1])
        return (blocks * span + (tps % per_span) * TILE).astype(jnp.int32)

    starts_d, starts_b, starts_a = starts_of(2), starts_of(-1, 1), starts_of(0)
    (kv_a,) = project([rows, sib_rows], w_kv, 0, (2 * HD,))
    pair_a = y_pair(kv_a)
    pair_a, w_sib, table, ends, starts_d, starts_b, starts_a = lax.optimization_barrier(
        (pair_a, w_sib, table, ends, starts_d, starts_b, starts_a)
    )
    all_a = x_all(pair_a)
    far0, far1 = halves(low, high)
    low, high, far0, far1, *all_a = lax.optimization_barrier((low, high, far0, far1, *all_a))
    far0, far1 = z_send(far0, 1), z_send(far1, -1)
    group_b = [low, swap(low), high, swap(high)]
    (kv_b,) = project(group_b, w_kv, 0, (2 * HD,))
    other_b = y_swap(kv_b)
    left0, right0 = x_send(kv_b, 1), x_send(kv_b, -1)
    left0, right0, other_b, w_out, w_sib = lax.optimization_barrier(
        (left0, right0, other_b, w_out, w_sib)
    )
    left1, right1 = x_send(other_b, 1), x_send(other_b, -1)
    all_b = [
        (kv_b, other_b),
        (right0, right1),
        (x_send(left0, 1), x_send(right1, -1)),
        (left0, left1),
    ]
    w_out, w_sib = load([w_out, w_sib], [(0, w_out.shape[1])] * 2)
    far0, far1, w_out, w_sib = lax.optimization_barrier((far0, far1, w_out, w_sib))
    group_d = [far0, far1, swap(far0), swap(far1)]
    (kv_d,) = project(group_d, w_kv, 0, (2 * HD,))
    pair_d = y_pair(kv_d)
    every = [rows, sib_rows, *group_b, *group_d]
    *every, pair_d = lax.optimization_barrier((*every, pair_d))
    (q_all,) = project(every, w_qkv, 0, (QW,))
    kvs, places = [], []
    for group, base in ((all_a, 0), (all_b, 256), (x_all(pair_d), 768)):
        for i, one in enumerate(group):
            parts = one if isinstance(one, tuple) else (one,)
            count = sum(part.shape[0] for part in parts) // 2
            for j in range(2):
                which, src = (len(kvs) + j, 0) if len(parts) == 2 else (len(kvs), j * count)
                places.append((which, src, (2 * i + j) * 1024 + base, count))
            kvs.extend(parts)

    d_own, d_send, packed = attend(q_all, 3, 1, kvs, tuple(places), True, table, ends, starts_d, 1024)
    d_sib = swap(d_send)
    (d_lo,) = out_project(d_own, d_sib, w_out, w_sib, 0)
    (d_hi,) = out_project(d_own, d_sib, w_out, w_sib, 1)
    from_low, from_high = z_send(d_lo, 1), z_send(d_hi, -1)
    whole = ((0, 0, 0, packed.shape[0]),)
    packed, d_lo, d_hi = lax.optimization_barrier((packed, d_lo, d_hi))
    b_own, b_send = attend(q_all, 1, 2, [packed], whole, False, table, ends, starts_b, 1024)
    b_sib = swap(b_send)
    prev_lo, next_lo = out_project(b_own, b_sib, w_out, w_sib, 0)
    prev_hi, next_hi = out_project(b_own, b_sib, w_out, w_sib, 1)
    early_hi, early_lo = z_send(next_hi, 1), z_send(prev_lo, -1)
    packed, next_hi, prev_hi, next_lo, prev_lo = lax.optimization_barrier(
        (packed, next_hi, prev_hi, next_lo, prev_lo)
    )
    sum_lo, sum_hi = add_two(next_lo, from_low, prev_hi, from_high)
    late_lo, late_hi = z_send(sum_lo, 1), z_send(sum_hi, -1)
    a_own, a_send = attend(q_all, 0, 1, [packed], whole, False, table, ends, starts_a, 1024)
    a_sib = swap(a_send)
    (a_lo,) = out_project(a_own, a_sib, w_out, w_sib, 0)
    (a_hi,) = out_project(a_own, a_sib, w_out, w_sib, 1)
    return final_sum(a_lo, a_hi, early_lo, early_hi, late_lo, late_hi)


def solution(mesh):
    placed = (P(("dp", "ctx", "tp"), None), P(), P(None, "tp"), P("tp", None), P("dp"), P("dp"))
    return jax.shard_map(
        shards, mesh=mesh, in_specs=placed, out_specs=P(("dp", "ctx", "tp"), None), check_vma=False
    )
```

```python
import functools

import jax
import jax.numpy as jnp
from jax import lax
from jax.experimental import pallas as pl
from jax.experimental.pallas import tpu as pltpu
from jax.sharding import PartitionSpec as P

HD = 128
GROUP = 4
QW = GROUP * HD
NZ = 4
NX = 4
TILE = 128
KTILE = 256
MIB = 1 << 20
MASKED = -3e38
LOWEST = -2e31
SHARE = 1e-4
LOG2E = 1.4426950408889634

Z_BASE = (0, 512, 768, 256)


def z_perm(dz, dc):
    return [
        (z * 2 + c, ((z + dz) % NZ) * 2 + (c + dc) % 2) for z in range(NZ) for c in range(2)
    ]


def x_perm(dx, dy):
    return [
        (x * 2 + y, ((x + dx) % NX) * 2 + (y + dy) % 2) for x in range(NX) for y in range(2)
    ]


def z_send(value, dz):
    return lax.ppermute(value, "tp", z_perm(dz, 0))


def swap(value):
    return lax.ppermute(value, "tp", z_perm(0, 1))


def x_send(value, dx):
    return lax.ppermute(value, "ctx", x_perm(dx, 0))


def y_swap(value):
    return lax.ppermute(value, "ctx", x_perm(0, 1))


def in_hbm(value):
    return pltpu.with_memory_space_constraint(value, pltpu.HBM)


def cost(flops, nbytes, trans=0):
    return pl.CostEstimate(
        flops=int(flops * SHARE), bytes_accessed=int(nbytes * SHARE), transcendentals=int(trans * SHARE)
    )


def norm_body(x_ref, gain_ref, out_ref):
    block = x_ref.shape[0]
    x = x_ref[...].astype(jnp.float32)
    mean_sq = jnp.mean(x * x, axis=-1, keepdims=True)
    at = pl.multiple_of(pl.program_id(0) * block, block)
    out_ref[pl.ds(at, block)] = (x * lax.rsqrt(mean_sq + 1e-05) * gain_ref[...]).astype(jnp.bfloat16)


def norm(tokens, gain, block=16):
    rows, width = tokens.shape
    return pl.pallas_call(
        norm_body,
        grid=(rows // block,),
        in_specs=[
            pl.BlockSpec((block, width), lambda i: (i, 0)),
            pl.BlockSpec((1, width), lambda i: (0, 0)),
        ],
        out_specs=pl.BlockSpec(memory_space=pltpu.VMEM),
        out_shape=jax.ShapeDtypeStruct((rows, width), jnp.bfloat16),
        cost_estimate=cost(6 * rows * width, 4 * rows * width),
        compiler_params=pltpu.CompilerParams(vmem_limit_bytes=8 * MIB),
        name="norm",
    )(tokens, gain)


def halves_body(low, high, out_low, out_high):
    half = out_low.shape[0]
    out_low[...] = low[:half]
    out_high[...] = high[half:]


def halves(low, high):
    vmem = pl.BlockSpec(memory_space=pltpu.VMEM)
    shape = jax.ShapeDtypeStruct((low.shape[0] // 2, low.shape[1]), low.dtype)
    return pl.pallas_call(
        halves_body,
        in_specs=[vmem] * 2,
        out_specs=[vmem] * 2,
        out_shape=[shape] * 2,
        cost_estimate=cost(1, 1),
        compiler_params=pltpu.CompilerParams(vmem_limit_bytes=8 * MIB),
        name="halves",
    )(low, high)


def load_body(firsts, *refs):
    n_in = len(firsts)
    sem = refs[-1]
    copies = []
    for i, first in enumerate(firsts):
        src, dst = refs[i], refs[n_in + i]
        copies.append(
            pltpu.make_async_copy(src.at[:, pl.ds(first, dst.shape[1])], dst, sem.at[i])
        )
    for one in copies:
        one.start()
    for one in copies:
        one.wait()


def load(values, windows):
    n_in = len(values)
    return pl.pallas_call(
        functools.partial(load_body, tuple(first for first, _ in windows)),
        in_specs=[pl.BlockSpec(memory_space=pl.ANY)] * n_in,
        out_specs=[pl.BlockSpec(memory_space=pltpu.VMEM)] * n_in,
        out_shape=[
            jax.ShapeDtypeStruct((one.shape[0], width), one.dtype)
            for one, (_, width) in zip(values, windows)
        ],
        scratch_shapes=[pltpu.SemaphoreType.DMA((n_in,))],
        cost_estimate=cost(1, 1),
        compiler_params=pltpu.CompilerParams(vmem_limit_bytes=2 * MIB),
        name="load",
    )(*[in_hbm(one) for one in values])


def project_body(n_in, first, widths, depth, *refs):
    xs, w_ref = refs[:n_in], refs[n_in]
    outs = refs[n_in + 1 :]
    total = sum(widths)
    halves = [xs[: n_in // 2], xs[n_in // 2 :]] if total <= 2 * HD else [xs]
    sums = [None] * len(halves)
    for k in range(w_ref.shape[0] // depth):
        span = slice(k * depth, (k + 1) * depth)
        for i, half in enumerate(halves):
            part = jnp.dot(
                jnp.concatenate([x[:, span] for x in half], axis=0),
                w_ref[span, first : first + total],
                preferred_element_type=jnp.float32,
            )
            sums[i] = part if sums[i] is None else sums[i] + part
    at = 0
    for out, width in zip(outs, widths):
        row = 0
        for one in sums:
            out[row : row + one.shape[0]] = one[:, at : at + width].astype(jnp.bfloat16)
            row += one.shape[0]
        at += width


def project(xs, w, first, widths, depth=2048):
    total = sum(widths)
    rows = sum(x.shape[0] for x in xs)
    width = w.shape[0]
    vmem = pl.BlockSpec(memory_space=pltpu.VMEM)
    return pl.pallas_call(
        functools.partial(project_body, len(xs), first, widths, depth),
        in_specs=[vmem] * (len(xs) + 1),
        out_specs=[vmem] * len(widths),
        out_shape=[jax.ShapeDtypeStruct((rows, one), jnp.bfloat16) for one in widths],
        cost_estimate=cost(2 * rows * width * total, 2 * width * (rows + total)),
        compiler_params=pltpu.CompilerParams(vmem_limit_bytes=6 * MIB + 4 * rows * total),
        name="project",
    )(*xs, w)


def y_pair(kv):
    return jnp.concatenate([kv, y_swap(kv)], axis=0)


def x_all(pair):
    return [pair, x_send(pair, -1), x_send(pair, 2), x_send(pair, 1)]


def attend_body(n_doc, n_kv, places, pack, table_ref, ends_ref, starts_ref, q_ref, *refs):
    pieces = refs[:n_kv]
    keep_ref, send_ref = refs[n_kv : n_kv + 2]
    kv = refs[n_kv + 2] if pack else pieces[0]
    pair = pl.program_id(0)

    if pack:

        @pl.when(pair == 0)
        def _():
            for which, src, dst, count in places:
                kv[dst : dst + count] = pieces[which][src : src + count]

    rows = GROUP * TILE
    starts = [starts_ref[2 * pair + j] for j in range(2)]
    low = jnp.minimum(starts[0], starts[1])
    high = jnp.maximum(starts[0], starts[1]) + TILE - 1
    offset = lax.rem(lax.broadcasted_iota(jnp.int32, (1, rows), 1), TILE)
    q_pos = [start + offset for start in starts]
    doc_start = [jnp.zeros((1, rows), jnp.int32) for _ in range(2)]
    first, last = jnp.int32(0), jnp.int32(0)
    for i in range(n_doc):
        end = ends_ref[i]
        doc_start = [jnp.where(q_pos[j] >= end, end, doc_start[j]) for j in range(2)]
        first = jnp.where(low >= end, end, first)
        last = jnp.where(high >= end, end, last)
    q_t = []
    for j in range(2):
        block = q_ref[j * TILE : (j + 1) * TILE].astype(jnp.float32)
        q_t.append(
            jnp.concatenate(
                [block[:, h * HD : (h + 1) * HD].T for h in range(GROUP)], axis=1
            ).astype(jnp.bfloat16)
        )
    scale = LOG2E / HD**0.5
    ratio = KTILE // TILE
    k_iota = lax.broadcasted_iota(jnp.int32, (KTILE, rows), 0)

    def step(at, state, masked):
        spots = [pl.multiple_of(table_ref[at * ratio + i], TILE) for i in range(ratio)]
        keys = jnp.concatenate([kv[pl.ds(spot, TILE), :HD] for spot in spots], axis=0)
        vals = jnp.concatenate([kv[pl.ds(spot, TILE), HD:] for spot in spots], axis=0)
        scores = [jnp.dot(keys, q_t[j], preferred_element_type=jnp.float32) for j in range(2)]
        out = []
        for j in range(2):
            top, total, acc = state[j]
            s = scores[j]
            if masked:
                base = at * KTILE
                allowed = (k_iota <= q_pos[j] - base) & (k_iota >= doc_start[j] - base)
                s = jnp.where(allowed, s, MASKED)
            new_top = jnp.maximum(top, jnp.max(s, axis=0, keepdims=True))
            e = jnp.exp2((s - new_top) * scale)
            factor = jnp.exp2((top - new_top) * scale)
            total = total * factor + jnp.sum(e, axis=0, keepdims=True)
            acc = acc * factor + lax.dot_general(
                vals,
                e.astype(jnp.bfloat16),
                (((0,), (0,)), ((), ())),
                preferred_element_type=jnp.float32,
            )
            out.append((new_top, total, acc))
        return tuple(out)

    state = tuple(
        (
            jnp.full((1, rows), LOWEST, jnp.float32),
            jnp.zeros((1, rows), jnp.float32),
            jnp.zeros((HD, rows), jnp.float32),
        )
        for _ in range(2)
    )
    begin, stop = first // KTILE, high // KTILE + 1
    inner = (last + KTILE - 1) // KTILE
    outer = jnp.maximum(inner, low // KTILE)
    masked_step = functools.partial(step, masked=True)
    state = lax.fori_loop(begin, jnp.minimum(inner, stop), masked_step, state)
    state = lax.fori_loop(inner, outer, functools.partial(step, masked=False), state)
    state = lax.fori_loop(outer, stop, masked_step, state)
    for (top, total, acc), out_ref in zip(state, (keep_ref, send_ref)):
        out_t = acc / total
        out_ref[...] = jnp.concatenate(
            [out_t[:, h * TILE : (h + 1) * TILE].T for h in range(GROUP)], axis=1
        ).astype(jnp.bfloat16)


def attend(q, first, pairs, kvs, places, pack, table, ends, starts, span):
    half = pairs * TILE
    count = sum(place[3] for place in places)
    vmem = pl.BlockSpec(memory_space=pltpu.VMEM)
    spec = pltpu.PrefetchScalarGridSpec(
        num_scalar_prefetch=3,
        grid=(pairs,),
        in_specs=[pl.BlockSpec((2 * TILE, QW), lambda i, *_: (first + i, 0))]
        + [vmem] * len(kvs),
        out_specs=[pl.BlockSpec((TILE, QW), lambda i, *_: (i, 0))] * 2 + [vmem] * pack,
    )
    return pl.pallas_call(
        functools.partial(attend_body, ends.shape[0], len(kvs), places, pack),
        grid_spec=spec,
        out_shape=[jax.ShapeDtypeStruct((half, QW), jnp.bfloat16)] * 2
        + [jax.ShapeDtypeStruct((count, 2 * HD), jnp.bfloat16)] * pack,
        cost_estimate=cost(
            2 * pairs * 4 * GROUP * TILE * span * HD * 2,
            count * 4 * HD + half * QW * 8,
            2 * pairs * GROUP * TILE * span,
        ),
        compiler_params=pltpu.CompilerParams(vmem_limit_bytes=6 * MIB),
        name="attend",
    )(table, ends, starts, q, *kvs)


def out_body(first, step, own_ref, sib_ref, w_own, w_sib, *outs):
    own, sib = own_ref[...], sib_ref[...]
    for n in range(outs[0].shape[1] // step):
        columns = slice(first + n * step, first + (n + 1) * step)
        sums = jnp.dot(own, w_own[:, columns], preferred_element_type=jnp.float32)
        sums += jnp.dot(sib, w_sib[:, columns], preferred_element_type=jnp.float32)
        for i, out in enumerate(outs):
            out[:, n * step : (n + 1) * step] = sums[i * TILE : (i + 1) * TILE].astype(jnp.bfloat16)


def out_project(own, sib, w_own, w_sib, half, step=512):
    depth, width = w_own.shape
    part = width // 2
    rows = own.shape[0]
    n_out = rows // TILE
    vmem = pl.BlockSpec(memory_space=pltpu.VMEM)
    return pl.pallas_call(
        functools.partial(out_body, half * part, step),
        in_specs=[vmem] * 4,
        out_specs=[vmem] * n_out,
        out_shape=[jax.ShapeDtypeStruct((TILE, part), jnp.bfloat16)] * n_out,
        cost_estimate=cost(
            4 * rows * depth * part, 4 * depth * part + 4 * rows * depth + 2 * rows * part
        ),
        compiler_params=pltpu.CompilerParams(vmem_limit_bytes=4 * MIB),
        name="out_project",
    )(own, sib, w_own, w_sib)


def final_body(p_lo, p_hi, a_lo, a_hi, b_lo, b_hi, out_ref):
    f32 = jnp.float32
    half = p_lo.shape[1]
    lo = p_lo[...].astype(f32) + a_lo[...].astype(f32) + b_lo[...].astype(f32)
    hi = p_hi[...].astype(f32) + a_hi[...].astype(f32) + b_hi[...].astype(f32)
    out_ref[:, :half] = lo.astype(jnp.bfloat16)
    out_ref[:, half:] = hi.astype(jnp.bfloat16)


def final_sum(*parts):
    rows, half = parts[0].shape
    block = 32
    return pl.pallas_call(
        final_body,
        grid=(rows // block,),
        in_specs=[pl.BlockSpec((block, half), lambda i: (i, 0))] * 6,
        out_specs=pl.BlockSpec((block, 2 * half), lambda i: (i, 0)),
        out_shape=jax.ShapeDtypeStruct((rows, 2 * half), jnp.bfloat16),
        cost_estimate=cost(6 * rows * half, 16 * rows * half),
        compiler_params=pltpu.CompilerParams(vmem_limit_bytes=24 * MIB),
        name="final_sum",
    )(*parts)


def add_body(a0, b0, a1, b1, out0, out1):
    f32 = jnp.float32
    out0[...] = (a0[...].astype(f32) + b0[...].astype(f32)).astype(jnp.bfloat16)
    out1[...] = (a1[...].astype(f32) + b1[...].astype(f32)).astype(jnp.bfloat16)


def add_two(a0, b0, a1, b1, block=32):
    rows, width = a0.shape
    one = pl.BlockSpec((block, width), lambda i: (i, 0))
    return pl.pallas_call(
        add_body,
        grid=(rows // block,),
        in_specs=[one] * 4,
        out_specs=[one] * 2,
        out_shape=[jax.ShapeDtypeStruct((rows, width), jnp.bfloat16)] * 2,
        cost_estimate=cost(2 * rows * width, 12 * rows * width),
        compiler_params=pltpu.CompilerParams(vmem_limit_bytes=16 * MIB),
        name="add_two",
    )(a0, b0, a1, b1)


def shards(tokens, norm_gain, w_qkv, w_out, doc_lengths, span_slots):
    ctx = lax.axis_index("ctx")
    tp = lax.axis_index("tp")
    x, y, z, core = ctx // 2, ctx % 2, tp // 2, tp % 2
    gain = norm_gain.reshape(1, -1)
    rows = norm(in_hbm(tokens), in_hbm(gain))
    low, high = z_send(rows, 1), z_send(rows, -1)
    sib_rows = swap(rows)
    w_sib = swap(w_out)
    w_qkv, rows = lax.optimization_barrier((w_qkv, rows))
    (w_kv,) = load([w_qkv], [(QW, 2 * HD)])
    sib_rows, w_kv = lax.optimization_barrier((sib_rows, w_kv))
    sib_rows, doc_lengths, span_slots = lax.optimization_barrier((sib_rows, doc_lengths, span_slots))

    n_spans = span_slots.shape[0]
    per_span = 4
    span = per_span * TILE
    ends = jnp.cumsum(doc_lengths).astype(jnp.int32)
    numbers = jnp.arange(n_spans, dtype=jnp.int32)
    slot_of = jnp.sum(
        jnp.where(span_slots[None, :] == numbers[:, None], numbers[None, :], 0), axis=1
    )
    tile_no = jnp.arange(per_span, dtype=jnp.int32)[None, :]
    slot = slot_of[:, None]
    tile_tp = (slot % 2) * per_span + tile_no
    rank = slot // 2
    rel_z = (tile_tp // 2 - z) % NZ
    z_base = jnp.where(rel_z == 0, Z_BASE[0], 0)
    for i in range(1, NZ):
        z_base = jnp.where(rel_z == i, Z_BASE[i], z_base)
    rel_src = ((rank // 2 - x) % NX) * 2 + (rank % 2 != y).astype(jnp.int32)
    table = rel_src * 1024 + z_base + (tile_tp % 2 != core).astype(jnp.int32) * TILE
    table = table.reshape(-1).astype(jnp.int32)
    own_spans = lax.dynamic_slice_in_dim(span_slots, 2 * ctx, 2, 0)

    def starts_of(*dzs):
        tps = jnp.stack([((z + dz) % NZ) * 2 + c for dz in dzs for c in (core, 1 - core)])
        blocks = jnp.where(tps // per_span == 0, own_spans[0], own_spans[1])
        return (blocks * span + (tps % per_span) * TILE).astype(jnp.int32)

    starts_d, starts_b, starts_a = starts_of(2), starts_of(-1, 1), starts_of(0)
    (kv_a,) = project([rows, sib_rows], w_kv, 0, (2 * HD,))
    pair_a = y_pair(kv_a)
    pair_a, w_sib, table, ends, starts_d, starts_b, starts_a = lax.optimization_barrier(
        (pair_a, w_sib, table, ends, starts_d, starts_b, starts_a)
    )
    all_a = x_all(pair_a)
    far0, far1 = halves(low, high)
    low, high, far0, far1, *all_a = lax.optimization_barrier((low, high, far0, far1, *all_a))
    far0, far1 = z_send(far0, 1), z_send(far1, -1)
    group_b = [low, swap(low), high, swap(high)]
    (kv_b,) = project(group_b, w_kv, 0, (2 * HD,))
    other_b = y_swap(kv_b)
    left0, right0 = x_send(kv_b, 1), x_send(kv_b, -1)
    w_out, w_sib, kv_b = lax.optimization_barrier((w_out, w_sib, kv_b))
    w_out, w_sib = load([w_out, w_sib], [(0, w_out.shape[1])] * 2)
    left0, right0, other_b, w_out, w_sib = lax.optimization_barrier(
        (left0, right0, other_b, w_out, w_sib)
    )
    left1, right1 = x_send(other_b, 1), x_send(other_b, -1)
    far0, far1, left1, right1 = lax.optimization_barrier((far0, far1, left1, right1))
    all_b = [
        (kv_b, other_b),
        (right0, right1),
        (x_send(left0, 1), x_send(right1, -1)),
        (left0, left1),
    ]
    group_d = [far0, far1, swap(far0), swap(far1)]
    (kv_d,) = project(group_d, w_kv, 0, (2 * HD,))
    pair_d = y_pair(kv_d)
    every = [rows, sib_rows, *group_b, *group_d]
    *every, pair_d = lax.optimization_barrier((*every, pair_d))
    (q_all,) = project(every, w_qkv, 0, (QW,))
    kvs, places = [], []
    for group, base in ((all_a, 0), (all_b, 256), (x_all(pair_d), 768)):
        for i, one in enumerate(group):
            parts = one if isinstance(one, tuple) else (one,)
            count = sum(part.shape[0] for part in parts) // 2
            for j in range(2):
                which, src = (len(kvs) + j, 0) if len(parts) == 2 else (len(kvs), j * count)
                places.append((which, src, (2 * i + j) * 1024 + base, count))
            kvs.extend(parts)

    d_own, d_send, packed = attend(q_all, 3, 1, kvs, tuple(places), True, table, ends, starts_d, 1024)
    d_sib = swap(d_send)
    (d_lo,) = out_project(d_own, d_sib, w_out, w_sib, 0)
    (d_hi,) = out_project(d_own, d_sib, w_out, w_sib, 1)
    from_low, from_high = z_send(d_lo, 1), z_send(d_hi, -1)
    whole = ((0, 0, 0, packed.shape[0]),)
    packed, d_lo, d_hi = lax.optimization_barrier((packed, d_lo, d_hi))
    b_own, b_send = attend(q_all, 1, 2, [packed], whole, False, table, ends, starts_b, 1024)
    b_sib = swap(b_send)
    prev_lo, next_lo = out_project(b_own, b_sib, w_out, w_sib, 0)
    prev_hi, next_hi = out_project(b_own, b_sib, w_out, w_sib, 1)
    early_hi, early_lo = z_send(next_hi, 1), z_send(prev_lo, -1)
    packed, next_hi, prev_hi, next_lo, prev_lo = lax.optimization_barrier(
        (packed, next_hi, prev_hi, next_lo, prev_lo)
    )
    sum_lo, sum_hi = add_two(next_lo, from_low, prev_hi, from_high)
    late_lo, late_hi = z_send(sum_lo, 1), z_send(sum_hi, -1)
    a_own, a_send = attend(q_all, 0, 1, [packed], whole, False, table, ends, starts_a, 1024)
    a_sib = swap(a_send)
    (a_lo,) = out_project(a_own, a_sib, w_out, w_sib, 0)
    (a_hi,) = out_project(a_own, a_sib, w_out, w_sib, 1)
    return final_sum(a_lo, a_hi, early_lo, early_hi, late_lo, late_hi)


def solution(mesh):
    placed = (P(("dp", "ctx", "tp"), None), P(), P(None, "tp"), P("tp", None), P("dp"), P("dp"))
    return jax.shard_map(
        shards, mesh=mesh, in_specs=placed, out_specs=P(("dp", "ctx", "tp"), None), check_vma=False
    )
```

```python
import functools

import jax
import jax.numpy as jnp
from jax import lax
from jax.experimental import pallas as pl
from jax.experimental.pallas import tpu as pltpu
from jax.sharding import PartitionSpec as P

HD = 128
GROUP = 4
QW = GROUP * HD
NZ = 4
NX = 4
TILE = 128
KTILE = 256
MIB = 1 << 20
MASKED = -3e38
LOWEST = -2e31
SHARE = 1e-4
LOG2E = 1.4426950408889634

Z_BASE = (0, 512, 768, 256)


def z_perm(dz, dc):
    return [
        (z * 2 + c, ((z + dz) % NZ) * 2 + (c + dc) % 2) for z in range(NZ) for c in range(2)
    ]


def x_perm(dx, dy):
    return [
        (x * 2 + y, ((x + dx) % NX) * 2 + (y + dy) % 2) for x in range(NX) for y in range(2)
    ]


def z_send(value, dz):
    return lax.ppermute(value, "tp", z_perm(dz, 0))


def swap(value):
    return lax.ppermute(value, "tp", z_perm(0, 1))


def x_send(value, dx):
    return lax.ppermute(value, "ctx", x_perm(dx, 0))


def y_swap(value):
    return lax.ppermute(value, "ctx", x_perm(0, 1))


def in_hbm(value):
    return pltpu.with_memory_space_constraint(value, pltpu.HBM)


def cost(flops, nbytes, trans=0):
    return pl.CostEstimate(
        flops=int(flops * SHARE), bytes_accessed=int(nbytes * SHARE), transcendentals=int(trans * SHARE)
    )


def norm_body(x_hbm, gain_ref, out_ref, x_v, sem):
    n = sem.shape[0]
    block = x_v.shape[0] // n
    copies = [
        pltpu.make_async_copy(
            x_hbm.at[pl.ds(i * block, block)], x_v.at[pl.ds(i * block, block)], sem.at[i]
        )
        for i in range(n)
    ]
    for one in copies:
        one.start()
    gain = gain_ref[...]
    for i, one in enumerate(copies):
        one.wait()
        x = x_v[i * block : (i + 1) * block].astype(jnp.float32)
        mean_sq = jnp.mean(x * x, axis=-1, keepdims=True)
        normed = x * lax.rsqrt(mean_sq + 1e-05) * gain
        out_ref[i * block : (i + 1) * block] = normed.astype(jnp.bfloat16)


def norm(tokens, gain, parts=8):
    rows, width = tokens.shape
    vmem = pl.BlockSpec(memory_space=pltpu.VMEM)
    return pl.pallas_call(
        norm_body,
        in_specs=[pl.BlockSpec(memory_space=pl.ANY), vmem],
        out_specs=vmem,
        out_shape=jax.ShapeDtypeStruct((rows, width), jnp.bfloat16),
        scratch_shapes=[
            pltpu.VMEM((rows, width), jnp.bfloat16),
            pltpu.SemaphoreType.DMA((parts,)),
        ],
        cost_estimate=cost(6 * rows * width, 4 * rows * width),
        compiler_params=pltpu.CompilerParams(vmem_limit_bytes=10 * MIB),
        name="norm",
    )(tokens, gain)


def halves_body(low, high, out_low, out_high):
    half = out_low.shape[0]
    out_low[...] = low[:half]
    out_high[...] = high[half:]


def halves(low, high):
    vmem = pl.BlockSpec(memory_space=pltpu.VMEM)
    shape = jax.ShapeDtypeStruct((low.shape[0] // 2, low.shape[1]), low.dtype)
    return pl.pallas_call(
        halves_body,
        in_specs=[vmem] * 2,
        out_specs=[vmem] * 2,
        out_shape=[shape] * 2,
        cost_estimate=cost(1, 1),
        compiler_params=pltpu.CompilerParams(vmem_limit_bytes=8 * MIB),
        name="halves",
    )(low, high)


def load_body(firsts, *refs):
    n_in = len(firsts)
    sem = refs[-1]
    copies = []
    for i, first in enumerate(firsts):
        src, dst = refs[i], refs[n_in + i]
        copies.append(
            pltpu.make_async_copy(src.at[:, pl.ds(first, dst.shape[1])], dst, sem.at[i])
        )
    for one in copies:
        one.start()
    for one in copies:
        one.wait()


def load(values, windows):
    n_in = len(values)
    return pl.pallas_call(
        functools.partial(load_body, tuple(first for first, _ in windows)),
        in_specs=[pl.BlockSpec(memory_space=pl.ANY)] * n_in,
        out_specs=[pl.BlockSpec(memory_space=pltpu.VMEM)] * n_in,
        out_shape=[
            jax.ShapeDtypeStruct((one.shape[0], width), one.dtype)
            for one, (_, width) in zip(values, windows)
        ],
        scratch_shapes=[pltpu.SemaphoreType.DMA((n_in,))],
        cost_estimate=cost(1, 1),
        compiler_params=pltpu.CompilerParams(vmem_limit_bytes=2 * MIB),
        name="load",
    )(*[in_hbm(one) for one in values])


def project_body(n_in, first, widths, depth, *refs):
    xs, w_ref = refs[:n_in], refs[n_in]
    outs = refs[n_in + 1 :]
    total = sum(widths)
    halves = [xs[: n_in // 2], xs[n_in // 2 :]] if total <= 2 * HD else [xs]
    sums = [None] * len(halves)
    for k in range(w_ref.shape[0] // depth):
        span = slice(k * depth, (k + 1) * depth)
        for i, half in enumerate(halves):
            part = jnp.dot(
                jnp.concatenate([x[:, span] for x in half], axis=0),
                w_ref[span, first : first + total],
                preferred_element_type=jnp.float32,
            )
            sums[i] = part if sums[i] is None else sums[i] + part
    at = 0
    for out, width in zip(outs, widths):
        row = 0
        for one in sums:
            out[row : row + one.shape[0]] = one[:, at : at + width].astype(jnp.bfloat16)
            row += one.shape[0]
        at += width


def project(xs, w, first, widths, depth=2048):
    total = sum(widths)
    rows = sum(x.shape[0] for x in xs)
    width = w.shape[0]
    vmem = pl.BlockSpec(memory_space=pltpu.VMEM)
    return pl.pallas_call(
        functools.partial(project_body, len(xs), first, widths, depth),
        in_specs=[vmem] * (len(xs) + 1),
        out_specs=[vmem] * len(widths),
        out_shape=[jax.ShapeDtypeStruct((rows, one), jnp.bfloat16) for one in widths],
        cost_estimate=cost(2 * rows * width * total, 2 * width * (rows + total)),
        compiler_params=pltpu.CompilerParams(vmem_limit_bytes=6 * MIB + 4 * rows * total),
        name="project",
    )(*xs, w)


def y_pair(kv):
    return jnp.concatenate([kv, y_swap(kv)], axis=0)


def x_all(pair):
    return [pair, x_send(pair, -1), x_send(pair, 2), x_send(pair, 1)]


def attend_body(n_doc, n_kv, places, pack, table_ref, ends_ref, starts_ref, q_ref, *refs):
    pieces = refs[:n_kv]
    keep_ref, send_ref = refs[n_kv : n_kv + 2]
    kv = refs[n_kv + 2] if pack else pieces[0]
    pair = pl.program_id(0)

    if pack:

        @pl.when(pair == 0)
        def _():
            for which, src, dst, count in places:
                kv[dst : dst + count] = pieces[which][src : src + count]

    rows = GROUP * TILE
    starts = [starts_ref[2 * pair + j] for j in range(2)]
    low = jnp.minimum(starts[0], starts[1])
    high = jnp.maximum(starts[0], starts[1]) + TILE - 1
    offset = lax.rem(lax.broadcasted_iota(jnp.int32, (1, rows), 1), TILE)
    q_pos = [start + offset for start in starts]
    doc_start = [jnp.zeros((1, rows), jnp.int32) for _ in range(2)]
    first, last = jnp.int32(0), jnp.int32(0)
    for i in range(n_doc):
        end = ends_ref[i]
        doc_start = [jnp.where(q_pos[j] >= end, end, doc_start[j]) for j in range(2)]
        first = jnp.where(low >= end, end, first)
        last = jnp.where(high >= end, end, last)
    q_t = []
    for j in range(2):
        block = q_ref[j * TILE : (j + 1) * TILE].astype(jnp.float32)
        q_t.append(
            jnp.concatenate(
                [block[:, h * HD : (h + 1) * HD].T for h in range(GROUP)], axis=1
            ).astype(jnp.bfloat16)
        )
    scale = LOG2E / HD**0.5
    ratio = KTILE // TILE
    k_iota = lax.broadcasted_iota(jnp.int32, (KTILE, rows), 0)

    def step(at, state, masked):
        spots = [pl.multiple_of(table_ref[at * ratio + i], TILE) for i in range(ratio)]
        keys = jnp.concatenate([kv[pl.ds(spot, TILE), :HD] for spot in spots], axis=0)
        vals = jnp.concatenate([kv[pl.ds(spot, TILE), HD:] for spot in spots], axis=0)
        scores = [jnp.dot(keys, q_t[j], preferred_element_type=jnp.float32) for j in range(2)]
        out = []
        for j in range(2):
            top, total, acc = state[j]
            s = scores[j]
            if masked:
                base = at * KTILE
                allowed = (k_iota <= q_pos[j] - base) & (k_iota >= doc_start[j] - base)
                s = jnp.where(allowed, s, MASKED)
            new_top = jnp.maximum(top, jnp.max(s, axis=0, keepdims=True))
            e = jnp.exp2((s - new_top) * scale)
            factor = jnp.exp2((top - new_top) * scale)
            total = total * factor + jnp.sum(e, axis=0, keepdims=True)
            acc = acc * factor + lax.dot_general(
                vals,
                e.astype(jnp.bfloat16),
                (((0,), (0,)), ((), ())),
                preferred_element_type=jnp.float32,
            )
            out.append((new_top, total, acc))
        return tuple(out)

    state = tuple(
        (
            jnp.full((1, rows), LOWEST, jnp.float32),
            jnp.zeros((1, rows), jnp.float32),
            jnp.zeros((HD, rows), jnp.float32),
        )
        for _ in range(2)
    )
    begin, stop = first // KTILE, high // KTILE + 1
    inner = (last + KTILE - 1) // KTILE
    outer = jnp.maximum(inner, low // KTILE)
    masked_step = functools.partial(step, masked=True)
    state = lax.fori_loop(begin, jnp.minimum(inner, stop), masked_step, state)
    state = lax.fori_loop(inner, outer, functools.partial(step, masked=False), state)
    state = lax.fori_loop(outer, stop, masked_step, state)
    for (top, total, acc), out_ref in zip(state, (keep_ref, send_ref)):
        out_t = acc / total
        out_ref[...] = jnp.concatenate(
            [out_t[:, h * TILE : (h + 1) * TILE].T for h in range(GROUP)], axis=1
        ).astype(jnp.bfloat16)


def attend(q, first, pairs, kvs, places, pack, table, ends, starts, span):
    half = pairs * TILE
    count = sum(place[3] for place in places)
    vmem = pl.BlockSpec(memory_space=pltpu.VMEM)
    spec = pltpu.PrefetchScalarGridSpec(
        num_scalar_prefetch=3,
        grid=(pairs,),
        in_specs=[pl.BlockSpec((2 * TILE, QW), lambda i, *_: (first + i, 0))]
        + [vmem] * len(kvs),
        out_specs=[pl.BlockSpec((TILE, QW), lambda i, *_: (i, 0))] * 2 + [vmem] * pack,
    )
    return pl.pallas_call(
        functools.partial(attend_body, ends.shape[0], len(kvs), places, pack),
        grid_spec=spec,
        out_shape=[jax.ShapeDtypeStruct((half, QW), jnp.bfloat16)] * 2
        + [jax.ShapeDtypeStruct((count, 2 * HD), jnp.bfloat16)] * pack,
        cost_estimate=cost(
            2 * pairs * 4 * GROUP * TILE * span * HD * 2,
            count * 4 * HD + half * QW * 8,
            2 * pairs * GROUP * TILE * span,
        ),
        compiler_params=pltpu.CompilerParams(vmem_limit_bytes=6 * MIB),
        name="attend",
    )(table, ends, starts, q, *kvs)


def out_body(first, step, own_ref, sib_ref, w_own, w_sib, *outs):
    own, sib = own_ref[...], sib_ref[...]
    for n in range(outs[0].shape[1] // step):
        columns = slice(first + n * step, first + (n + 1) * step)
        sums = jnp.dot(own, w_own[:, columns], preferred_element_type=jnp.float32)
        sums += jnp.dot(sib, w_sib[:, columns], preferred_element_type=jnp.float32)
        for i, out in enumerate(outs):
            out[:, n * step : (n + 1) * step] = sums[i * TILE : (i + 1) * TILE].astype(jnp.bfloat16)


def out_project(own, sib, w_own, w_sib, half, step=512):
    depth, width = w_own.shape
    part = width // 2
    rows = own.shape[0]
    n_out = rows // TILE
    vmem = pl.BlockSpec(memory_space=pltpu.VMEM)
    return pl.pallas_call(
        functools.partial(out_body, half * part, step),
        in_specs=[vmem] * 4,
        out_specs=[vmem] * n_out,
        out_shape=[jax.ShapeDtypeStruct((TILE, part), jnp.bfloat16)] * n_out,
        cost_estimate=cost(
            4 * rows * depth * part, 4 * depth * part + 4 * rows * depth + 2 * rows * part
        ),
        compiler_params=pltpu.CompilerParams(vmem_limit_bytes=4 * MIB),
        name="out_project",
    )(own, sib, w_own, w_sib)


def final_body(p_lo, p_hi, a_lo, a_hi, b_lo, b_hi, out_ref):
    f32 = jnp.float32
    half = p_lo.shape[1]
    lo = p_lo[...].astype(f32) + a_lo[...].astype(f32) + b_lo[...].astype(f32)
    hi = p_hi[...].astype(f32) + a_hi[...].astype(f32) + b_hi[...].astype(f32)
    out_ref[:, :half] = lo.astype(jnp.bfloat16)
    out_ref[:, half:] = hi.astype(jnp.bfloat16)


def final_sum(*parts):
    rows, half = parts[0].shape
    block = 32
    return pl.pallas_call(
        final_body,
        grid=(rows // block,),
        in_specs=[pl.BlockSpec((block, half), lambda i: (i, 0))] * 6,
        out_specs=pl.BlockSpec((block, 2 * half), lambda i: (i, 0)),
        out_shape=jax.ShapeDtypeStruct((rows, 2 * half), jnp.bfloat16),
        cost_estimate=cost(6 * rows * half, 16 * rows * half),
        compiler_params=pltpu.CompilerParams(vmem_limit_bytes=24 * MIB),
        name="final_sum",
    )(*parts)


def add_body(a0, b0, a1, b1, out0, out1):
    f32 = jnp.float32
    out0[...] = (a0[...].astype(f32) + b0[...].astype(f32)).astype(jnp.bfloat16)
    out1[...] = (a1[...].astype(f32) + b1[...].astype(f32)).astype(jnp.bfloat16)


def add_two(a0, b0, a1, b1, block=32):
    rows, width = a0.shape
    one = pl.BlockSpec((block, width), lambda i: (i, 0))
    return pl.pallas_call(
        add_body,
        grid=(rows // block,),
        in_specs=[one] * 4,
        out_specs=[one] * 2,
        out_shape=[jax.ShapeDtypeStruct((rows, width), jnp.bfloat16)] * 2,
        cost_estimate=cost(2 * rows * width, 12 * rows * width),
        compiler_params=pltpu.CompilerParams(vmem_limit_bytes=16 * MIB),
        name="add_two",
    )(a0, b0, a1, b1)


def shards(tokens, norm_gain, w_qkv, w_out, doc_lengths, span_slots):
    ctx = lax.axis_index("ctx")
    tp = lax.axis_index("tp")
    x, y, z, core = ctx // 2, ctx % 2, tp // 2, tp % 2
    gain = norm_gain.reshape(1, -1)
    rows = norm(in_hbm(tokens), in_hbm(gain))
    low, high = z_send(rows, 1), z_send(rows, -1)
    sib_rows = swap(rows)
    w_sib = swap(w_out)
    w_qkv, rows = lax.optimization_barrier((w_qkv, rows))
    (w_kv,) = load([w_qkv], [(QW, 2 * HD)])
    sib_rows, w_kv = lax.optimization_barrier((sib_rows, w_kv))
    sib_rows, doc_lengths, span_slots = lax.optimization_barrier((sib_rows, doc_lengths, span_slots))

    n_spans = span_slots.shape[0]
    per_span = 4
    span = per_span * TILE
    ends = jnp.cumsum(doc_lengths).astype(jnp.int32)
    numbers = jnp.arange(n_spans, dtype=jnp.int32)
    slot_of = jnp.sum(
        jnp.where(span_slots[None, :] == numbers[:, None], numbers[None, :], 0), axis=1
    )
    tile_no = jnp.arange(per_span, dtype=jnp.int32)[None, :]
    slot = slot_of[:, None]
    tile_tp = (slot % 2) * per_span + tile_no
    rank = slot // 2
    rel_z = (tile_tp // 2 - z) % NZ
    z_base = jnp.where(rel_z == 0, Z_BASE[0], 0)
    for i in range(1, NZ):
        z_base = jnp.where(rel_z == i, Z_BASE[i], z_base)
    rel_src = ((rank // 2 - x) % NX) * 2 + (rank % 2 != y).astype(jnp.int32)
    table = rel_src * 1024 + z_base + (tile_tp % 2 != core).astype(jnp.int32) * TILE
    table = table.reshape(-1).astype(jnp.int32)
    own_spans = lax.dynamic_slice_in_dim(span_slots, 2 * ctx, 2, 0)

    def starts_of(*dzs):
        tps = jnp.stack([((z + dz) % NZ) * 2 + c for dz in dzs for c in (core, 1 - core)])
        blocks = jnp.where(tps // per_span == 0, own_spans[0], own_spans[1])
        return (blocks * span + (tps % per_span) * TILE).astype(jnp.int32)

    starts_d, starts_b, starts_a = starts_of(2), starts_of(-1, 1), starts_of(0)
    (kv_a,) = project([rows, sib_rows], w_kv, 0, (2 * HD,))
    pair_a = y_pair(kv_a)
    pair_a, w_sib, table, ends, starts_d, starts_b, starts_a = lax.optimization_barrier(
        (pair_a, w_sib, table, ends, starts_d, starts_b, starts_a)
    )
    all_a = x_all(pair_a)
    far0, far1 = halves(low, high)
    low, high, far0, far1, *all_a = lax.optimization_barrier((low, high, far0, far1, *all_a))
    far0, far1 = z_send(far0, 1), z_send(far1, -1)
    group_b = [low, swap(low), high, swap(high)]
    (kv_b,) = project(group_b, w_kv, 0, (2 * HD,))
    other_b = y_swap(kv_b)
    left0, right0 = x_send(kv_b, 1), x_send(kv_b, -1)
    w_out, w_sib, kv_b = lax.optimization_barrier((w_out, w_sib, kv_b))
    w_out, w_sib = load([w_out, w_sib], [(0, w_out.shape[1])] * 2)
    left0, right0, other_b, w_out, w_sib = lax.optimization_barrier(
        (left0, right0, other_b, w_out, w_sib)
    )
    left1, right1 = x_send(other_b, 1), x_send(other_b, -1)
    *group_b, other_b = lax.optimization_barrier((*group_b, other_b))
    (q_b,) = project(group_b, w_qkv, 0, (QW,))
    far0, far1, left1, right1, q_b = lax.optimization_barrier((far0, far1, left1, right1, q_b))
    all_b = [
        (kv_b, other_b),
        (right0, right1),
        (x_send(left0, 1), x_send(right1, -1)),
        (left0, left1),
    ]
    group_d = [far0, far1, swap(far0), swap(far1)]
    (kv_d,) = project(group_d, w_kv, 0, (2 * HD,))
    pair_d = y_pair(kv_d)
    *group_d, pair_d = lax.optimization_barrier((*group_d, pair_d))
    (q_d,) = project(group_d, w_qkv, 0, (QW,))
    kvs, places = [], []
    for group, base in ((all_a, 0), (all_b, 256), (x_all(pair_d), 768)):
        for i, one in enumerate(group):
            parts = one if isinstance(one, tuple) else (one,)
            count = sum(part.shape[0] for part in parts) // 2
            for j in range(2):
                which, src = (len(kvs) + j, 0) if len(parts) == 2 else (len(kvs), j * count)
                places.append((which, src, (2 * i + j) * 1024 + base, count))
            kvs.extend(parts)

    d_own, d_send, packed = attend(q_d, 0, 1, kvs, tuple(places), True, table, ends, starts_d, 1024)
    d_sib = swap(d_send)
    (d_lo,) = out_project(d_own, d_sib, w_out, w_sib, 0)
    (d_hi,) = out_project(d_own, d_sib, w_out, w_sib, 1)
    from_low, from_high = z_send(d_lo, 1), z_send(d_hi, -1)
    whole = ((0, 0, 0, packed.shape[0]),)
    packed, d_lo, d_hi = lax.optimization_barrier((packed, d_lo, d_hi))
    b_own, b_send = attend(q_b, 0, 2, [packed], whole, False, table, ends, starts_b, 1024)
    b_sib = swap(b_send)
    prev_lo, next_lo = out_project(b_own, b_sib, w_out, w_sib, 0)
    prev_hi, next_hi = out_project(b_own, b_sib, w_out, w_sib, 1)
    early_hi, early_lo = z_send(next_hi, 1), z_send(prev_lo, -1)
    sum_lo, sum_hi = add_two(next_lo, from_low, prev_hi, from_high)
    late_lo, late_hi = z_send(sum_lo, 1), z_send(sum_hi, -1)
    rows, sib_rows, packed, sum_lo, sum_hi = lax.optimization_barrier(
        (rows, sib_rows, packed, sum_lo, sum_hi)
    )
    (q_a,) = project([rows, sib_rows], w_qkv, 0, (QW,))
    a_own, a_send = attend(q_a, 0, 1, [packed], whole, False, table, ends, starts_a, 1024)
    a_sib = swap(a_send)
    (a_lo,) = out_project(a_own, a_sib, w_out, w_sib, 0)
    (a_hi,) = out_project(a_own, a_sib, w_out, w_sib, 1)
    return final_sum(a_lo, a_hi, early_lo, early_hi, late_lo, late_hi)


def solution(mesh):
    placed = (P(("dp", "ctx", "tp"), None), P(), P(None, "tp"), P("tp", None), P("dp"), P("dp"))
    return jax.shard_map(
        shards, mesh=mesh, in_specs=placed, out_specs=P(("dp", "ctx", "tp"), None), check_vma=False
    )
```

```python
import functools

import jax
import jax.numpy as jnp
from jax import lax
from jax.experimental import pallas as pl
from jax.experimental.pallas import tpu as pltpu
from jax.sharding import PartitionSpec as P

HD = 128
GROUP = 4
QW = GROUP * HD
NZ = 4
NX = 4
TILE = 128
KTILE = 256
MIB = 1 << 20
MASKED = -3e38
LOWEST = -2e31
SHARE = 1e-4
LOG2E = 1.4426950408889634

Z_BASE = (0, 512, 768, 256)


def z_perm(dz, dc):
    return [
        (z * 2 + c, ((z + dz) % NZ) * 2 + (c + dc) % 2) for z in range(NZ) for c in range(2)
    ]


def x_perm(dx, dy):
    return [
        (x * 2 + y, ((x + dx) % NX) * 2 + (y + dy) % 2) for x in range(NX) for y in range(2)
    ]


def z_send(value, dz):
    return lax.ppermute(value, "tp", z_perm(dz, 0))


def swap(value):
    return lax.ppermute(value, "tp", z_perm(0, 1))


def x_send(value, dx):
    return lax.ppermute(value, "ctx", x_perm(dx, 0))


def y_swap(value):
    return lax.ppermute(value, "ctx", x_perm(0, 1))


def in_hbm(value):
    return pltpu.with_memory_space_constraint(value, pltpu.HBM)


def cost(flops, nbytes, trans=0):
    return pl.CostEstimate(
        flops=int(flops * SHARE), bytes_accessed=int(nbytes * SHARE), transcendentals=int(trans * SHARE)
    )


def norm_body(x_ref, gain_ref, out_ref):
    block = x_ref.shape[0]
    x = x_ref[...].astype(jnp.float32)
    mean_sq = jnp.mean(x * x, axis=-1, keepdims=True)
    at = pl.multiple_of(pl.program_id(0) * block, block)
    out_ref[pl.ds(at, block)] = (x * lax.rsqrt(mean_sq + 1e-05) * gain_ref[...]).astype(jnp.bfloat16)


def norm(tokens, gain, block=64):
    rows, width = tokens.shape
    return pl.pallas_call(
        norm_body,
        grid=(rows // block,),
        in_specs=[
            pl.BlockSpec((block, width), lambda i: (i, 0)),
            pl.BlockSpec((1, width), lambda i: (0, 0)),
        ],
        out_specs=pl.BlockSpec(memory_space=pltpu.VMEM),
        out_shape=jax.ShapeDtypeStruct((rows, width), jnp.bfloat16),
        cost_estimate=cost(6 * rows * width, 4 * rows * width),
        compiler_params=pltpu.CompilerParams(vmem_limit_bytes=12 * MIB),
        name="norm",
    )(tokens, gain)


def halves_body(low, high, out_low, out_high):
    half = out_low.shape[0]
    out_low[...] = low[:half]
    out_high[...] = high[half:]


def halves(low, high):
    vmem = pl.BlockSpec(memory_space=pltpu.VMEM)
    shape = jax.ShapeDtypeStruct((low.shape[0] // 2, low.shape[1]), low.dtype)
    return pl.pallas_call(
        halves_body,
        in_specs=[vmem] * 2,
        out_specs=[vmem] * 2,
        out_shape=[shape] * 2,
        cost_estimate=cost(1, 1),
        compiler_params=pltpu.CompilerParams(vmem_limit_bytes=8 * MIB),
        name="halves",
    )(low, high)


def load_body(firsts, *refs):
    n_in = len(firsts)
    sem = refs[-1]
    copies = []
    for i, first in enumerate(firsts):
        src, dst = refs[i], refs[n_in + i]
        copies.append(
            pltpu.make_async_copy(src.at[:, pl.ds(first, dst.shape[1])], dst, sem.at[i])
        )
    for one in copies:
        one.start()
    for one in copies:
        one.wait()


def load(values, windows):
    n_in = len(values)
    return pl.pallas_call(
        functools.partial(load_body, tuple(first for first, _ in windows)),
        in_specs=[pl.BlockSpec(memory_space=pl.ANY)] * n_in,
        out_specs=[pl.BlockSpec(memory_space=pltpu.VMEM)] * n_in,
        out_shape=[
            jax.ShapeDtypeStruct((one.shape[0], width), one.dtype)
            for one, (_, width) in zip(values, windows)
        ],
        scratch_shapes=[pltpu.SemaphoreType.DMA((n_in,))],
        cost_estimate=cost(1, 1),
        compiler_params=pltpu.CompilerParams(vmem_limit_bytes=2 * MIB),
        name="load",
    )(*[in_hbm(one) for one in values])


def project_body(n_in, first, widths, depth, *refs):
    xs, w_ref = refs[:n_in], refs[n_in]
    outs = refs[n_in + 1 :]
    total = sum(widths)
    halves = [xs[: n_in // 2], xs[n_in // 2 :]] if total <= 2 * HD else [xs]
    sums = [None] * len(halves)
    for k in range(w_ref.shape[0] // depth):
        span = slice(k * depth, (k + 1) * depth)
        for i, half in enumerate(halves):
            part = jnp.dot(
                jnp.concatenate([x[:, span] for x in half], axis=0),
                w_ref[span, first : first + total],
                preferred_element_type=jnp.float32,
            )
            sums[i] = part if sums[i] is None else sums[i] + part
    at = 0
    for out, width in zip(outs, widths):
        row = 0
        for one in sums:
            out[row : row + one.shape[0]] = one[:, at : at + width].astype(jnp.bfloat16)
            row += one.shape[0]
        at += width


def project(xs, w, first, widths, depth=2048):
    total = sum(widths)
    rows = sum(x.shape[0] for x in xs)
    width = w.shape[0]
    vmem = pl.BlockSpec(memory_space=pltpu.VMEM)
    return pl.pallas_call(
        functools.partial(project_body, len(xs), first, widths, depth),
        in_specs=[vmem] * (len(xs) + 1),
        out_specs=[vmem] * len(widths),
        out_shape=[jax.ShapeDtypeStruct((rows, one), jnp.bfloat16) for one in widths],
        cost_estimate=cost(2 * rows * width * total, 2 * width * (rows + total)),
        compiler_params=pltpu.CompilerParams(vmem_limit_bytes=6 * MIB + 4 * rows * total),
        name="project",
    )(*xs, w)


def y_pair(kv):
    return jnp.concatenate([kv, y_swap(kv)], axis=0)


def x_all(pair):
    return [pair, x_send(pair, -1), x_send(pair, 2), x_send(pair, 1)]


def attend_body(n_doc, n_kv, places, pack, table_ref, ends_ref, starts_ref, q_ref, *refs):
    pieces = refs[:n_kv]
    keep_ref, send_ref = refs[n_kv : n_kv + 2]
    kv = refs[n_kv + 2] if pack else pieces[0]
    pair = pl.program_id(0)

    if pack:

        @pl.when(pair == 0)
        def _():
            for which, src, dst, count in places:
                kv[dst : dst + count] = pieces[which][src : src + count]

    rows = GROUP * TILE
    starts = [starts_ref[2 * pair + j] for j in range(2)]
    low = jnp.minimum(starts[0], starts[1])
    high = jnp.maximum(starts[0], starts[1]) + TILE - 1
    offset = lax.rem(lax.broadcasted_iota(jnp.int32, (1, rows), 1), TILE)
    q_pos = [start + offset for start in starts]
    doc_start = [jnp.zeros((1, rows), jnp.int32) for _ in range(2)]
    first, last = jnp.int32(0), jnp.int32(0)
    for i in range(n_doc):
        end = ends_ref[i]
        doc_start = [jnp.where(q_pos[j] >= end, end, doc_start[j]) for j in range(2)]
        first = jnp.where(low >= end, end, first)
        last = jnp.where(high >= end, end, last)
    q_t = []
    for j in range(2):
        block = q_ref[j * TILE : (j + 1) * TILE].astype(jnp.float32)
        q_t.append(
            jnp.concatenate(
                [block[:, h * HD : (h + 1) * HD].T for h in range(GROUP)], axis=1
            ).astype(jnp.bfloat16)
        )
    scale = LOG2E / HD**0.5
    ratio = KTILE // TILE
    k_iota = lax.broadcasted_iota(jnp.int32, (KTILE, rows), 0)

    def step(at, state, masked):
        spots = [pl.multiple_of(table_ref[at * ratio + i], TILE) for i in range(ratio)]
        keys = jnp.concatenate([kv[pl.ds(spot, TILE), :HD] for spot in spots], axis=0)
        vals = jnp.concatenate([kv[pl.ds(spot, TILE), HD:] for spot in spots], axis=0)
        scores = [jnp.dot(keys, q_t[j], preferred_element_type=jnp.float32) for j in range(2)]
        out = []
        for j in range(2):
            top, total, acc = state[j]
            s = scores[j]
            if masked:
                base = at * KTILE
                allowed = (k_iota <= q_pos[j] - base) & (k_iota >= doc_start[j] - base)
                s = jnp.where(allowed, s, MASKED)
            new_top = jnp.maximum(top, jnp.max(s, axis=0, keepdims=True))
            e = jnp.exp2((s - new_top) * scale)
            factor = jnp.exp2((top - new_top) * scale)
            total = total * factor + jnp.sum(e, axis=0, keepdims=True)
            acc = acc * factor + lax.dot_general(
                vals,
                e.astype(jnp.bfloat16),
                (((0,), (0,)), ((), ())),
                preferred_element_type=jnp.float32,
            )
            out.append((new_top, total, acc))
        return tuple(out)

    state = tuple(
        (
            jnp.full((1, rows), LOWEST, jnp.float32),
            jnp.zeros((1, rows), jnp.float32),
            jnp.zeros((HD, rows), jnp.float32),
        )
        for _ in range(2)
    )
    begin, stop = first // KTILE, high // KTILE + 1
    inner = (last + KTILE - 1) // KTILE
    outer = jnp.maximum(inner, low // KTILE)
    masked_step = functools.partial(step, masked=True)
    state = lax.fori_loop(begin, jnp.minimum(inner, stop), masked_step, state)
    state = lax.fori_loop(inner, outer, functools.partial(step, masked=False), state)
    state = lax.fori_loop(outer, stop, masked_step, state)
    for (top, total, acc), out_ref in zip(state, (keep_ref, send_ref)):
        out_t = acc / total
        out_ref[...] = jnp.concatenate(
            [out_t[:, h * TILE : (h + 1) * TILE].T for h in range(GROUP)], axis=1
        ).astype(jnp.bfloat16)


def attend(q, first, pairs, kvs, places, pack, table, ends, starts, span):
    half = pairs * TILE
    count = sum(place[3] for place in places)
    vmem = pl.BlockSpec(memory_space=pltpu.VMEM)
    spec = pltpu.PrefetchScalarGridSpec(
        num_scalar_prefetch=3,
        grid=(pairs,),
        in_specs=[pl.BlockSpec((2 * TILE, QW), lambda i, *_: (first + i, 0))]
        + [vmem] * len(kvs),
        out_specs=[pl.BlockSpec((TILE, QW), lambda i, *_: (i, 0))] * 2 + [vmem] * pack,
    )
    return pl.pallas_call(
        functools.partial(attend_body, ends.shape[0], len(kvs), places, pack),
        grid_spec=spec,
        out_shape=[jax.ShapeDtypeStruct((half, QW), jnp.bfloat16)] * 2
        + [jax.ShapeDtypeStruct((count, 2 * HD), jnp.bfloat16)] * pack,
        cost_estimate=cost(
            2 * pairs * 4 * GROUP * TILE * span * HD * 2,
            count * 4 * HD + half * QW * 8,
            2 * pairs * GROUP * TILE * span,
        ),
        compiler_params=pltpu.CompilerParams(vmem_limit_bytes=6 * MIB),
        name="attend",
    )(table, ends, starts, q, *kvs)


def out_body(first, step, own_ref, sib_ref, w_own, w_sib, *outs):
    own, sib = own_ref[...], sib_ref[...]
    for n in range(outs[0].shape[1] // step):
        columns = slice(first + n * step, first + (n + 1) * step)
        sums = jnp.dot(own, w_own[:, columns], preferred_element_type=jnp.float32)
        sums += jnp.dot(sib, w_sib[:, columns], preferred_element_type=jnp.float32)
        for i, out in enumerate(outs):
            out[:, n * step : (n + 1) * step] = sums[i * TILE : (i + 1) * TILE].astype(jnp.bfloat16)


def out_project(own, sib, w_own, w_sib, half, step=512):
    depth, width = w_own.shape
    part = width // 2
    rows = own.shape[0]
    n_out = rows // TILE
    vmem = pl.BlockSpec(memory_space=pltpu.VMEM)
    return pl.pallas_call(
        functools.partial(out_body, half * part, step),
        in_specs=[vmem] * 4,
        out_specs=[vmem] * n_out,
        out_shape=[jax.ShapeDtypeStruct((TILE, part), jnp.bfloat16)] * n_out,
        cost_estimate=cost(
            4 * rows * depth * part, 4 * depth * part + 4 * rows * depth + 2 * rows * part
        ),
        compiler_params=pltpu.CompilerParams(vmem_limit_bytes=4 * MIB),
        name="out_project",
    )(own, sib, w_own, w_sib)


def final_body(p_lo, p_hi, a_lo, a_hi, b_lo, b_hi, out_ref):
    f32 = jnp.float32
    half = p_lo.shape[1]
    lo = p_lo[...].astype(f32) + a_lo[...].astype(f32) + b_lo[...].astype(f32)
    hi = p_hi[...].astype(f32) + a_hi[...].astype(f32) + b_hi[...].astype(f32)
    out_ref[:, :half] = lo.astype(jnp.bfloat16)
    out_ref[:, half:] = hi.astype(jnp.bfloat16)


def final_sum(*parts):
    rows, half = parts[0].shape
    block = 32
    return pl.pallas_call(
        final_body,
        grid=(rows // block,),
        in_specs=[pl.BlockSpec((block, half), lambda i: (i, 0))] * 6,
        out_specs=pl.BlockSpec((block, 2 * half), lambda i: (i, 0)),
        out_shape=jax.ShapeDtypeStruct((rows, 2 * half), jnp.bfloat16),
        cost_estimate=cost(6 * rows * half, 16 * rows * half),
        compiler_params=pltpu.CompilerParams(vmem_limit_bytes=24 * MIB),
        name="final_sum",
    )(*parts)


def add_body(a0, b0, a1, b1, out0, out1):
    f32 = jnp.float32
    out0[...] = (a0[...].astype(f32) + b0[...].astype(f32)).astype(jnp.bfloat16)
    out1[...] = (a1[...].astype(f32) + b1[...].astype(f32)).astype(jnp.bfloat16)


def add_two(a0, b0, a1, b1, block=32):
    rows, width = a0.shape
    one = pl.BlockSpec((block, width), lambda i: (i, 0))
    return pl.pallas_call(
        add_body,
        grid=(rows // block,),
        in_specs=[one] * 4,
        out_specs=[one] * 2,
        out_shape=[jax.ShapeDtypeStruct((rows, width), jnp.bfloat16)] * 2,
        cost_estimate=cost(2 * rows * width, 12 * rows * width),
        compiler_params=pltpu.CompilerParams(vmem_limit_bytes=16 * MIB),
        name="add_two",
    )(a0, b0, a1, b1)


def shards(tokens, norm_gain, w_qkv, w_out, doc_lengths, span_slots):
    ctx = lax.axis_index("ctx")
    tp = lax.axis_index("tp")
    x, y, z, core = ctx // 2, ctx % 2, tp // 2, tp % 2
    gain = norm_gain.reshape(1, -1)
    rows = norm(in_hbm(tokens), in_hbm(gain))
    low, high = z_send(rows, 1), z_send(rows, -1)
    sib_rows = swap(rows)
    w_sib = swap(w_out)
    w_qkv, rows = lax.optimization_barrier((w_qkv, rows))
    (w_kv,) = load([w_qkv], [(QW, 2 * HD)])
    sib_rows, w_kv = lax.optimization_barrier((sib_rows, w_kv))
    sib_rows, doc_lengths, span_slots = lax.optimization_barrier((sib_rows, doc_lengths, span_slots))

    n_spans = span_slots.shape[0]
    per_span = 4
    span = per_span * TILE
    ends = jnp.cumsum(doc_lengths).astype(jnp.int32)
    numbers = jnp.arange(n_spans, dtype=jnp.int32)
    slot_of = jnp.sum(
        jnp.where(span_slots[None, :] == numbers[:, None], numbers[None, :], 0), axis=1
    )
    tile_no = jnp.arange(per_span, dtype=jnp.int32)[None, :]
    slot = slot_of[:, None]
    tile_tp = (slot % 2) * per_span + tile_no
    rank = slot // 2
    rel_z = (tile_tp // 2 - z) % NZ
    z_base = jnp.where(rel_z == 0, Z_BASE[0], 0)
    for i in range(1, NZ):
        z_base = jnp.where(rel_z == i, Z_BASE[i], z_base)
    rel_src = ((rank // 2 - x) % NX) * 2 + (rank % 2 != y).astype(jnp.int32)
    table = rel_src * 1024 + z_base + (tile_tp % 2 != core).astype(jnp.int32) * TILE
    table = table.reshape(-1).astype(jnp.int32)
    own_spans = lax.dynamic_slice_in_dim(span_slots, 2 * ctx, 2, 0)

    def starts_of(*dzs):
        tps = jnp.stack([((z + dz) % NZ) * 2 + c for dz in dzs for c in (core, 1 - core)])
        blocks = jnp.where(tps // per_span == 0, own_spans[0], own_spans[1])
        return (blocks * span + (tps % per_span) * TILE).astype(jnp.int32)

    starts_d, starts_b, starts_a = starts_of(2), starts_of(-1, 1), starts_of(0)
    (kv_a,) = project([rows, sib_rows], w_kv, 0, (2 * HD,))
    pair_a = y_pair(kv_a)
    pair_a, w_sib, table, ends, starts_d, starts_b, starts_a = lax.optimization_barrier(
        (pair_a, w_sib, table, ends, starts_d, starts_b, starts_a)
    )
    all_a = x_all(pair_a)
    far0, far1 = halves(low, high)
    low, high, far0, far1, *all_a = lax.optimization_barrier((low, high, far0, far1, *all_a))
    far0, far1 = z_send(far0, 1), z_send(far1, -1)
    group_b = [low, swap(low), high, swap(high)]
    (kv_b,) = project(group_b, w_kv, 0, (2 * HD,))
    other_b = y_swap(kv_b)
    left0, right0 = x_send(kv_b, 1), x_send(kv_b, -1)
    w_out, w_sib, kv_b = lax.optimization_barrier((w_out, w_sib, kv_b))
    w_out, w_sib = load([w_out, w_sib], [(0, w_out.shape[1])] * 2)
    left0, right0, other_b, w_out, w_sib = lax.optimization_barrier(
        (left0, right0, other_b, w_out, w_sib)
    )
    left1, right1 = x_send(other_b, 1), x_send(other_b, -1)
    *group_b, other_b = lax.optimization_barrier((*group_b, other_b))
    (q_b,) = project(group_b, w_qkv, 0, (QW,))
    far0, far1, left1, right1, q_b = lax.optimization_barrier((far0, far1, left1, right1, q_b))
    all_b = [
        (kv_b, other_b),
        (right0, right1),
        (x_send(left0, 1), x_send(right1, -1)),
        (left0, left1),
    ]
    group_d = [far0, far1, swap(far0), swap(far1)]
    (kv_d,) = project(group_d, w_kv, 0, (2 * HD,))
    other_d = y_swap(kv_d)
    left2, right2 = x_send(kv_d, 1), x_send(kv_d, -1)
    *group_d, other_d, left2, right2 = lax.optimization_barrier((*group_d, other_d, left2, right2))
    left3, right3 = x_send(other_d, 1), x_send(other_d, -1)
    all_d = [
        (kv_d, other_d),
        (right2, right3),
        (x_send(left2, 1), x_send(right3, -1)),
        (left2, left3),
    ]
    (q_d,) = project(group_d, w_qkv, 0, (QW,))
    kvs, places = [], []
    for group, base in ((all_a, 0), (all_b, 256), (all_d, 768)):
        for i, one in enumerate(group):
            parts = one if isinstance(one, tuple) else (one,)
            count = sum(part.shape[0] for part in parts) // 2
            for j in range(2):
                which, src = (len(kvs) + j, 0) if len(parts) == 2 else (len(kvs), j * count)
                places.append((which, src, (2 * i + j) * 1024 + base, count))
            kvs.extend(parts)

    d_own, d_send, packed = attend(q_d, 0, 1, kvs, tuple(places), True, table, ends, starts_d, 1024)
    d_sib = swap(d_send)
    (d_lo,) = out_project(d_own, d_sib, w_out, w_sib, 0)
    (d_hi,) = out_project(d_own, d_sib, w_out, w_sib, 1)
    from_low, from_high = z_send(d_lo, 1), z_send(d_hi, -1)
    whole = ((0, 0, 0, packed.shape[0]),)
    packed, d_lo, d_hi = lax.optimization_barrier((packed, d_lo, d_hi))
    b_own, b_send = attend(q_b, 0, 2, [packed], whole, False, table, ends, starts_b, 1024)
    b_sib = swap(b_send)
    prev_lo, next_lo = out_project(b_own, b_sib, w_out, w_sib, 0)
    prev_hi, next_hi = out_project(b_own, b_sib, w_out, w_sib, 1)
    early_hi, early_lo = z_send(next_hi, 1), z_send(prev_lo, -1)
    sum_lo, sum_hi = add_two(next_lo, from_low, prev_hi, from_high)
    late_lo, late_hi = z_send(sum_lo, 1), z_send(sum_hi, -1)
    rows, sib_rows, packed, sum_lo, sum_hi = lax.optimization_barrier(
        (rows, sib_rows, packed, sum_lo, sum_hi)
    )
    (q_a,) = project([rows, sib_rows], w_qkv, 0, (QW,))
    a_own, a_send = attend(q_a, 0, 1, [packed], whole, False, table, ends, starts_a, 1024)
    a_sib = swap(a_send)
    (a_lo,) = out_project(a_own, a_sib, w_out, w_sib, 0)
    (a_hi,) = out_project(a_own, a_sib, w_out, w_sib, 1)
    return final_sum(a_lo, a_hi, early_lo, early_hi, late_lo, late_hi)


def solution(mesh):
    placed = (P(("dp", "ctx", "tp"), None), P(), P(None, "tp"), P("tp", None), P("dp"), P("dp"))
    return jax.shard_map(
        shards, mesh=mesh, in_specs=placed, out_specs=P(("dp", "ctx", "tp"), None), check_vma=False
    )
```

```python
import functools

import jax
import jax.numpy as jnp
from jax import lax
from jax.experimental import pallas as pl
from jax.experimental.pallas import tpu as pltpu
from jax.sharding import PartitionSpec as P

HD = 128
GROUP = 4
QW = GROUP * HD
NZ = 4
NX = 4
TILE = 128
KTILE = 256
MIB = 1 << 20
MASKED = -3e38
LOWEST = -2e31
SHARE = 1e-4
LOG2E = 1.4426950408889634

Z_BASE = (0, 512, 768, 256)


def z_perm(dz, dc):
    return [
        (z * 2 + c, ((z + dz) % NZ) * 2 + (c + dc) % 2) for z in range(NZ) for c in range(2)
    ]


def x_perm(dx, dy):
    return [
        (x * 2 + y, ((x + dx) % NX) * 2 + (y + dy) % 2) for x in range(NX) for y in range(2)
    ]


def z_send(value, dz):
    return lax.ppermute(value, "tp", z_perm(dz, 0))


def swap(value):
    return lax.ppermute(value, "tp", z_perm(0, 1))


def x_send(value, dx):
    return lax.ppermute(value, "ctx", x_perm(dx, 0))


def y_swap(value):
    return lax.ppermute(value, "ctx", x_perm(0, 1))


def in_hbm(value):
    return pltpu.with_memory_space_constraint(value, pltpu.HBM)


def cost(flops, nbytes, trans=0):
    return pl.CostEstimate(
        flops=int(flops * SHARE), bytes_accessed=int(nbytes * SHARE), transcendentals=int(trans * SHARE)
    )


def norm_body(x_ref, gain_ref, out_ref):
    block = x_ref.shape[0]
    x = x_ref[...].astype(jnp.float32)
    mean_sq = jnp.mean(x * x, axis=-1, keepdims=True)
    at = pl.multiple_of(pl.program_id(0) * block, block)
    out_ref[pl.ds(at, block)] = (x * lax.rsqrt(mean_sq + 1e-05) * gain_ref[...]).astype(jnp.bfloat16)


def norm(tokens, gain, block=64):
    rows, width = tokens.shape
    return pl.pallas_call(
        norm_body,
        grid=(rows // block,),
        in_specs=[
            pl.BlockSpec((block, width), lambda i: (i, 0)),
            pl.BlockSpec((1, width), lambda i: (0, 0)),
        ],
        out_specs=pl.BlockSpec(memory_space=pltpu.VMEM),
        out_shape=jax.ShapeDtypeStruct((rows, width), jnp.bfloat16),
        cost_estimate=cost(6 * rows * width, 4 * rows * width),
        compiler_params=pltpu.CompilerParams(vmem_limit_bytes=12 * MIB),
        name="norm",
    )(tokens, gain)


def halves_body(low, high, out_low, out_high):
    half = out_low.shape[0]
    out_low[...] = low[:half]
    out_high[...] = high[half:]


def halves(low, high):
    vmem = pl.BlockSpec(memory_space=pltpu.VMEM)
    shape = jax.ShapeDtypeStruct((low.shape[0] // 2, low.shape[1]), low.dtype)
    return pl.pallas_call(
        halves_body,
        in_specs=[vmem] * 2,
        out_specs=[vmem] * 2,
        out_shape=[shape] * 2,
        cost_estimate=cost(1, 1),
        compiler_params=pltpu.CompilerParams(vmem_limit_bytes=8 * MIB),
        name="halves",
    )(low, high)


def load_body(firsts, *refs):
    n_in = len(firsts)
    sem = refs[-1]
    copies = []
    for i, first in enumerate(firsts):
        src, dst = refs[i], refs[n_in + i]
        copies.append(
            pltpu.make_async_copy(src.at[:, pl.ds(first, dst.shape[1])], dst, sem.at[i])
        )
    for one in copies:
        one.start()
    for one in copies:
        one.wait()


def load(values, windows):
    n_in = len(values)
    return pl.pallas_call(
        functools.partial(load_body, tuple(first for first, _ in windows)),
        in_specs=[pl.BlockSpec(memory_space=pl.ANY)] * n_in,
        out_specs=[pl.BlockSpec(memory_space=pltpu.VMEM)] * n_in,
        out_shape=[
            jax.ShapeDtypeStruct((one.shape[0], width), one.dtype)
            for one, (_, width) in zip(values, windows)
        ],
        scratch_shapes=[pltpu.SemaphoreType.DMA((n_in,))],
        cost_estimate=cost(1, 1),
        compiler_params=pltpu.CompilerParams(vmem_limit_bytes=2 * MIB),
        name="load",
    )(*[in_hbm(one) for one in values])


def project_body(n_in, first, widths, depth, *refs):
    xs, w_ref = refs[:n_in], refs[n_in]
    outs = refs[n_in + 1 :]
    total = sum(widths)
    halves = [xs[: n_in // 2], xs[n_in // 2 :]] if total <= 2 * HD else [xs]
    sums = [None] * len(halves)
    for k in range(w_ref.shape[0] // depth):
        span = slice(k * depth, (k + 1) * depth)
        for i, half in enumerate(halves):
            part = jnp.dot(
                jnp.concatenate([x[:, span] for x in half], axis=0),
                w_ref[span, first : first + total],
                preferred_element_type=jnp.float32,
            )
            sums[i] = part if sums[i] is None else sums[i] + part
    at = 0
    for out, width in zip(outs, widths):
        row = 0
        for one in sums:
            out[row : row + one.shape[0]] = one[:, at : at + width].astype(jnp.bfloat16)
            row += one.shape[0]
        at += width


def project(xs, w, first, widths, depth=2048):
    total = sum(widths)
    rows = sum(x.shape[0] for x in xs)
    width = w.shape[0]
    vmem = pl.BlockSpec(memory_space=pltpu.VMEM)
    return pl.pallas_call(
        functools.partial(project_body, len(xs), first, widths, depth),
        in_specs=[vmem] * (len(xs) + 1),
        out_specs=[vmem] * len(widths),
        out_shape=[jax.ShapeDtypeStruct((rows, one), jnp.bfloat16) for one in widths],
        cost_estimate=cost(2 * rows * width * total, 2 * width * (rows + total)),
        compiler_params=pltpu.CompilerParams(vmem_limit_bytes=6 * MIB + 4 * rows * total),
        name="project",
    )(*xs, w)


def y_pair(kv):
    return jnp.concatenate([kv, y_swap(kv)], axis=0)


def x_all(pair):
    return [pair, x_send(pair, -1), x_send(pair, 2), x_send(pair, 1)]


def attend_body(n_doc, n_kv, places, pack, table_ref, ends_ref, starts_ref, q_ref, *refs):
    pieces = refs[:n_kv]
    keep_ref, send_ref = refs[n_kv : n_kv + 2]
    kv = refs[n_kv + 2] if pack else pieces[0]
    pair = pl.program_id(0)

    if pack:

        @pl.when(pair == 0)
        def _():
            for which, src, dst, count in places:
                kv[dst : dst + count] = pieces[which][src : src + count]

    rows = GROUP * TILE
    starts = [starts_ref[2 * pair + j] for j in range(2)]
    low = jnp.minimum(starts[0], starts[1])
    high = jnp.maximum(starts[0], starts[1]) + TILE - 1
    offset = lax.rem(lax.broadcasted_iota(jnp.int32, (1, rows), 1), TILE)
    q_pos = [start + offset for start in starts]
    doc_start = [jnp.zeros((1, rows), jnp.int32) for _ in range(2)]
    first, last = jnp.int32(0), jnp.int32(0)
    for i in range(n_doc):
        end = ends_ref[i]
        doc_start = [jnp.where(q_pos[j] >= end, end, doc_start[j]) for j in range(2)]
        first = jnp.where(low >= end, end, first)
        last = jnp.where(high >= end, end, last)
    q_t = []
    for j in range(2):
        block = q_ref[j * TILE : (j + 1) * TILE].astype(jnp.float32)
        q_t.append(
            jnp.concatenate(
                [block[:, h * HD : (h + 1) * HD].T for h in range(GROUP)], axis=1
            ).astype(jnp.bfloat16)
        )
    scale = LOG2E / HD**0.5
    ratio = KTILE // TILE
    k_iota = lax.broadcasted_iota(jnp.int32, (KTILE, rows), 0)

    def step(at, state, masked):
        spots = [pl.multiple_of(table_ref[at * ratio + i], TILE) for i in range(ratio)]
        keys = jnp.concatenate([kv[pl.ds(spot, TILE), :HD] for spot in spots], axis=0)
        vals = jnp.concatenate([kv[pl.ds(spot, TILE), HD:] for spot in spots], axis=0)
        scores = [jnp.dot(keys, q_t[j], preferred_element_type=jnp.float32) for j in range(2)]
        out = []
        for j in range(2):
            top, total, acc = state[j]
            s = scores[j]
            if masked:
                base = at * KTILE
                allowed = (k_iota <= q_pos[j] - base) & (k_iota >= doc_start[j] - base)
                s = jnp.where(allowed, s, MASKED)
            new_top = jnp.maximum(top, jnp.max(s, axis=0, keepdims=True))
            e = jnp.exp2((s - new_top) * scale)
            factor = jnp.exp2((top - new_top) * scale)
            total = total * factor + jnp.sum(e, axis=0, keepdims=True)
            acc = acc * factor + lax.dot_general(
                vals,
                e.astype(jnp.bfloat16),
                (((0,), (0,)), ((), ())),
                preferred_element_type=jnp.float32,
            )
            out.append((new_top, total, acc))
        return tuple(out)

    state = tuple(
        (
            jnp.full((1, rows), LOWEST, jnp.float32),
            jnp.zeros((1, rows), jnp.float32),
            jnp.zeros((HD, rows), jnp.float32),
        )
        for _ in range(2)
    )
    begin, stop = first // KTILE, high // KTILE + 1
    inner = (last + KTILE - 1) // KTILE
    outer = jnp.maximum(inner, low // KTILE)
    masked_step = functools.partial(step, masked=True)
    state = lax.fori_loop(begin, jnp.minimum(inner, stop), masked_step, state)
    state = lax.fori_loop(inner, outer, functools.partial(step, masked=False), state)
    state = lax.fori_loop(outer, stop, masked_step, state)
    for (top, total, acc), out_ref in zip(state, (keep_ref, send_ref)):
        out_t = acc / total
        out_ref[...] = jnp.concatenate(
            [out_t[:, h * TILE : (h + 1) * TILE].T for h in range(GROUP)], axis=1
        ).astype(jnp.bfloat16)


def attend(q, first, pairs, kvs, places, pack, table, ends, starts, span):
    half = pairs * TILE
    count = sum(place[3] for place in places)
    vmem = pl.BlockSpec(memory_space=pltpu.VMEM)
    spec = pltpu.PrefetchScalarGridSpec(
        num_scalar_prefetch=3,
        grid=(pairs,),
        in_specs=[pl.BlockSpec((2 * TILE, QW), lambda i, *_: (first + i, 0))]
        + [vmem] * len(kvs),
        out_specs=[pl.BlockSpec((TILE, QW), lambda i, *_: (i, 0))] * 2 + [vmem] * pack,
    )
    return pl.pallas_call(
        functools.partial(attend_body, ends.shape[0], len(kvs), places, pack),
        grid_spec=spec,
        out_shape=[jax.ShapeDtypeStruct((half, QW), jnp.bfloat16)] * 2
        + [jax.ShapeDtypeStruct((count, 2 * HD), jnp.bfloat16)] * pack,
        cost_estimate=cost(
            2 * pairs * 4 * GROUP * TILE * span * HD * 2,
            count * 4 * HD + half * QW * 8,
            2 * pairs * GROUP * TILE * span,
        ),
        compiler_params=pltpu.CompilerParams(vmem_limit_bytes=6 * MIB),
        name="attend",
    )(table, ends, starts, q, *kvs)


def out_body(first, step, own_ref, sib_ref, w_own, w_sib, *outs):
    own, sib = own_ref[...], sib_ref[...]
    for n in range(outs[0].shape[1] // step):
        columns = slice(first + n * step, first + (n + 1) * step)
        sums = jnp.dot(own, w_own[:, columns], preferred_element_type=jnp.float32)
        sums += jnp.dot(sib, w_sib[:, columns], preferred_element_type=jnp.float32)
        for i, out in enumerate(outs):
            out[:, n * step : (n + 1) * step] = sums[i * TILE : (i + 1) * TILE].astype(jnp.bfloat16)


def out_project(own, sib, w_own, w_sib, half, step=512):
    depth, width = w_own.shape
    part = width // 2
    rows = own.shape[0]
    n_out = rows // TILE
    vmem = pl.BlockSpec(memory_space=pltpu.VMEM)
    return pl.pallas_call(
        functools.partial(out_body, half * part, step),
        in_specs=[vmem] * 4,
        out_specs=[vmem] * n_out,
        out_shape=[jax.ShapeDtypeStruct((TILE, part), jnp.bfloat16)] * n_out,
        cost_estimate=cost(
            4 * rows * depth * part, 4 * depth * part + 4 * rows * depth + 2 * rows * part
        ),
        compiler_params=pltpu.CompilerParams(vmem_limit_bytes=4 * MIB),
        name="out_project",
    )(own, sib, w_own, w_sib)


def final_body(p_lo, p_hi, a_lo, a_hi, b_lo, b_hi, out_ref):
    f32 = jnp.float32
    half = p_lo.shape[1]
    lo = p_lo[...].astype(f32) + a_lo[...].astype(f32) + b_lo[...].astype(f32)
    hi = p_hi[...].astype(f32) + a_hi[...].astype(f32) + b_hi[...].astype(f32)
    out_ref[:, :half] = lo.astype(jnp.bfloat16)
    out_ref[:, half:] = hi.astype(jnp.bfloat16)


def final_sum(*parts):
    rows, half = parts[0].shape
    block = 32
    return pl.pallas_call(
        final_body,
        grid=(rows // block,),
        in_specs=[pl.BlockSpec((block, half), lambda i: (i, 0))] * 6,
        out_specs=pl.BlockSpec((block, 2 * half), lambda i: (i, 0)),
        out_shape=jax.ShapeDtypeStruct((rows, 2 * half), jnp.bfloat16),
        cost_estimate=cost(6 * rows * half, 16 * rows * half),
        compiler_params=pltpu.CompilerParams(vmem_limit_bytes=24 * MIB),
        name="final_sum",
    )(*parts)


def add_body(a0, b0, a1, b1, out0, out1):
    f32 = jnp.float32
    out0[...] = (a0[...].astype(f32) + b0[...].astype(f32)).astype(jnp.bfloat16)
    out1[...] = (a1[...].astype(f32) + b1[...].astype(f32)).astype(jnp.bfloat16)


def add_two(a0, b0, a1, b1, block=32):
    rows, width = a0.shape
    one = pl.BlockSpec((block, width), lambda i: (i, 0))
    return pl.pallas_call(
        add_body,
        grid=(rows // block,),
        in_specs=[one] * 4,
        out_specs=[one] * 2,
        out_shape=[jax.ShapeDtypeStruct((rows, width), jnp.bfloat16)] * 2,
        cost_estimate=cost(2 * rows * width, 12 * rows * width),
        compiler_params=pltpu.CompilerParams(vmem_limit_bytes=16 * MIB),
        name="add_two",
    )(a0, b0, a1, b1)


def shards(tokens, norm_gain, w_qkv, w_out, doc_lengths, span_slots):
    ctx = lax.axis_index("ctx")
    tp = lax.axis_index("tp")
    x, y, z, core = ctx // 2, ctx % 2, tp // 2, tp % 2
    gain = norm_gain.reshape(1, -1)
    rows = norm(in_hbm(tokens), in_hbm(gain))
    low, high = z_send(rows, 1), z_send(rows, -1)
    sib_rows = swap(rows)
    w_sib = swap(w_out)
    w_qkv, rows = lax.optimization_barrier((w_qkv, rows))
    (w_kv,) = load([w_qkv], [(QW, 2 * HD)])
    sib_rows, w_kv = lax.optimization_barrier((sib_rows, w_kv))
    sib_rows, doc_lengths, span_slots = lax.optimization_barrier((sib_rows, doc_lengths, span_slots))

    n_spans = span_slots.shape[0]
    per_span = 4
    span = per_span * TILE
    ends = jnp.cumsum(doc_lengths).astype(jnp.int32)
    numbers = jnp.arange(n_spans, dtype=jnp.int32)
    slot_of = jnp.sum(
        jnp.where(span_slots[None, :] == numbers[:, None], numbers[None, :], 0), axis=1
    )
    tile_no = jnp.arange(per_span, dtype=jnp.int32)[None, :]
    slot = slot_of[:, None]
    tile_tp = (slot % 2) * per_span + tile_no
    rank = slot // 2
    rel_z = (tile_tp // 2 - z) % NZ
    z_base = jnp.where(rel_z == 0, Z_BASE[0], 0)
    for i in range(1, NZ):
        z_base = jnp.where(rel_z == i, Z_BASE[i], z_base)
    rel_src = ((rank // 2 - x) % NX) * 2 + (rank % 2 != y).astype(jnp.int32)
    table = rel_src * 1024 + z_base + (tile_tp % 2 != core).astype(jnp.int32) * TILE
    table = table.reshape(-1).astype(jnp.int32)
    own_spans = lax.dynamic_slice_in_dim(span_slots, 2 * ctx, 2, 0)

    def starts_of(*dzs):
        tps = jnp.stack([((z + dz) % NZ) * 2 + c for dz in dzs for c in (core, 1 - core)])
        blocks = jnp.where(tps // per_span == 0, own_spans[0], own_spans[1])
        return (blocks * span + (tps % per_span) * TILE).astype(jnp.int32)

    starts_d, starts_b, starts_a = starts_of(2), starts_of(-1, 1), starts_of(0)
    (kv_a,) = project([rows, sib_rows], w_kv, 0, (2 * HD,))
    pair_a = y_pair(kv_a)
    pair_a, w_sib, table, ends, starts_d, starts_b, starts_a = lax.optimization_barrier(
        (pair_a, w_sib, table, ends, starts_d, starts_b, starts_a)
    )
    all_a = x_all(pair_a)
    far0, far1 = halves(low, high)
    low, high, far0, far1, *all_a = lax.optimization_barrier((low, high, far0, far1, *all_a))
    group_b = [low, swap(low), high, swap(high)]
    far0, far1 = z_send(far0, 1), z_send(far1, -1)
    (kv_b,) = project(group_b, w_kv, 0, (2 * HD,))
    other_b = y_swap(kv_b)
    left0, right0 = x_send(kv_b, 1), x_send(kv_b, -1)
    w_out, w_sib, kv_b = lax.optimization_barrier((w_out, w_sib, kv_b))
    w_out, w_sib = load([w_out, w_sib], [(0, w_out.shape[1])] * 2)
    left0, right0, other_b, w_out, w_sib = lax.optimization_barrier(
        (left0, right0, other_b, w_out, w_sib)
    )
    left1, right1 = x_send(other_b, 1), x_send(other_b, -1)
    *group_b, other_b = lax.optimization_barrier((*group_b, other_b))
    (q_b,) = project(group_b, w_qkv, 0, (QW,))
    far0, far1, left1, right1, q_b = lax.optimization_barrier((far0, far1, left1, right1, q_b))
    all_b = [
        (kv_b, other_b),
        (right0, right1),
        (x_send(left0, 1), x_send(right1, -1)),
        (left0, left1),
    ]
    group_d = [far0, far1, swap(far0), swap(far1)]
    (kv_d,) = project(group_d, w_kv, 0, (2 * HD,))
    other_d = y_swap(kv_d)
    left2, right2 = x_send(kv_d, 1), x_send(kv_d, -1)
    *group_d, other_d, left2, right2 = lax.optimization_barrier((*group_d, other_d, left2, right2))
    left3, right3 = x_send(other_d, 1), x_send(other_d, -1)
    all_d = [
        (kv_d, other_d),
        (right2, right3),
        (x_send(left2, 1), x_send(other_d, 2)),
        (left2, left3),
    ]
    (q_d,) = project(group_d, w_qkv, 0, (QW,))
    kvs, places = [], []
    for group, base in ((all_a, 0), (all_b, 256), (all_d, 768)):
        for i, one in enumerate(group):
            parts = one if isinstance(one, tuple) else (one,)
            count = sum(part.shape[0] for part in parts) // 2
            for j in range(2):
                which, src = (len(kvs) + j, 0) if len(parts) == 2 else (len(kvs), j * count)
                places.append((which, src, (2 * i + j) * 1024 + base, count))
            kvs.extend(parts)

    d_own, d_send, packed = attend(q_d, 0, 1, kvs, tuple(places), True, table, ends, starts_d, 1024)
    d_sib = swap(d_send)
    (d_lo,) = out_project(d_own, d_sib, w_out, w_sib, 0)
    (d_hi,) = out_project(d_own, d_sib, w_out, w_sib, 1)
    from_low, from_high = z_send(d_lo, 1), z_send(d_hi, -1)
    whole = ((0, 0, 0, packed.shape[0]),)
    packed, d_lo, d_hi = lax.optimization_barrier((packed, d_lo, d_hi))
    b_own, b_send = attend(q_b, 0, 2, [packed], whole, False, table, ends, starts_b, 1024)
    b_sib = swap(b_send)
    prev_lo, next_lo = out_project(b_own, b_sib, w_out, w_sib, 0)
    prev_hi, next_hi = out_project(b_own, b_sib, w_out, w_sib, 1)
    early_hi, early_lo = z_send(next_hi, 1), z_send(prev_lo, -1)
    sum_lo, sum_hi = add_two(next_lo, from_low, prev_hi, from_high)
    late_lo, late_hi = z_send(sum_lo, 1), z_send(sum_hi, -1)
    rows, sib_rows, packed, sum_lo, sum_hi = lax.optimization_barrier(
        (rows, sib_rows, packed, sum_lo, sum_hi)
    )
    (q_a,) = project([rows, sib_rows], w_qkv, 0, (QW,))
    a_own, a_send = attend(q_a, 0, 1, [packed], whole, False, table, ends, starts_a, 1024)
    a_sib = swap(a_send)
    (a_lo,) = out_project(a_own, a_sib, w_out, w_sib, 0)
    (a_hi,) = out_project(a_own, a_sib, w_out, w_sib, 1)
    return final_sum(a_lo, a_hi, early_lo, early_hi, late_lo, late_hi)


def solution(mesh):
    placed = (P(("dp", "ctx", "tp"), None), P(), P(None, "tp"), P("tp", None), P("dp"), P("dp"))
    return jax.shard_map(
        shards, mesh=mesh, in_specs=placed, out_specs=P(("dp", "ctx", "tp"), None), check_vma=False
    )
```

```python
import functools

import jax
import jax.numpy as jnp
from jax import lax
from jax.experimental import pallas as pl
from jax.experimental.pallas import tpu as pltpu
from jax.sharding import PartitionSpec as P

HD = 128
GROUP = 4
QW = GROUP * HD
NZ = 4
NX = 4
TILE = 128
KTILE = 256
MIB = 1 << 20
MASKED = -3e38
LOWEST = -2e31
SHARE = 1e-4
LOG2E = 1.4426950408889634

Z_BASE = (0, 512, 768, 256)


def z_perm(dz, dc):
    return [
        (z * 2 + c, ((z + dz) % NZ) * 2 + (c + dc) % 2) for z in range(NZ) for c in range(2)
    ]


def x_perm(dx, dy):
    return [
        (x * 2 + y, ((x + dx) % NX) * 2 + (y + dy) % 2) for x in range(NX) for y in range(2)
    ]


def z_send(value, dz):
    return lax.ppermute(value, "tp", z_perm(dz, 0))


def swap(value):
    return lax.ppermute(value, "tp", z_perm(0, 1))


def x_send(value, dx):
    return lax.ppermute(value, "ctx", x_perm(dx, 0))


def y_swap(value):
    return lax.ppermute(value, "ctx", x_perm(0, 1))


def in_hbm(value):
    return pltpu.with_memory_space_constraint(value, pltpu.HBM)


def cost(flops, nbytes, trans=0):
    return pl.CostEstimate(
        flops=int(flops * SHARE), bytes_accessed=int(nbytes * SHARE), transcendentals=int(trans * SHARE)
    )


def norm_body(x_ref, gain_ref, out_ref):
    block = x_ref.shape[0]
    x = x_ref[...].astype(jnp.float32)
    mean_sq = jnp.mean(x * x, axis=-1, keepdims=True)
    at = pl.multiple_of(pl.program_id(0) * block, block)
    out_ref[pl.ds(at, block)] = (x * lax.rsqrt(mean_sq + 1e-05) * gain_ref[...]).astype(jnp.bfloat16)


def norm(tokens, gain, block=64):
    rows, width = tokens.shape
    return pl.pallas_call(
        norm_body,
        grid=(rows // block,),
        in_specs=[
            pl.BlockSpec((block, width), lambda i: (i, 0)),
            pl.BlockSpec((1, width), lambda i: (0, 0)),
        ],
        out_specs=pl.BlockSpec(memory_space=pltpu.VMEM),
        out_shape=jax.ShapeDtypeStruct((rows, width), jnp.bfloat16),
        cost_estimate=cost(6 * rows * width, 4 * rows * width),
        compiler_params=pltpu.CompilerParams(vmem_limit_bytes=12 * MIB),
        name="norm",
    )(tokens, gain)


def halves_body(low, high, out_low, out_high):
    half = out_low.shape[0]
    out_low[...] = low[:half]
    out_high[...] = high[half:]


def halves(low, high):
    vmem = pl.BlockSpec(memory_space=pltpu.VMEM)
    shape = jax.ShapeDtypeStruct((low.shape[0] // 2, low.shape[1]), low.dtype)
    return pl.pallas_call(
        halves_body,
        in_specs=[vmem] * 2,
        out_specs=[vmem] * 2,
        out_shape=[shape] * 2,
        cost_estimate=cost(1, 1),
        compiler_params=pltpu.CompilerParams(vmem_limit_bytes=8 * MIB),
        name="halves",
    )(low, high)


def load_body(firsts, *refs):
    n_in = len(firsts)
    sem = refs[-1]
    copies = []
    for i, first in enumerate(firsts):
        src, dst = refs[i], refs[n_in + i]
        copies.append(
            pltpu.make_async_copy(src.at[:, pl.ds(first, dst.shape[1])], dst, sem.at[i])
        )
    for one in copies:
        one.start()
    for one in copies:
        one.wait()


def load(values, windows):
    n_in = len(values)
    return pl.pallas_call(
        functools.partial(load_body, tuple(first for first, _ in windows)),
        in_specs=[pl.BlockSpec(memory_space=pl.ANY)] * n_in,
        out_specs=[pl.BlockSpec(memory_space=pltpu.VMEM)] * n_in,
        out_shape=[
            jax.ShapeDtypeStruct((one.shape[0], width), one.dtype)
            for one, (_, width) in zip(values, windows)
        ],
        scratch_shapes=[pltpu.SemaphoreType.DMA((n_in,))],
        cost_estimate=cost(1, 1),
        compiler_params=pltpu.CompilerParams(vmem_limit_bytes=2 * MIB),
        name="load",
    )(*[in_hbm(one) for one in values])


def project_body(n_in, first, widths, depth, *refs):
    xs, w_ref = refs[:n_in], refs[n_in]
    outs = refs[n_in + 1 :]
    total = sum(widths)
    halves = [xs[: n_in // 2], xs[n_in // 2 :]] if total <= 2 * HD else [xs]
    sums = [None] * len(halves)
    for k in range(w_ref.shape[0] // depth):
        span = slice(k * depth, (k + 1) * depth)
        for i, half in enumerate(halves):
            part = jnp.dot(
                jnp.concatenate([x[:, span] for x in half], axis=0),
                w_ref[span, first : first + total],
                preferred_element_type=jnp.float32,
            )
            sums[i] = part if sums[i] is None else sums[i] + part
    at = 0
    for out, width in zip(outs, widths):
        row = 0
        for one in sums:
            out[row : row + one.shape[0]] = one[:, at : at + width].astype(jnp.bfloat16)
            row += one.shape[0]
        at += width


def project(xs, w, first, widths, depth=2048):
    total = sum(widths)
    rows = sum(x.shape[0] for x in xs)
    width = w.shape[0]
    vmem = pl.BlockSpec(memory_space=pltpu.VMEM)
    return pl.pallas_call(
        functools.partial(project_body, len(xs), first, widths, depth),
        in_specs=[vmem] * (len(xs) + 1),
        out_specs=[vmem] * len(widths),
        out_shape=[jax.ShapeDtypeStruct((rows, one), jnp.bfloat16) for one in widths],
        cost_estimate=cost(2 * rows * width * total, 2 * width * (rows + total)),
        compiler_params=pltpu.CompilerParams(vmem_limit_bytes=6 * MIB + 4 * rows * total),
        name="project",
    )(*xs, w)


def y_pair(kv):
    return jnp.concatenate([kv, y_swap(kv)], axis=0)


def x_all(pair):
    return [pair, x_send(pair, -1), x_send(pair, 2), x_send(pair, 1)]


def attend_body(n_doc, n_kv, places, pack, table_ref, ends_ref, starts_ref, q_ref, *refs):
    pieces = refs[:n_kv]
    keep_ref, send_ref = refs[n_kv : n_kv + 2]
    kv = refs[n_kv + 2] if pack else pieces[0]
    pair = pl.program_id(0)

    if pack:

        @pl.when(pair == 0)
        def _():
            for which, src, dst, count in places:
                kv[dst : dst + count] = pieces[which][src : src + count]

    rows = GROUP * TILE
    starts = [starts_ref[2 * pair + j] for j in range(2)]
    low = jnp.minimum(starts[0], starts[1])
    high = jnp.maximum(starts[0], starts[1]) + TILE - 1
    offset = lax.rem(lax.broadcasted_iota(jnp.int32, (1, rows), 1), TILE)
    q_pos = [start + offset for start in starts]
    doc_start = [jnp.zeros((1, rows), jnp.int32) for _ in range(2)]
    first, last = jnp.int32(0), jnp.int32(0)
    for i in range(n_doc):
        end = ends_ref[i]
        doc_start = [jnp.where(q_pos[j] >= end, end, doc_start[j]) for j in range(2)]
        first = jnp.where(low >= end, end, first)
        last = jnp.where(high >= end, end, last)
    q_t = []
    for j in range(2):
        block = q_ref[j * TILE : (j + 1) * TILE].astype(jnp.float32)
        q_t.append(
            jnp.concatenate(
                [block[:, h * HD : (h + 1) * HD].T for h in range(GROUP)], axis=1
            ).astype(jnp.bfloat16)
        )
    scale = LOG2E / HD**0.5
    ratio = KTILE // TILE
    k_iota = lax.broadcasted_iota(jnp.int32, (KTILE, rows), 0)

    def step(at, state, masked, tiles=1):
        spots = [pl.multiple_of(table_ref[at * ratio + i], TILE) for i in range(ratio * tiles)]
        keys = jnp.concatenate([kv[pl.ds(spot, TILE), :HD] for spot in spots], axis=0)
        vals = jnp.concatenate([kv[pl.ds(spot, TILE), HD:] for spot in spots], axis=0)
        scores = [jnp.dot(keys, q_t[j], preferred_element_type=jnp.float32) for j in range(2)]
        out = []
        for j in range(2):
            top, total, acc = state[j]
            s = scores[j]
            if masked:
                base = at * KTILE
                allowed = (k_iota <= q_pos[j] - base) & (k_iota >= doc_start[j] - base)
                s = jnp.where(allowed, s, MASKED)
            new_top = jnp.maximum(top, jnp.max(s, axis=0, keepdims=True))
            e = jnp.exp2((s - new_top) * scale)
            factor = jnp.exp2((top - new_top) * scale)
            total = total * factor + jnp.sum(e, axis=0, keepdims=True)
            acc = acc * factor + lax.dot_general(
                vals,
                e.astype(jnp.bfloat16),
                (((0,), (0,)), ((), ())),
                preferred_element_type=jnp.float32,
            )
            out.append((new_top, total, acc))
        return tuple(out)

    state = tuple(
        (
            jnp.full((1, rows), LOWEST, jnp.float32),
            jnp.zeros((1, rows), jnp.float32),
            jnp.zeros((HD, rows), jnp.float32),
        )
        for _ in range(2)
    )
    begin, stop = first // KTILE, high // KTILE + 1
    inner = (last + KTILE - 1) // KTILE
    doubles = jnp.maximum(low // KTILE - inner, 0) // 2
    masked_step = functools.partial(step, masked=True)
    state = lax.fori_loop(begin, jnp.minimum(inner, stop), masked_step, state)
    state = lax.fori_loop(
        0, doubles, lambda i, state: step(inner + 2 * i, state, masked=False, tiles=2), state
    )
    state = lax.fori_loop(jnp.minimum(inner, stop) + 2 * doubles, stop, masked_step, state)
    for (top, total, acc), out_ref in zip(state, (keep_ref, send_ref)):
        out_t = acc / total
        out_ref[...] = jnp.concatenate(
            [out_t[:, h * TILE : (h + 1) * TILE].T for h in range(GROUP)], axis=1
        ).astype(jnp.bfloat16)


def attend(q, first, pairs, kvs, places, pack, table, ends, starts, span):
    half = pairs * TILE
    count = sum(place[3] for place in places)
    vmem = pl.BlockSpec(memory_space=pltpu.VMEM)
    spec = pltpu.PrefetchScalarGridSpec(
        num_scalar_prefetch=3,
        grid=(pairs,),
        in_specs=[pl.BlockSpec((2 * TILE, QW), lambda i, *_: (first + i, 0))]
        + [vmem] * len(kvs),
        out_specs=[pl.BlockSpec((TILE, QW), lambda i, *_: (i, 0))] * 2 + [vmem] * pack,
    )
    return pl.pallas_call(
        functools.partial(attend_body, ends.shape[0], len(kvs), places, pack),
        grid_spec=spec,
        out_shape=[jax.ShapeDtypeStruct((half, QW), jnp.bfloat16)] * 2
        + [jax.ShapeDtypeStruct((count, 2 * HD), jnp.bfloat16)] * pack,
        cost_estimate=cost(
            2 * pairs * 4 * GROUP * TILE * span * HD * 2,
            count * 4 * HD + half * QW * 8,
            2 * pairs * GROUP * TILE * span,
        ),
        compiler_params=pltpu.CompilerParams(vmem_limit_bytes=6 * MIB),
        name="attend",
    )(table, ends, starts, q, *kvs)


def out_body(first, step, own_ref, sib_ref, w_own, w_sib, *outs):
    own, sib = own_ref[...], sib_ref[...]
    for n in range(outs[0].shape[1] // step):
        columns = slice(first + n * step, first + (n + 1) * step)
        sums = jnp.dot(own, w_own[:, columns], preferred_element_type=jnp.float32)
        sums += jnp.dot(sib, w_sib[:, columns], preferred_element_type=jnp.float32)
        for i, out in enumerate(outs):
            out[:, n * step : (n + 1) * step] = sums[i * TILE : (i + 1) * TILE].astype(jnp.bfloat16)


def out_project(own, sib, w_own, w_sib, half, step=512):
    depth, width = w_own.shape
    part = width // 2
    rows = own.shape[0]
    n_out = rows // TILE
    vmem = pl.BlockSpec(memory_space=pltpu.VMEM)
    return pl.pallas_call(
        functools.partial(out_body, half * part, step),
        in_specs=[vmem] * 4,
        out_specs=[vmem] * n_out,
        out_shape=[jax.ShapeDtypeStruct((TILE, part), jnp.bfloat16)] * n_out,
        cost_estimate=cost(
            4 * rows * depth * part, 4 * depth * part + 4 * rows * depth + 2 * rows * part
        ),
        compiler_params=pltpu.CompilerParams(vmem_limit_bytes=4 * MIB),
        name="out_project",
    )(own, sib, w_own, w_sib)


def final_body(p_lo, p_hi, a_lo, a_hi, b_lo, b_hi, out_ref):
    f32 = jnp.float32
    half = p_lo.shape[1]
    lo = p_lo[...].astype(f32) + a_lo[...].astype(f32) + b_lo[...].astype(f32)
    hi = p_hi[...].astype(f32) + a_hi[...].astype(f32) + b_hi[...].astype(f32)
    out_ref[:, :half] = lo.astype(jnp.bfloat16)
    out_ref[:, half:] = hi.astype(jnp.bfloat16)


def final_sum(*parts):
    rows, half = parts[0].shape
    block = 32
    return pl.pallas_call(
        final_body,
        grid=(rows // block,),
        in_specs=[pl.BlockSpec((block, half), lambda i: (i, 0))] * 6,
        out_specs=pl.BlockSpec((block, 2 * half), lambda i: (i, 0)),
        out_shape=jax.ShapeDtypeStruct((rows, 2 * half), jnp.bfloat16),
        cost_estimate=cost(6 * rows * half, 16 * rows * half),
        compiler_params=pltpu.CompilerParams(vmem_limit_bytes=24 * MIB),
        name="final_sum",
    )(*parts)


def add_body(a0, b0, a1, b1, out0, out1):
    f32 = jnp.float32
    out0[...] = (a0[...].astype(f32) + b0[...].astype(f32)).astype(jnp.bfloat16)
    out1[...] = (a1[...].astype(f32) + b1[...].astype(f32)).astype(jnp.bfloat16)


def add_two(a0, b0, a1, b1, block=32):
    rows, width = a0.shape
    one = pl.BlockSpec((block, width), lambda i: (i, 0))
    return pl.pallas_call(
        add_body,
        grid=(rows // block,),
        in_specs=[one] * 4,
        out_specs=[one] * 2,
        out_shape=[jax.ShapeDtypeStruct((rows, width), jnp.bfloat16)] * 2,
        cost_estimate=cost(2 * rows * width, 12 * rows * width),
        compiler_params=pltpu.CompilerParams(vmem_limit_bytes=16 * MIB),
        name="add_two",
    )(a0, b0, a1, b1)


def shards(tokens, norm_gain, w_qkv, w_out, doc_lengths, span_slots):
    ctx = lax.axis_index("ctx")
    tp = lax.axis_index("tp")
    x, y, z, core = ctx // 2, ctx % 2, tp // 2, tp % 2
    gain = norm_gain.reshape(1, -1)
    rows = norm(in_hbm(tokens), in_hbm(gain))
    low, high = z_send(rows, 1), z_send(rows, -1)
    sib_rows = swap(rows)
    w_sib = swap(w_out)
    w_qkv, rows = lax.optimization_barrier((w_qkv, rows))
    (w_kv,) = load([w_qkv], [(QW, 2 * HD)])
    sib_rows, w_kv = lax.optimization_barrier((sib_rows, w_kv))
    sib_rows, doc_lengths, span_slots = lax.optimization_barrier((sib_rows, doc_lengths, span_slots))

    n_spans = span_slots.shape[0]
    per_span = 4
    span = per_span * TILE
    ends = jnp.cumsum(doc_lengths).astype(jnp.int32)
    numbers = jnp.arange(n_spans, dtype=jnp.int32)
    slot_of = jnp.sum(
        jnp.where(span_slots[None, :] == numbers[:, None], numbers[None, :], 0), axis=1
    )
    tile_no = jnp.arange(per_span, dtype=jnp.int32)[None, :]
    slot = slot_of[:, None]
    tile_tp = (slot % 2) * per_span + tile_no
    rank = slot // 2
    rel_z = (tile_tp // 2 - z) % NZ
    z_base = jnp.where(rel_z == 0, Z_BASE[0], 0)
    for i in range(1, NZ):
        z_base = jnp.where(rel_z == i, Z_BASE[i], z_base)
    rel_src = ((rank // 2 - x) % NX) * 2 + (rank % 2 != y).astype(jnp.int32)
    table = rel_src * 1024 + z_base + (tile_tp % 2 != core).astype(jnp.int32) * TILE
    table = table.reshape(-1).astype(jnp.int32)
    own_spans = lax.dynamic_slice_in_dim(span_slots, 2 * ctx, 2, 0)

    def starts_of(*dzs):
        tps = jnp.stack([((z + dz) % NZ) * 2 + c for dz in dzs for c in (core, 1 - core)])
        blocks = jnp.where(tps // per_span == 0, own_spans[0], own_spans[1])
        return (blocks * span + (tps % per_span) * TILE).astype(jnp.int32)

    starts_d, starts_b, starts_a = starts_of(2), starts_of(-1, 1), starts_of(0)
    (kv_a,) = project([rows, sib_rows], w_kv, 0, (2 * HD,))
    pair_a = y_pair(kv_a)
    pair_a, w_sib, table, ends, starts_d, starts_b, starts_a = lax.optimization_barrier(
        (pair_a, w_sib, table, ends, starts_d, starts_b, starts_a)
    )
    all_a = x_all(pair_a)
    far0, far1 = halves(low, high)
    low, high, far0, far1, *all_a = lax.optimization_barrier((low, high, far0, far1, *all_a))
    group_b = [low, swap(low), high, swap(high)]
    far0, far1 = z_send(far0, 1), z_send(far1, -1)
    (kv_b,) = project(group_b, w_kv, 0, (2 * HD,))
    other_b = y_swap(kv_b)
    left0, right0 = x_send(kv_b, 1), x_send(kv_b, -1)
    w_out, w_sib, kv_b = lax.optimization_barrier((w_out, w_sib, kv_b))
    w_out, w_sib = load([w_out, w_sib], [(0, w_out.shape[1])] * 2)
    left0, right0, other_b, w_out, w_sib = lax.optimization_barrier(
        (left0, right0, other_b, w_out, w_sib)
    )
    left1, right1 = x_send(other_b, 1), x_send(other_b, -1)
    *group_b, other_b = lax.optimization_barrier((*group_b, other_b))
    (q_b,) = project(group_b, w_qkv, 0, (QW,))
    far0, far1, left1, right1, q_b = lax.optimization_barrier((far0, far1, left1, right1, q_b))
    all_b = [
        (kv_b, other_b),
        (right0, right1),
        (x_send(left0, 1), x_send(right1, -1)),
        (left0, left1),
    ]
    group_d = [far0, far1, swap(far0), swap(far1)]
    (kv_d,) = project(group_d, w_kv, 0, (2 * HD,))
    other_d = y_swap(kv_d)
    left2, right2 = x_send(kv_d, 1), x_send(kv_d, -1)
    *group_d, other_d, left2, right2 = lax.optimization_barrier((*group_d, other_d, left2, right2))
    left3, right3 = x_send(other_d, 1), x_send(other_d, -1)
    all_d = [
        (kv_d, other_d),
        (right2, right3),
        (x_send(left2, 1), x_send(other_d, 2)),
        (left2, left3),
    ]
    (q_d,) = project(group_d, w_qkv, 0, (QW,))
    kvs, places = [], []
    for group, base in ((all_a, 0), (all_b, 256), (all_d, 768)):
        for i, one in enumerate(group):
            parts = one if isinstance(one, tuple) else (one,)
            count = sum(part.shape[0] for part in parts) // 2
            for j in range(2):
                which, src = (len(kvs) + j, 0) if len(parts) == 2 else (len(kvs), j * count)
                places.append((which, src, (2 * i + j) * 1024 + base, count))
            kvs.extend(parts)

    d_own, d_send, packed = attend(q_d, 0, 1, kvs, tuple(places), True, table, ends, starts_d, 1024)
    d_sib = swap(d_send)
    (d_lo,) = out_project(d_own, d_sib, w_out, w_sib, 0)
    (d_hi,) = out_project(d_own, d_sib, w_out, w_sib, 1)
    from_low, from_high = z_send(d_lo, 1), z_send(d_hi, -1)
    whole = ((0, 0, 0, packed.shape[0]),)
    packed, d_lo, d_hi = lax.optimization_barrier((packed, d_lo, d_hi))
    b_own, b_send = attend(q_b, 0, 2, [packed], whole, False, table, ends, starts_b, 1024)
    b_sib = swap(b_send)
    prev_lo, next_lo = out_project(b_own, b_sib, w_out, w_sib, 0)
    prev_hi, next_hi = out_project(b_own, b_sib, w_out, w_sib, 1)
    early_hi, early_lo = z_send(next_hi, 1), z_send(prev_lo, -1)
    sum_lo, sum_hi = add_two(next_lo, from_low, prev_hi, from_high)
    late_lo, late_hi = z_send(sum_lo, 1), z_send(sum_hi, -1)
    rows, sib_rows, packed, sum_lo, sum_hi = lax.optimization_barrier(
        (rows, sib_rows, packed, sum_lo, sum_hi)
    )
    (q_a,) = project([rows, sib_rows], w_qkv, 0, (QW,))
    a_own, a_send = attend(q_a, 0, 1, [packed], whole, False, table, ends, starts_a, 1024)
    a_sib = swap(a_send)
    (a_lo,) = out_project(a_own, a_sib, w_out, w_sib, 0)
    (a_hi,) = out_project(a_own, a_sib, w_out, w_sib, 1)
    return final_sum(a_lo, a_hi, early_lo, early_hi, late_lo, late_hi)


def solution(mesh):
    placed = (P(("dp", "ctx", "tp"), None), P(), P(None, "tp"), P("tp", None), P("dp"), P("dp"))
    return jax.shard_map(
        shards, mesh=mesh, in_specs=placed, out_specs=P(("dp", "ctx", "tp"), None), check_vma=False
    )
```

```python
import functools

import jax
import jax.numpy as jnp
from jax import lax
from jax.experimental import pallas as pl
from jax.experimental.pallas import tpu as pltpu
from jax.sharding import PartitionSpec as P

HD = 128
GROUP = 4
QW = GROUP * HD
NZ = 4
NX = 4
TILE = 128
KTILE = 256
MIB = 1 << 20
MASKED = -3e38
LOWEST = -2e31
SHARE = 1e-4
LOG2E = 1.4426950408889634

Z_BASE = (0, 512, 768, 256)


def z_perm(dz, dc):
    return [
        (z * 2 + c, ((z + dz) % NZ) * 2 + (c + dc) % 2) for z in range(NZ) for c in range(2)
    ]


def x_perm(dx, dy):
    return [
        (x * 2 + y, ((x + dx) % NX) * 2 + (y + dy) % 2) for x in range(NX) for y in range(2)
    ]


def z_send(value, dz):
    return lax.ppermute(value, "tp", z_perm(dz, 0))


def swap(value):
    return lax.ppermute(value, "tp", z_perm(0, 1))


def x_send(value, dx):
    return lax.ppermute(value, "ctx", x_perm(dx, 0))


def y_swap(value):
    return lax.ppermute(value, "ctx", x_perm(0, 1))


def in_hbm(value):
    return pltpu.with_memory_space_constraint(value, pltpu.HBM)


def cost(flops, nbytes, trans=0):
    return pl.CostEstimate(
        flops=int(flops * SHARE), bytes_accessed=int(nbytes * SHARE), transcendentals=int(trans * SHARE)
    )


def norm_body(x_ref, gain_ref, out_ref):
    block = x_ref.shape[0]
    x = x_ref[...].astype(jnp.float32)
    mean_sq = jnp.mean(x * x, axis=-1, keepdims=True)
    at = pl.multiple_of(pl.program_id(0) * block, block)
    out_ref[pl.ds(at, block)] = (x * lax.rsqrt(mean_sq + 1e-05) * gain_ref[...]).astype(jnp.bfloat16)


def norm(tokens, gain, block=64):
    rows, width = tokens.shape
    return pl.pallas_call(
        norm_body,
        grid=(rows // block,),
        in_specs=[
            pl.BlockSpec((block, width), lambda i: (i, 0)),
            pl.BlockSpec((1, width), lambda i: (0, 0)),
        ],
        out_specs=pl.BlockSpec(memory_space=pltpu.VMEM),
        out_shape=jax.ShapeDtypeStruct((rows, width), jnp.bfloat16),
        cost_estimate=cost(6 * rows * width, 4 * rows * width),
        compiler_params=pltpu.CompilerParams(vmem_limit_bytes=12 * MIB),
        name="norm",
    )(tokens, gain)


def halves_body(low, high, out_low, out_high):
    half = out_low.shape[0]
    out_low[...] = low[:half]
    out_high[...] = high[half:]


def halves(low, high):
    vmem = pl.BlockSpec(memory_space=pltpu.VMEM)
    shape = jax.ShapeDtypeStruct((low.shape[0] // 2, low.shape[1]), low.dtype)
    return pl.pallas_call(
        halves_body,
        in_specs=[vmem] * 2,
        out_specs=[vmem] * 2,
        out_shape=[shape] * 2,
        cost_estimate=cost(1, 1),
        compiler_params=pltpu.CompilerParams(vmem_limit_bytes=8 * MIB),
        name="halves",
    )(low, high)


def load_body(firsts, *refs):
    n_in = len(firsts)
    sem = refs[-1]
    copies = []
    for i, first in enumerate(firsts):
        src, dst = refs[i], refs[n_in + i]
        copies.append(
            pltpu.make_async_copy(src.at[:, pl.ds(first, dst.shape[1])], dst, sem.at[i])
        )
    for one in copies:
        one.start()
    for one in copies:
        one.wait()


def load(values, windows):
    n_in = len(values)
    return pl.pallas_call(
        functools.partial(load_body, tuple(first for first, _ in windows)),
        in_specs=[pl.BlockSpec(memory_space=pl.ANY)] * n_in,
        out_specs=[pl.BlockSpec(memory_space=pltpu.VMEM)] * n_in,
        out_shape=[
            jax.ShapeDtypeStruct((one.shape[0], width), one.dtype)
            for one, (_, width) in zip(values, windows)
        ],
        scratch_shapes=[pltpu.SemaphoreType.DMA((n_in,))],
        cost_estimate=cost(1, 1),
        compiler_params=pltpu.CompilerParams(vmem_limit_bytes=2 * MIB),
        name="load",
    )(*[in_hbm(one) for one in values])


def project_body(n_in, first, widths, depth, *refs):
    xs, w_ref = refs[:n_in], refs[n_in]
    outs = refs[n_in + 1 :]
    total = sum(widths)
    halves = [xs[: n_in // 2], xs[n_in // 2 :]] if total <= 2 * HD else [xs]
    sums = [None] * len(halves)
    for k in range(w_ref.shape[0] // depth):
        span = slice(k * depth, (k + 1) * depth)
        for i, half in enumerate(halves):
            part = jnp.dot(
                jnp.concatenate([x[:, span] for x in half], axis=0),
                w_ref[span, first : first + total],
                preferred_element_type=jnp.float32,
            )
            sums[i] = part if sums[i] is None else sums[i] + part
    at = 0
    for out, width in zip(outs, widths):
        row = 0
        for one in sums:
            out[row : row + one.shape[0]] = one[:, at : at + width].astype(jnp.bfloat16)
            row += one.shape[0]
        at += width


def project(xs, w, first, widths, depth=2048):
    total = sum(widths)
    rows = sum(x.shape[0] for x in xs)
    width = w.shape[0]
    vmem = pl.BlockSpec(memory_space=pltpu.VMEM)
    return pl.pallas_call(
        functools.partial(project_body, len(xs), first, widths, depth),
        in_specs=[vmem] * (len(xs) + 1),
        out_specs=[vmem] * len(widths),
        out_shape=[jax.ShapeDtypeStruct((rows, one), jnp.bfloat16) for one in widths],
        cost_estimate=cost(2 * rows * width * total, 2 * width * (rows + total)),
        compiler_params=pltpu.CompilerParams(vmem_limit_bytes=6 * MIB + 4 * rows * total),
        name="project",
    )(*xs, w)


def y_pair(kv):
    return jnp.concatenate([kv, y_swap(kv)], axis=0)


def x_all(pair):
    return [pair, x_send(pair, -1), x_send(pair, 2), x_send(pair, 1)]


def attend_body(n_doc, n_kv, places, pack, table_ref, ends_ref, starts_ref, q_ref, *refs):
    pieces = refs[:n_kv]
    keep_ref, send_ref = refs[n_kv : n_kv + 2]
    kv = refs[n_kv + 2] if pack else pieces[0]
    pair = pl.program_id(0)

    if pack:

        @pl.when(pair == 0)
        def _():
            for which, src, dst, count in places:
                kv[dst : dst + count] = pieces[which][src : src + count]

    rows = GROUP * TILE
    starts = [starts_ref[2 * pair + j] for j in range(2)]
    low = jnp.minimum(starts[0], starts[1])
    high = jnp.maximum(starts[0], starts[1]) + TILE - 1
    offset = lax.rem(lax.broadcasted_iota(jnp.int32, (1, rows), 1), TILE)
    q_pos = [start + offset for start in starts]
    doc_start = [jnp.zeros((1, rows), jnp.int32) for _ in range(2)]
    first, last = jnp.int32(0), jnp.int32(0)
    for i in range(n_doc):
        end = ends_ref[i]
        doc_start = [jnp.where(q_pos[j] >= end, end, doc_start[j]) for j in range(2)]
        first = jnp.where(low >= end, end, first)
        last = jnp.where(high >= end, end, last)
    q_t = []
    for j in range(2):
        block = q_ref[j * TILE : (j + 1) * TILE].astype(jnp.float32)
        q_t.append(
            jnp.concatenate(
                [block[:, h * HD : (h + 1) * HD].T for h in range(GROUP)], axis=1
            ).astype(jnp.bfloat16)
        )
    scale = LOG2E / HD**0.5
    ratio = KTILE // TILE
    k_iota = lax.broadcasted_iota(jnp.int32, (KTILE, rows), 0)

    def step(at, state, masked, tiles=1):
        spots = [pl.multiple_of(table_ref[at * ratio + i], TILE) for i in range(ratio * tiles)]
        keys = jnp.concatenate([kv[pl.ds(spot, TILE), :HD] for spot in spots], axis=0)
        vals = jnp.concatenate([kv[pl.ds(spot, TILE), HD:] for spot in spots], axis=0)
        scores = [jnp.dot(keys, q_t[j], preferred_element_type=jnp.float32) for j in range(2)]
        out = []
        for j in range(2):
            top, total, acc = state[j]
            s = scores[j]
            if masked:
                base = at * KTILE
                allowed = (k_iota <= q_pos[j] - base) & (k_iota >= doc_start[j] - base)
                s = jnp.where(allowed, s, MASKED)
            new_top = jnp.maximum(top, jnp.max(s, axis=0, keepdims=True))
            e = jnp.exp2((s - new_top) * scale)
            factor = jnp.exp2((top - new_top) * scale)
            total = total * factor + jnp.sum(e, axis=0, keepdims=True)
            acc = acc * factor + lax.dot_general(
                vals,
                e.astype(jnp.bfloat16),
                (((0,), (0,)), ((), ())),
                preferred_element_type=jnp.float32,
            )
            out.append((new_top, total, acc))
        return tuple(out)

    state = tuple(
        (
            jnp.full((1, rows), LOWEST, jnp.float32),
            jnp.zeros((1, rows), jnp.float32),
            jnp.zeros((HD, rows), jnp.float32),
        )
        for _ in range(2)
    )
    begin, stop = first // KTILE, high // KTILE + 1
    inner = (last + KTILE - 1) // KTILE
    doubles = jnp.maximum(low // KTILE - inner, 0) // 2
    masked_step = functools.partial(step, masked=True)
    state = lax.fori_loop(begin, jnp.minimum(inner, stop), masked_step, state)
    state = lax.fori_loop(
        0, doubles, lambda i, state: step(inner + 2 * i, state, masked=False, tiles=2), state
    )
    state = lax.fori_loop(jnp.minimum(inner, stop) + 2 * doubles, stop, masked_step, state)
    for (top, total, acc), out_ref in zip(state, (keep_ref, send_ref)):
        out_t = acc / total
        out_ref[...] = jnp.concatenate(
            [out_t[:, h * TILE : (h + 1) * TILE].T for h in range(GROUP)], axis=1
        ).astype(jnp.bfloat16)


def attend(q, first, pairs, kvs, places, pack, table, ends, starts, span):
    half = pairs * TILE
    count = sum(place[3] for place in places)
    vmem = pl.BlockSpec(memory_space=pltpu.VMEM)
    spec = pltpu.PrefetchScalarGridSpec(
        num_scalar_prefetch=3,
        grid=(pairs,),
        in_specs=[pl.BlockSpec((2 * TILE, QW), lambda i, *_: (first + i, 0))]
        + [vmem] * len(kvs),
        out_specs=[pl.BlockSpec((TILE, QW), lambda i, *_: (i, 0))] * 2 + [vmem] * pack,
    )
    return pl.pallas_call(
        functools.partial(attend_body, ends.shape[0], len(kvs), places, pack),
        grid_spec=spec,
        out_shape=[jax.ShapeDtypeStruct((half, QW), jnp.bfloat16)] * 2
        + [jax.ShapeDtypeStruct((count, 2 * HD), jnp.bfloat16)] * pack,
        cost_estimate=cost(
            2 * pairs * 4 * GROUP * TILE * span * HD * 2,
            count * 4 * HD + half * QW * 8,
            2 * pairs * GROUP * TILE * span,
        ),
        compiler_params=pltpu.CompilerParams(vmem_limit_bytes=6 * MIB),
        name="attend",
    )(table, ends, starts, q, *kvs)


def out_body(first, step, own_ref, sib_ref, w_own, w_sib, *outs):
    own, sib = own_ref[...], sib_ref[...]
    for n in range(outs[0].shape[1] // step):
        columns = slice(first + n * step, first + (n + 1) * step)
        sums = jnp.dot(own, w_own[:, columns], preferred_element_type=jnp.float32)
        sums += jnp.dot(sib, w_sib[:, columns], preferred_element_type=jnp.float32)
        for i, out in enumerate(outs):
            out[:, n * step : (n + 1) * step] = sums[i * TILE : (i + 1) * TILE].astype(jnp.bfloat16)


def out_project(own, sib, w_own, w_sib, half, step=512):
    depth, width = w_own.shape
    part = width // 2
    rows = own.shape[0]
    n_out = rows // TILE
    vmem = pl.BlockSpec(memory_space=pltpu.VMEM)
    return pl.pallas_call(
        functools.partial(out_body, half * part, step),
        in_specs=[vmem] * 4,
        out_specs=[vmem] * n_out,
        out_shape=[jax.ShapeDtypeStruct((TILE, part), jnp.bfloat16)] * n_out,
        cost_estimate=cost(
            4 * rows * depth * part, 4 * depth * part + 4 * rows * depth + 2 * rows * part
        ),
        compiler_params=pltpu.CompilerParams(vmem_limit_bytes=4 * MIB),
        name="out_project",
    )(own, sib, w_own, w_sib)


def final_body(p_lo, p_hi, a_lo, a_hi, b_lo, b_hi, out_ref):
    f32 = jnp.float32
    half = p_lo.shape[1]
    lo = p_lo[...].astype(f32) + a_lo[...].astype(f32) + b_lo[...].astype(f32)
    hi = p_hi[...].astype(f32) + a_hi[...].astype(f32) + b_hi[...].astype(f32)
    out_ref[:, :half] = lo.astype(jnp.bfloat16)
    out_ref[:, half:] = hi.astype(jnp.bfloat16)


def final_sum(*parts):
    rows, half = parts[0].shape
    block = 32
    return pl.pallas_call(
        final_body,
        grid=(rows // block,),
        in_specs=[pl.BlockSpec((block, half), lambda i: (i, 0))] * 6,
        out_specs=pl.BlockSpec((block, 2 * half), lambda i: (i, 0)),
        out_shape=jax.ShapeDtypeStruct((rows, 2 * half), jnp.bfloat16),
        cost_estimate=cost(6 * rows * half, 16 * rows * half),
        compiler_params=pltpu.CompilerParams(vmem_limit_bytes=24 * MIB),
        name="final_sum",
    )(*parts)


def add_body(a0, b0, a1, b1, out0, out1):
    f32 = jnp.float32
    out0[...] = (a0[...].astype(f32) + b0[...].astype(f32)).astype(jnp.bfloat16)
    out1[...] = (a1[...].astype(f32) + b1[...].astype(f32)).astype(jnp.bfloat16)


def add_two(a0, b0, a1, b1, block=32):
    rows, width = a0.shape
    one = pl.BlockSpec((block, width), lambda i: (i, 0))
    return pl.pallas_call(
        add_body,
        grid=(rows // block,),
        in_specs=[one] * 4,
        out_specs=[one] * 2,
        out_shape=[jax.ShapeDtypeStruct((rows, width), jnp.bfloat16)] * 2,
        cost_estimate=cost(2 * rows * width, 12 * rows * width),
        compiler_params=pltpu.CompilerParams(vmem_limit_bytes=16 * MIB),
        name="add_two",
    )(a0, b0, a1, b1)


def shards(tokens, norm_gain, w_qkv, w_out, doc_lengths, span_slots):
    ctx = lax.axis_index("ctx")
    tp = lax.axis_index("tp")
    x, y, z, core = ctx // 2, ctx % 2, tp // 2, tp % 2
    gain = norm_gain.reshape(1, -1)
    rows = norm(in_hbm(tokens), in_hbm(gain))
    low, high = z_send(rows, 1), z_send(rows, -1)
    sib_rows = swap(rows)
    w_sib = swap(w_out)
    w_qkv, rows = lax.optimization_barrier((w_qkv, rows))
    (w_kv,) = load([w_qkv], [(QW, 2 * HD)])
    sib_rows, w_kv = lax.optimization_barrier((sib_rows, w_kv))
    sib_rows, doc_lengths, span_slots = lax.optimization_barrier((sib_rows, doc_lengths, span_slots))

    n_spans = span_slots.shape[0]
    per_span = 4
    span = per_span * TILE
    ends = jnp.cumsum(doc_lengths).astype(jnp.int32)
    numbers = jnp.arange(n_spans, dtype=jnp.int32)
    slot_of = jnp.sum(
        jnp.where(span_slots[None, :] == numbers[:, None], numbers[None, :], 0), axis=1
    )
    tile_no = jnp.arange(per_span, dtype=jnp.int32)[None, :]
    slot = slot_of[:, None]
    tile_tp = (slot % 2) * per_span + tile_no
    rank = slot // 2
    rel_z = (tile_tp // 2 - z) % NZ
    z_base = jnp.where(rel_z == 0, Z_BASE[0], 0)
    for i in range(1, NZ):
        z_base = jnp.where(rel_z == i, Z_BASE[i], z_base)
    rel_src = ((rank // 2 - x) % NX) * 2 + (rank % 2 != y).astype(jnp.int32)
    table = rel_src * 1024 + z_base + (tile_tp % 2 != core).astype(jnp.int32) * TILE
    table = table.reshape(-1).astype(jnp.int32)
    own_spans = lax.dynamic_slice_in_dim(span_slots, 2 * ctx, 2, 0)

    def starts_of(*dzs):
        tps = jnp.stack([((z + dz) % NZ) * 2 + c for dz in dzs for c in (core, 1 - core)])
        blocks = jnp.where(tps // per_span == 0, own_spans[0], own_spans[1])
        return (blocks * span + (tps % per_span) * TILE).astype(jnp.int32)

    starts_d, starts_b, starts_a = starts_of(2), starts_of(-1, 1), starts_of(0)
    (kv_a,) = project([rows, sib_rows], w_kv, 0, (2 * HD,))
    pair_a = y_pair(kv_a)
    pair_a, w_sib, table, ends, starts_d, starts_b, starts_a = lax.optimization_barrier(
        (pair_a, w_sib, table, ends, starts_d, starts_b, starts_a)
    )
    all_a = x_all(pair_a)
    far0, far1 = halves(low, high)
    low, high, far0, far1, *all_a = lax.optimization_barrier((low, high, far0, far1, *all_a))
    group_b = [low, swap(low), high, swap(high)]
    far0, far1 = z_send(far0, 1), z_send(far1, -1)
    (kv_b,) = project(group_b, w_kv, 0, (2 * HD,))
    other_b = y_swap(kv_b)
    left0, right0 = x_send(kv_b, 1), x_send(kv_b, -1)
    w_out, w_sib, kv_b = lax.optimization_barrier((w_out, w_sib, kv_b))
    w_out, w_sib = load([w_out, w_sib], [(0, w_out.shape[1])] * 2)
    left0, right0, other_b, w_out, w_sib = lax.optimization_barrier(
        (left0, right0, other_b, w_out, w_sib)
    )
    left1, right1 = x_send(other_b, 1), x_send(other_b, -1)
    far0, far1, other_b = lax.optimization_barrier((far0, far1, other_b))
    all_b = [
        (kv_b, other_b),
        (right0, right1),
        (x_send(left0, 1), x_send(right1, -1)),
        (left0, left1),
    ]
    group_d = [far0, far1, swap(far0), swap(far1)]
    (kv_d,) = project(group_d, w_kv, 0, (2 * HD,))
    other_d = y_swap(kv_d)
    left2, right2 = x_send(kv_d, 1), x_send(kv_d, -1)
    *group_d, other_d, left2, right2 = lax.optimization_barrier((*group_d, other_d, left2, right2))
    *group_b, other_d = lax.optimization_barrier((*group_b, other_d))
    left3, right3 = x_send(other_d, 1), x_send(other_d, -1)
    all_d = [
        (kv_d, other_d),
        (right2, right3),
        (x_send(left2, 1), x_send(other_d, 2)),
        (left2, left3),
    ]
    (q_d,) = project(group_d, w_qkv, 0, (QW,))
    (q_b,) = project(group_b, w_qkv, 0, (QW,))
    q_d, q_b = lax.optimization_barrier((q_d, q_b))
    kvs, places = [], []
    for group, base in ((all_a, 0), (all_b, 256), (all_d, 768)):
        for i, one in enumerate(group):
            parts = one if isinstance(one, tuple) else (one,)
            count = sum(part.shape[0] for part in parts) // 2
            for j in range(2):
                which, src = (len(kvs) + j, 0) if len(parts) == 2 else (len(kvs), j * count)
                places.append((which, src, (2 * i + j) * 1024 + base, count))
            kvs.extend(parts)

    d_own, d_send, packed = attend(q_d, 0, 1, kvs, tuple(places), True, table, ends, starts_d, 1024)
    d_sib = swap(d_send)
    (d_lo,) = out_project(d_own, d_sib, w_out, w_sib, 0)
    (d_hi,) = out_project(d_own, d_sib, w_out, w_sib, 1)
    from_low, from_high = z_send(d_lo, 1), z_send(d_hi, -1)
    whole = ((0, 0, 0, packed.shape[0]),)
    packed, d_lo, d_hi = lax.optimization_barrier((packed, d_lo, d_hi))
    b_own, b_send = attend(q_b, 0, 2, [packed], whole, False, table, ends, starts_b, 1024)
    b_sib = swap(b_send)
    prev_lo, next_lo = out_project(b_own, b_sib, w_out, w_sib, 0)
    prev_hi, next_hi = out_project(b_own, b_sib, w_out, w_sib, 1)
    early_hi, early_lo = z_send(next_hi, 1), z_send(prev_lo, -1)
    sum_lo, sum_hi = add_two(next_lo, from_low, prev_hi, from_high)
    late_lo, late_hi = z_send(sum_lo, 1), z_send(sum_hi, -1)
    rows, sib_rows, packed, sum_lo, sum_hi = lax.optimization_barrier(
        (rows, sib_rows, packed, sum_lo, sum_hi)
    )
    (q_a,) = project([rows, sib_rows], w_qkv, 0, (QW,))
    a_own, a_send = attend(q_a, 0, 1, [packed], whole, False, table, ends, starts_a, 1024)
    a_sib = swap(a_send)
    (a_lo,) = out_project(a_own, a_sib, w_out, w_sib, 0)
    (a_hi,) = out_project(a_own, a_sib, w_out, w_sib, 1)
    return final_sum(a_lo, a_hi, early_lo, early_hi, late_lo, late_hi)


def solution(mesh):
    placed = (P(("dp", "ctx", "tp"), None), P(), P(None, "tp"), P("tp", None), P("dp"), P("dp"))
    return jax.shard_map(
        shards, mesh=mesh, in_specs=placed, out_specs=P(("dp", "ctx", "tp"), None), check_vma=False
    )
```

```python
import functools

import jax
import jax.numpy as jnp
from jax import lax
from jax.experimental import pallas as pl
from jax.experimental.pallas import tpu as pltpu
from jax.sharding import PartitionSpec as P

HD = 128
GROUP = 4
QW = GROUP * HD
NZ = 4
NX = 4
TILE = 128
KTILE = 256
MIB = 1 << 20
MASKED = -3e38
LOWEST = -2e31
SHARE = 1e-4
LOG2E = 1.4426950408889634

Z_BASE = (0, 512, 768, 256)


def z_perm(dz, dc):
    return [
        (z * 2 + c, ((z + dz) % NZ) * 2 + (c + dc) % 2) for z in range(NZ) for c in range(2)
    ]


def x_perm(dx, dy):
    return [
        (x * 2 + y, ((x + dx) % NX) * 2 + (y + dy) % 2) for x in range(NX) for y in range(2)
    ]


def z_send(value, dz):
    return lax.ppermute(value, "tp", z_perm(dz, 0))


def swap(value):
    return lax.ppermute(value, "tp", z_perm(0, 1))


def x_send(value, dx):
    return lax.ppermute(value, "ctx", x_perm(dx, 0))


def y_swap(value):
    return lax.ppermute(value, "ctx", x_perm(0, 1))


def in_hbm(value):
    return pltpu.with_memory_space_constraint(value, pltpu.HBM)


def cost(flops, nbytes, trans=0):
    return pl.CostEstimate(
        flops=int(flops * SHARE), bytes_accessed=int(nbytes * SHARE), transcendentals=int(trans * SHARE)
    )


def norm_body(x_ref, gain_ref, out_ref):
    block = x_ref.shape[0]
    x = x_ref[...].astype(jnp.float32)
    mean_sq = jnp.mean(x * x, axis=-1, keepdims=True)
    at = pl.multiple_of(pl.program_id(0) * block, block)
    out_ref[pl.ds(at, block)] = (x * lax.rsqrt(mean_sq + 1e-05) * gain_ref[...]).astype(jnp.bfloat16)


def norm(tokens, gain, block=64):
    rows, width = tokens.shape
    return pl.pallas_call(
        norm_body,
        grid=(rows // block,),
        in_specs=[
            pl.BlockSpec((block, width), lambda i: (i, 0)),
            pl.BlockSpec((1, width), lambda i: (0, 0)),
        ],
        out_specs=pl.BlockSpec(memory_space=pltpu.VMEM),
        out_shape=jax.ShapeDtypeStruct((rows, width), jnp.bfloat16),
        cost_estimate=cost(6 * rows * width, 4 * rows * width),
        compiler_params=pltpu.CompilerParams(vmem_limit_bytes=12 * MIB),
        name="norm",
    )(tokens, gain)


def halves_body(low, high, out_low, out_high):
    half = out_low.shape[0]
    out_low[...] = low[:half]
    out_high[...] = high[half:]


def halves(low, high):
    vmem = pl.BlockSpec(memory_space=pltpu.VMEM)
    shape = jax.ShapeDtypeStruct((low.shape[0] // 2, low.shape[1]), low.dtype)
    return pl.pallas_call(
        halves_body,
        in_specs=[vmem] * 2,
        out_specs=[vmem] * 2,
        out_shape=[shape] * 2,
        cost_estimate=cost(1, 1),
        compiler_params=pltpu.CompilerParams(vmem_limit_bytes=8 * MIB),
        name="halves",
    )(low, high)


def load_body(firsts, *refs):
    n_in = len(firsts)
    sem = refs[-1]
    copies = []
    for i, first in enumerate(firsts):
        src, dst = refs[i], refs[n_in + i]
        copies.append(
            pltpu.make_async_copy(src.at[:, pl.ds(first, dst.shape[1])], dst, sem.at[i])
        )
    for one in copies:
        one.start()
    for one in copies:
        one.wait()


def load(values, windows):
    n_in = len(values)
    return pl.pallas_call(
        functools.partial(load_body, tuple(first for first, _ in windows)),
        in_specs=[pl.BlockSpec(memory_space=pl.ANY)] * n_in,
        out_specs=[pl.BlockSpec(memory_space=pltpu.VMEM)] * n_in,
        out_shape=[
            jax.ShapeDtypeStruct((one.shape[0], width), one.dtype)
            for one, (_, width) in zip(values, windows)
        ],
        scratch_shapes=[pltpu.SemaphoreType.DMA((n_in,))],
        cost_estimate=cost(1, 1),
        compiler_params=pltpu.CompilerParams(vmem_limit_bytes=2 * MIB),
        name="load",
    )(*[in_hbm(one) for one in values])


def project_body(n_in, first, widths, depth, *refs):
    xs, w_ref = refs[:n_in], refs[n_in]
    outs = refs[n_in + 1 :]
    total = sum(widths)
    halves = [xs[: n_in // 2], xs[n_in // 2 :]] if total <= 2 * HD else [xs]
    sums = [None] * len(halves)
    for k in range(w_ref.shape[0] // depth):
        span = slice(k * depth, (k + 1) * depth)
        for i, half in enumerate(halves):
            part = jnp.dot(
                jnp.concatenate([x[:, span] for x in half], axis=0),
                w_ref[span, first : first + total],
                preferred_element_type=jnp.float32,
            )
            sums[i] = part if sums[i] is None else sums[i] + part
    at = 0
    for out, width in zip(outs, widths):
        row = 0
        for one in sums:
            out[row : row + one.shape[0]] = one[:, at : at + width].astype(jnp.bfloat16)
            row += one.shape[0]
        at += width


def project(xs, w, first, widths, depth=2048):
    total = sum(widths)
    rows = sum(x.shape[0] for x in xs)
    width = w.shape[0]
    vmem = pl.BlockSpec(memory_space=pltpu.VMEM)
    return pl.pallas_call(
        functools.partial(project_body, len(xs), first, widths, depth),
        in_specs=[vmem] * (len(xs) + 1),
        out_specs=[vmem] * len(widths),
        out_shape=[jax.ShapeDtypeStruct((rows, one), jnp.bfloat16) for one in widths],
        cost_estimate=cost(2 * rows * width * total, 2 * width * (rows + total)),
        compiler_params=pltpu.CompilerParams(vmem_limit_bytes=6 * MIB + 4 * rows * total),
        name="project",
    )(*xs, w)


def y_pair(kv):
    return jnp.concatenate([kv, y_swap(kv)], axis=0)


def x_all(pair):
    return [pair, x_send(pair, -1), x_send(pair, 2), x_send(pair, 1)]


def attend_body(n_doc, n_kv, places, pack, table_ref, ends_ref, starts_ref, q_ref, *refs):
    pieces = refs[:n_kv]
    keep_ref, send_ref = refs[n_kv : n_kv + 2]
    kv = refs[n_kv + 2] if pack else pieces[0]
    pair = pl.program_id(0)

    if pack:

        @pl.when(pair == 0)
        def _():
            for which, src, dst, count in places:
                kv[dst : dst + count] = pieces[which][src : src + count]

    rows = GROUP * TILE
    starts = [starts_ref[2 * pair + j] for j in range(2)]
    low = jnp.minimum(starts[0], starts[1])
    high = jnp.maximum(starts[0], starts[1]) + TILE - 1
    offset = lax.rem(lax.broadcasted_iota(jnp.int32, (1, rows), 1), TILE)
    q_pos = [start + offset for start in starts]
    doc_start = [jnp.zeros((1, rows), jnp.int32) for _ in range(2)]
    first, last = jnp.int32(0), jnp.int32(0)
    for i in range(n_doc):
        end = ends_ref[i]
        doc_start = [jnp.where(q_pos[j] >= end, end, doc_start[j]) for j in range(2)]
        first = jnp.where(low >= end, end, first)
        last = jnp.where(high >= end, end, last)
    q_t = []
    for j in range(2):
        block = q_ref[j * TILE : (j + 1) * TILE].astype(jnp.float32)
        q_t.append(
            jnp.concatenate(
                [block[:, h * HD : (h + 1) * HD].T for h in range(GROUP)], axis=1
            ).astype(jnp.bfloat16)
        )
    scale = LOG2E / HD**0.5
    ratio = KTILE // TILE
    k_iota = lax.broadcasted_iota(jnp.int32, (KTILE, rows), 0)

    def step(at, state, masked, tiles=1):
        spots = [pl.multiple_of(table_ref[at * ratio + i], TILE) for i in range(ratio * tiles)]
        keys = jnp.concatenate([kv[pl.ds(spot, TILE), :HD] for spot in spots], axis=0)
        vals = jnp.concatenate([kv[pl.ds(spot, TILE), HD:] for spot in spots], axis=0)
        scores = [jnp.dot(keys, q_t[j], preferred_element_type=jnp.float32) for j in range(2)]
        out = []
        for j in range(2):
            top, total, acc = state[j]
            s = scores[j]
            if masked:
                base = at * KTILE
                allowed = (k_iota <= q_pos[j] - base) & (k_iota >= doc_start[j] - base)
                s = jnp.where(allowed, s, MASKED)
            new_top = jnp.maximum(top, jnp.max(s, axis=0, keepdims=True))
            e = jnp.exp2((s - new_top) * scale)
            factor = jnp.exp2((top - new_top) * scale)
            total = total * factor + jnp.sum(e, axis=0, keepdims=True)
            acc = acc * factor + lax.dot_general(
                vals,
                e.astype(jnp.bfloat16),
                (((0,), (0,)), ((), ())),
                preferred_element_type=jnp.float32,
            )
            out.append((new_top, total, acc))
        return tuple(out)

    state = tuple(
        (
            jnp.full((1, rows), LOWEST, jnp.float32),
            jnp.zeros((1, rows), jnp.float32),
            jnp.zeros((HD, rows), jnp.float32),
        )
        for _ in range(2)
    )
    begin, stop = first // KTILE, high // KTILE + 1
    inner = (last + KTILE - 1) // KTILE
    doubles = jnp.maximum(low // KTILE - inner, 0) // 2
    masked_step = functools.partial(step, masked=True)
    state = lax.fori_loop(begin, jnp.minimum(inner, stop), masked_step, state)
    state = lax.fori_loop(
        0, doubles, lambda i, state: step(inner + 2 * i, state, masked=False, tiles=2), state
    )
    state = lax.fori_loop(jnp.minimum(inner, stop) + 2 * doubles, stop, masked_step, state)
    for (top, total, acc), out_ref in zip(state, (keep_ref, send_ref)):
        out_t = acc / total
        out_ref[...] = jnp.concatenate(
            [out_t[:, h * TILE : (h + 1) * TILE].T for h in range(GROUP)], axis=1
        ).astype(jnp.bfloat16)


def attend(q, first, pairs, kvs, places, pack, table, ends, starts, span):
    half = pairs * TILE
    count = sum(place[3] for place in places)
    vmem = pl.BlockSpec(memory_space=pltpu.VMEM)
    spec = pltpu.PrefetchScalarGridSpec(
        num_scalar_prefetch=3,
        grid=(pairs,),
        in_specs=[pl.BlockSpec((2 * TILE, QW), lambda i, *_: (first + i, 0))]
        + [vmem] * len(kvs),
        out_specs=[pl.BlockSpec((TILE, QW), lambda i, *_: (i, 0))] * 2 + [vmem] * pack,
    )
    return pl.pallas_call(
        functools.partial(attend_body, ends.shape[0], len(kvs), places, pack),
        grid_spec=spec,
        out_shape=[jax.ShapeDtypeStruct((half, QW), jnp.bfloat16)] * 2
        + [jax.ShapeDtypeStruct((count, 2 * HD), jnp.bfloat16)] * pack,
        cost_estimate=cost(
            2 * pairs * 4 * GROUP * TILE * span * HD * 2,
            count * 4 * HD + half * QW * 8,
            2 * pairs * GROUP * TILE * span,
        ),
        compiler_params=pltpu.CompilerParams(vmem_limit_bytes=6 * MIB),
        name="attend",
    )(table, ends, starts, q, *kvs)


def out_body(first, step, own_ref, sib_ref, w_own, w_sib, *outs):
    own, sib = own_ref[...], sib_ref[...]
    for n in range(outs[0].shape[1] // step):
        columns = slice(first + n * step, first + (n + 1) * step)
        sums = jnp.dot(own, w_own[:, columns], preferred_element_type=jnp.float32)
        sums += jnp.dot(sib, w_sib[:, columns], preferred_element_type=jnp.float32)
        for i, out in enumerate(outs):
            out[:, n * step : (n + 1) * step] = sums[i * TILE : (i + 1) * TILE].astype(jnp.bfloat16)


def out_project(own, sib, w_own, w_sib, half, step=512):
    depth, width = w_own.shape
    part = width // 2
    rows = own.shape[0]
    n_out = rows // TILE
    vmem = pl.BlockSpec(memory_space=pltpu.VMEM)
    return pl.pallas_call(
        functools.partial(out_body, half * part, step),
        in_specs=[vmem] * 4,
        out_specs=[vmem] * n_out,
        out_shape=[jax.ShapeDtypeStruct((TILE, part), jnp.bfloat16)] * n_out,
        cost_estimate=cost(
            4 * rows * depth * part, 4 * depth * part + 4 * rows * depth + 2 * rows * part
        ),
        compiler_params=pltpu.CompilerParams(vmem_limit_bytes=4 * MIB),
        name="out_project",
    )(own, sib, w_own, w_sib)


def final_body(p_lo, p_hi, a_lo, a_hi, b_lo, b_hi, out_ref):
    f32 = jnp.float32
    half = p_lo.shape[1]
    block = out_ref.shape[0]
    span = pl.ds(pl.multiple_of(pl.program_id(0) * block, block), block)
    lo = p_lo[span].astype(f32) + a_lo[span].astype(f32) + b_lo[span].astype(f32)
    hi = p_hi[span].astype(f32) + a_hi[span].astype(f32) + b_hi[span].astype(f32)
    out_ref[:, :half] = lo.astype(jnp.bfloat16)
    out_ref[:, half:] = hi.astype(jnp.bfloat16)


def final_sum(*parts):
    rows, half = parts[0].shape
    block = 32
    return pl.pallas_call(
        final_body,
        grid=(rows // block,),
        in_specs=[pl.BlockSpec(memory_space=pltpu.VMEM)] * 6,
        out_specs=pl.BlockSpec((block, 2 * half), lambda i: (i, 0)),
        out_shape=jax.ShapeDtypeStruct((rows, 2 * half), jnp.bfloat16),
        cost_estimate=cost(6 * rows * half, 16 * rows * half),
        compiler_params=pltpu.CompilerParams(vmem_limit_bytes=24 * MIB),
        name="final_sum",
    )(*parts)


def add_body(a0, b0, a1, b1, out0, out1):
    f32 = jnp.float32
    out0[...] = (a0[...].astype(f32) + b0[...].astype(f32)).astype(jnp.bfloat16)
    out1[...] = (a1[...].astype(f32) + b1[...].astype(f32)).astype(jnp.bfloat16)


def add_two(a0, b0, a1, b1, block=32):
    rows, width = a0.shape
    one = pl.BlockSpec((block, width), lambda i: (i, 0))
    return pl.pallas_call(
        add_body,
        grid=(rows // block,),
        in_specs=[one] * 4,
        out_specs=[one] * 2,
        out_shape=[jax.ShapeDtypeStruct((rows, width), jnp.bfloat16)] * 2,
        cost_estimate=cost(2 * rows * width, 12 * rows * width),
        compiler_params=pltpu.CompilerParams(vmem_limit_bytes=16 * MIB),
        name="add_two",
    )(a0, b0, a1, b1)


def shards(tokens, norm_gain, w_qkv, w_out, doc_lengths, span_slots):
    ctx = lax.axis_index("ctx")
    tp = lax.axis_index("tp")
    x, y, z, core = ctx // 2, ctx % 2, tp // 2, tp % 2
    gain = norm_gain.reshape(1, -1)
    rows = norm(in_hbm(tokens), in_hbm(gain))
    low, high = z_send(rows, 1), z_send(rows, -1)
    sib_rows = swap(rows)
    w_sib = swap(w_out)
    w_qkv, rows = lax.optimization_barrier((w_qkv, rows))
    (w_kv,) = load([w_qkv], [(QW, 2 * HD)])
    sib_rows, w_kv = lax.optimization_barrier((sib_rows, w_kv))
    sib_rows, doc_lengths, span_slots = lax.optimization_barrier((sib_rows, doc_lengths, span_slots))

    n_spans = span_slots.shape[0]
    per_span = 4
    span = per_span * TILE
    ends = jnp.cumsum(doc_lengths).astype(jnp.int32)
    numbers = jnp.arange(n_spans, dtype=jnp.int32)
    slot_of = jnp.sum(
        jnp.where(span_slots[None, :] == numbers[:, None], numbers[None, :], 0), axis=1
    )
    tile_no = jnp.arange(per_span, dtype=jnp.int32)[None, :]
    slot = slot_of[:, None]
    tile_tp = (slot % 2) * per_span + tile_no
    rank = slot // 2
    rel_z = (tile_tp // 2 - z) % NZ
    z_base = jnp.where(rel_z == 0, Z_BASE[0], 0)
    for i in range(1, NZ):
        z_base = jnp.where(rel_z == i, Z_BASE[i], z_base)
    rel_src = ((rank // 2 - x) % NX) * 2 + (rank % 2 != y).astype(jnp.int32)
    table = rel_src * 1024 + z_base + (tile_tp % 2 != core).astype(jnp.int32) * TILE
    table = table.reshape(-1).astype(jnp.int32)
    own_spans = lax.dynamic_slice_in_dim(span_slots, 2 * ctx, 2, 0)

    def starts_of(*dzs):
        tps = jnp.stack([((z + dz) % NZ) * 2 + c for dz in dzs for c in (core, 1 - core)])
        blocks = jnp.where(tps // per_span == 0, own_spans[0], own_spans[1])
        return (blocks * span + (tps % per_span) * TILE).astype(jnp.int32)

    starts_d, starts_b, starts_a = starts_of(2), starts_of(-1, 1), starts_of(0)
    (kv_a,) = project([rows, sib_rows], w_kv, 0, (2 * HD,))
    pair_a = y_pair(kv_a)
    pair_a, w_sib, table, ends, starts_d, starts_b, starts_a = lax.optimization_barrier(
        (pair_a, w_sib, table, ends, starts_d, starts_b, starts_a)
    )
    all_a = x_all(pair_a)
    far0, far1 = halves(low, high)
    low, high, far0, far1, *all_a = lax.optimization_barrier((low, high, far0, far1, *all_a))
    group_b = [low, swap(low), high, swap(high)]
    far0, far1 = z_send(far0, 1), z_send(far1, -1)
    (kv_b,) = project(group_b, w_kv, 0, (2 * HD,))
    other_b = y_swap(kv_b)
    left0, right0 = x_send(kv_b, 1), x_send(kv_b, -1)
    w_out, w_sib, kv_b = lax.optimization_barrier((w_out, w_sib, kv_b))
    w_out, w_sib = load([w_out, w_sib], [(0, w_out.shape[1])] * 2)
    left0, right0, other_b, w_out, w_sib = lax.optimization_barrier(
        (left0, right0, other_b, w_out, w_sib)
    )
    left1, right1 = x_send(other_b, 1), x_send(other_b, -1)
    *group_b, other_b = lax.optimization_barrier((*group_b, other_b))
    (q_b,) = project(group_b, w_qkv, 0, (QW,))
    far0, far1, left1, right1, q_b = lax.optimization_barrier((far0, far1, left1, right1, q_b))
    all_b = [
        (kv_b, other_b),
        (right0, right1),
        (x_send(left0, 1), x_send(right1, -1)),
        (left0, left1),
    ]
    group_d = [far0, far1, swap(far0), swap(far1)]
    (kv_d,) = project(group_d, w_kv, 0, (2 * HD,))
    other_d = y_swap(kv_d)
    left2, right2 = x_send(kv_d, 1), x_send(kv_d, -1)
    *group_d, other_d, left2, right2 = lax.optimization_barrier((*group_d, other_d, left2, right2))
    left3, right3 = x_send(other_d, 1), x_send(other_d, -1)
    all_d = [
        (kv_d, other_d),
        (right2, right3),
        (x_send(left2, 1), x_send(other_d, 2)),
        (left2, left3),
    ]
    (q_d,) = project(group_d, w_qkv, 0, (QW,))
    kvs, places = [], []
    for group, base in ((all_a, 0), (all_b, 256), (all_d, 768)):
        for i, one in enumerate(group):
            parts = one if isinstance(one, tuple) else (one,)
            count = sum(part.shape[0] for part in parts) // 2
            for j in range(2):
                which, src = (len(kvs) + j, 0) if len(parts) == 2 else (len(kvs), j * count)
                places.append((which, src, (2 * i + j) * 1024 + base, count))
            kvs.extend(parts)

    d_own, d_send, packed = attend(q_d, 0, 1, kvs, tuple(places), True, table, ends, starts_d, 1024)
    d_sib = swap(d_send)
    (d_lo,) = out_project(d_own, d_sib, w_out, w_sib, 0)
    (d_hi,) = out_project(d_own, d_sib, w_out, w_sib, 1)
    from_low, from_high = z_send(d_lo, 1), z_send(d_hi, -1)
    whole = ((0, 0, 0, packed.shape[0]),)
    packed, d_lo, d_hi = lax.optimization_barrier((packed, d_lo, d_hi))
    b_own, b_send = attend(q_b, 0, 2, [packed], whole, False, table, ends, starts_b, 1024)
    b_sib = swap(b_send)
    prev_lo, next_lo = out_project(b_own, b_sib, w_out, w_sib, 0)
    prev_hi, next_hi = out_project(b_own, b_sib, w_out, w_sib, 1)
    early_hi, early_lo = z_send(next_hi, 1), z_send(prev_lo, -1)
    sum_lo, sum_hi = add_two(next_lo, from_low, prev_hi, from_high)
    late_lo, late_hi = z_send(sum_lo, 1), z_send(sum_hi, -1)
    rows, sib_rows, packed, sum_lo, sum_hi = lax.optimization_barrier(
        (rows, sib_rows, packed, sum_lo, sum_hi)
    )
    (q_a,) = project([rows, sib_rows], w_qkv, 0, (QW,))
    a_own, a_send = attend(q_a, 0, 1, [packed], whole, False, table, ends, starts_a, 1024)
    a_sib = swap(a_send)
    (a_lo,) = out_project(a_own, a_sib, w_out, w_sib, 0)
    (a_hi,) = out_project(a_own, a_sib, w_out, w_sib, 1)
    return final_sum(a_lo, a_hi, early_lo, early_hi, late_lo, late_hi)


def solution(mesh):
    placed = (P(("dp", "ctx", "tp"), None), P(), P(None, "tp"), P("tp", None), P("dp"), P("dp"))
    return jax.shard_map(
        shards, mesh=mesh, in_specs=placed, out_specs=P(("dp", "ctx", "tp"), None), check_vma=False
    )
```
